32 devices in a mesh: domain: 2 (over x), fsdp: 16 (over z, y, core).
Axes of the slice: x: 2, y: 2, z: 4, core: 2. Of those that a mesh axis runs over, the one named last changes fastest.
Arguments:
- gradients: bfloat16 [2, 4, 4096, 512], P('domain', None, 'fsdp')
- row_counts: int32 [4], replicated, may hold values from 2048 to 4096, as said below
- domain_ids: int32 [2], replicated, may hold values from 0 to 7
- domain_weights: float32 [8], replicated, may hold values from 0.2 to 2
Outputs:
- updates: float32 [4, 4096, 512], P('domain', 'fsdp')
- new_weights: float32 [8], replicated
The draws below stay inside these ranges and needn't reach their ends.
Inputs may be any that keep to these rules, and one draw needn't show every extreme that they name: `row_counts`: each matrix has 4096 or 2048 rows, and both counts occur.
All inputs are finite; a program needn't handle non-finite values.
Results may differ from the reference program's by a relative error of at most 0.0071.
Values may be sent and summed in bfloat16 or wider, within the bound.
No kernel may reach another device: no remote copies, remote signals or barrier semaphores. Data moves between devices by JAX's collectives and lax.ppermute only.
A program may use at most 64 MiB of HBM per device.

```python
import math
import jax
import jax.numpy as jnp
from jax import lax

ROWS = 4096
LAT = 512
DOMAINS = 8
NS_ITERS = 3
GROUPS = 2
MATS = 4


def draw_gradients(key, part):
    key_rows, key_cols, key_groups, key_base = jax.random.split(key, 4)
    row_axis = jnp.arange(ROWS, dtype=jnp.float32)
    row_scale = jnp.power(10.0, row_axis / ROWS) * jnp.exp(jax.random.uniform(key_rows, (ROWS,), jnp.float32, -0.3, 0.3))
    group_scale = jnp.power(2.0, jax.random.uniform(key_groups, (GROUPS,), jnp.float32, -1.0, 1.0))
    col_scale = jnp.power(10.0, jax.random.uniform(key_cols, (LAT,), jnp.float32, 0.0, 1.0))
    base_part = jax.random.normal(key_base, (GROUPS, MATS, ROWS, LAT), jnp.float32)
    values = base_part * group_scale[:, None, None, None] * row_scale[None, None, :, None] * col_scale[None, None, None, :] * 0.1
    return values.astype(jnp.bfloat16)


def draw_row_counts(key, part):
    key_base, key_first, key_second = jax.random.split(key, 3)
    counts = ROWS - ROWS // 2 * jax.random.randint(key_base, (MATS,), 0, 2)
    first_pos = jax.random.randint(key_first, (), 0, MATS)
    second = (first_pos + 1 + jax.random.randint(key_second, (), 0, MATS - 1)) % MATS
    matrix_pos = jnp.arange(MATS, dtype=jnp.int32)
    counts = jnp.where(matrix_pos == first_pos, ROWS, counts)
    counts = jnp.where(matrix_pos == second, ROWS // 2, counts)
    return counts.astype(jnp.int32)


def setup_inputs(seed: int = 0) -> dict:
    arg_keys = jax.random.split(jax.random.key(seed), 5)
    gradients = draw_gradients(jax.random.fold_in(arg_keys[4], 71), 0)
    row_counts = draw_row_counts(jax.random.fold_in(arg_keys[4], 71), 0)
    domain_ids = jax.random.randint(arg_keys[2], (GROUPS,), 0, DOMAINS).astype(jnp.int32)
    domain_weights = jnp.clip(jnp.exp(jax.random.uniform(arg_keys[3], (DOMAINS,), jnp.float32, math.log(0.2), math.log(2.0))), 0.2, 2.0)
    return {"gradients": gradients, "row_counts": row_counts, "domain_ids": domain_ids, "domain_weights": domain_weights}


COEF_A = 3.4445
COEF_B = -4.775
COEF_C = 2.0315
MUON_SCALE = 0.2
ETA = 4.0

def group_mixing(domain_ids, domain_weights, kind_count):
    weight_share = domain_weights / jnp.sum(domain_weights)
    onehot = (domain_ids[:, None] == jnp.arange(kind_count, dtype=jnp.int32)[None, :]).astype(jnp.float32)
    counts = lax.optimization_barrier(jnp.sum(onehot, axis=0))
    per_member = weight_share / jnp.maximum(counts, 1.0)
    group_mix = lax.optimization_barrier(jnp.sum(onehot * per_member[None, :], axis=1))
    return (weight_share, onehot, counts, group_mix)

def newton_steps(iterate):
    for repeat in range(NS_ITERS):
        gram_full = lax.dot_general(iterate, iterate, (((0,), (0,)), ((), ())), preferred_element_type=jnp.float32)
        gram_full = lax.optimization_barrier(gram_full.astype(jnp.bfloat16))
        square = jnp.dot(gram_full, gram_full, preferred_element_type=jnp.float32)
        poly_term = (COEF_B * gram_full.astype(jnp.float32) + COEF_C * square).astype(jnp.bfloat16)
        iterate = lax.optimization_barrier((COEF_A * iterate.astype(jnp.float32) + jnp.dot(iterate, poly_term, preferred_element_type=jnp.float32)).astype(jnp.bfloat16))
    return iterate

def reference(gradients, row_counts, domain_ids, domain_weights):
    weight_share, onehot, counts, group_mix = group_mixing(domain_ids, domain_weights, DOMAINS)
    row_index = jnp.arange(ROWS, dtype=jnp.int32)
    update_scale = MUON_SCALE * math.sqrt(ROWS)

    def per_matrix(matrix_pos):
        grads_one = lax.dynamic_index_in_dim(gradients, matrix_pos, 1, keepdims=False)
        row_limit = lax.dynamic_index_in_dim(row_counts, matrix_pos, 0, keepdims=False)
        row_mask = (row_index < row_limit)[None, :, None]
        masked = jnp.where(row_mask, grads_one.astype(jnp.float32), jnp.zeros((), jnp.float32))
        combined = lax.optimization_barrier(jnp.sum(group_mix[:, None, None] * masked, axis=0))
        aligned = lax.optimization_barrier(jnp.sum(masked * combined[None], axis=(1, 2)))
        squares = lax.optimization_barrier(jnp.sum(masked * masked, axis=(1, 2)))
        frob_sq = jnp.sum(combined * combined)
        start = lax.optimization_barrier((combined / (jnp.sqrt(frob_sq) + 1e-07)).astype(jnp.bfloat16))
        finished = newton_steps(start)
        return (finished.astype(jnp.float32) * update_scale, aligned, squares, frob_sq)
    updates, aligned, squares, frob_sq = lax.map(per_matrix, jnp.arange(MATS, dtype=jnp.int32))
    total_sq = jnp.sum(frob_sq)
    cosine = lax.optimization_barrier(jnp.sum(aligned, axis=0)) / (jnp.sqrt(lax.optimization_barrier(jnp.sum(squares, axis=0))) * jnp.sqrt(total_sq) + 1e-06)
    score = lax.optimization_barrier(jnp.sum(onehot * cosine[:, None], axis=0)) / jnp.maximum(counts, 1.0)
    raised = weight_share * jnp.exp(ETA * score)
    return (updates, raised / jnp.sum(raised))
```

```python
import functools
import math

import jax
import jax.numpy as jnp
from jax import lax
from jax.experimental import pallas as pl
from jax.experimental.pallas import tpu as pltpu
from jax.sharding import PartitionSpec as P

NS_ITERS = 3
COEF_A = 3.4445
COEF_B = -4.775
COEF_C = 2.0315
MUON_SCALE = 0.2
ETA = 4.0

AXES = ("domain", "fsdp")
BLOCK = 128
SQUARE = 4
TAIL = 16
HALF_SPAN = 16384.0
TINY = 1e-30
F32 = jnp.float32


def group_mixing(domain_ids, domain_weights, kind_count):
    weight_share = domain_weights / jnp.sum(domain_weights)
    onehot = (domain_ids[:, None] == jnp.arange(kind_count, dtype=jnp.int32)[None, :]).astype(F32)
    counts = jnp.sum(onehot, axis=0)
    per_member = weight_share / jnp.maximum(counts, 1.0)
    group_mix = jnp.sum(onehot * per_member[None, :], axis=1)
    return (weight_share, onehot, counts, group_mix)


def block_plan(columns):
    count = columns // BLOCK
    off = [(i, j) for i in range(count) for j in range(i + 1, count)]
    folded = [(i, i) for i in range(0, count, 2)]
    per_piece = (len(off) + len(folded)) // SQUARE
    pieces = []
    for p in range(SQUARE):
        take = per_piece - (1 if p >= SQUARE - len(folded) else 0)
        pieces.append([off.pop(0) for _ in range(take)])
    for n, pair in enumerate(folded):
        pieces[SQUARE - len(folded) + n].append(pair)
    return pieces


def lane_pick(row, index):
    lanes = lax.broadcasted_iota(jnp.int32, row.shape, 1)
    return jnp.sum(jnp.where(lanes == index, row, 0.0), axis=1, keepdims=True)


def encode_row(row):
    power = jnp.clip(jnp.floor(jnp.log2(jnp.abs(row))), -120.0, 120.0)
    scaled = row * jnp.exp2(-power)
    high = scaled.astype(jnp.bfloat16).astype(F32)
    rest = scaled - high
    mid = rest.astype(jnp.bfloat16).astype(F32)
    low = (rest - mid).astype(jnp.bfloat16).astype(F32)
    return (high, mid * 256.0, low * 65536.0, power)


def decode_row(parts):
    high, mid, low, power = parts
    return ((high + mid * (1.0 / 256.0)) + low * (1.0 / 65536.0)) * jnp.exp2(power)


def tail_rows(rows):
    index = lax.broadcasted_iota(jnp.int32, (TAIL, BLOCK), 0)
    out = jnp.zeros((TAIL, BLOCK), F32)
    for n, row in enumerate(rows):
        out = jnp.where(index == n, row, out)
    return out


def gram_kernel(lanes, domains, mix_ref, lim_ref, pos_ref, *refs):
    blocks = refs[: domains * lanes]
    comb_ref, pay_ref, own_ref, piece_ref, diag_ref = refs[domains * lanes :]
    rows, columns = blocks[0].shape
    domain_pos, quad = pos_ref[0], pos_ref[1]
    aligned = [jnp.zeros((1, 1), F32)] * domains
    squares = [jnp.zeros((1, 1), F32)] * domains
    frob = jnp.zeros((1, 1), F32)
    row_index = lax.broadcasted_iota(jnp.int32, (rows, 1), 0)

    def total(v):
        return jnp.sum(jnp.sum(v, axis=0, keepdims=True), axis=1, keepdims=True)

    for kl in range(lanes):
        keep = row_index < lim_ref[kl]
        masked = [
            jnp.where(keep, blocks[kd * lanes + kl][...].astype(F32), 0.0)
            for kd in range(domains)
        ]
        combined = mix_ref[0] * masked[0]
        for kd in range(1, domains):
            combined = combined + mix_ref[kd] * masked[kd]
        for kd in range(domains):
            aligned[kd] = aligned[kd] + total(masked[kd] * combined)
            squares[kd] = squares[kd] + total(masked[kd] * masked[kd])
        frob = frob + total(combined * combined)
        comb_ref[pl.ds(kl * rows, rows), :] = combined
    rounded = comb_ref[...].astype(jnp.bfloat16)
    gram = lax.dot_general(
        rounded, rounded, (((0,), (0,)), ((), ())), preferred_element_type=F32
    )

    lane = lax.broadcasted_iota(jnp.int32, (1, BLOCK), 1)
    scal = jnp.where(lane == 2 * domains, frob, 0.0)
    for kd in range(domains):
        group = domain_pos ^ kd
        scal = jnp.where(lane == group, aligned[kd], scal)
        scal = jnp.where(lane == domains + group, squares[kd], scal)
    parts = encode_row(scal)
    scal = decode_row(parts)
    frob = lane_pick(scal, 2 * domains)
    scale = jnp.where(frob > TINY, HALF_SPAN / jnp.maximum(frob, TINY), 0.0)

    row_id = lax.broadcasted_iota(jnp.int32, (BLOCK, BLOCK), 0)
    col_id = lax.broadcasted_iota(jnp.int32, (BLOCK, BLOCK), 1)

    def part(i, j):
        return gram[i * BLOCK : (i + 1) * BLOCK, j * BLOCK : (j + 1) * BLOCK]

    for p, entries in enumerate(block_plan(columns)):
        diag = jnp.zeros((1, BLOCK), F32)
        for n, (i, j) in enumerate(entries):
            if i == j:
                upper, lower = part(i, i), part(i + 1, i + 1)
                value = jnp.where(row_id < col_id, upper, lower)
                diag = jnp.sum(jnp.where(row_id == col_id, upper, 0.0), axis=0, keepdims=True)
            else:
                value = part(i, j)
            piece_ref[p, pl.ds(n * BLOCK, BLOCK), :] = value
        diag_ref[p] = jnp.broadcast_to(diag, diag_ref.shape[1:])
    body_rows = piece_ref.shape[1]
    for k in range(SQUARE):
        value = piece_ref[quad ^ k]
        diag = diag_ref[quad ^ k][0:1]
        if k == 0:
            own_ref[pl.ds(0, body_rows), :] = value
            own_ref[pl.ds(body_rows, TAIL), :] = tail_rows([diag, scal])
        else:
            pay_ref[k - 1, pl.ds(0, body_rows), :] = value * scale
            pay_ref[k - 1, pl.ds(body_rows, TAIL), :] = tail_rows([diag * scale, *parts])


def sum_kernel(scalar_lane, count, *refs):
    own_ref, got, (out_ref, pay_ref) = refs[0], refs[1 : 1 + count], refs[1 + count :]
    body_rows = own_ref.shape[0] - TAIL
    terms = []
    for ref in (None, *got):
        if ref is None:
            terms.append(
                (
                    own_ref[pl.ds(0, body_rows), :],
                    own_ref[pl.ds(body_rows, 1), :],
                    own_ref[pl.ds(body_rows + 1, 1), :],
                )
            )
            continue
        scal = decode_row([ref[pl.ds(body_rows + 1 + n, 1), :] for n in range(4)])
        scale = lane_pick(scal, scalar_lane) * (1.0 / HALF_SPAN)
        terms.append(
            (ref[pl.ds(0, body_rows), :] * scale, ref[pl.ds(body_rows, 1), :] * scale, scal)
        )
    while len(terms) > 1:
        terms = [
            tuple(x + y for x, y in zip(terms[n], terms[n + 1])) for n in range(0, len(terms), 2)
        ]
    value, diag, scal = terms[0]
    parts = encode_row(scal)
    scal = decode_row(parts)
    frob = lane_pick(scal, scalar_lane)
    scale = jnp.where(frob > TINY, HALF_SPAN / jnp.maximum(frob, TINY), 0.0)
    out_ref[pl.ds(0, body_rows), :] = value
    out_ref[pl.ds(body_rows, TAIL), :] = tail_rows([diag, scal])
    pay_ref[pl.ds(0, body_rows), :] = value * scale
    pay_ref[pl.ds(body_rows, TAIL), :] = tail_rows([diag * scale, *parts])


def newton_kernel(scalar_lane, pos_ref, comb_ref, own_ref, *refs):
    got, (done_ref, piece_ref, diag_ref, gram_ref) = refs[: SQUARE - 1], refs[SQUARE - 1 :]
    quad = pos_ref[1]
    body_rows = own_ref.shape[0] - TAIL
    columns = comb_ref.shape[1]
    scal = own_ref[pl.ds(body_rows + 1, 1), :]
    frob = lane_pick(scal, scalar_lane)
    inv = 1.0 / (jnp.sqrt(frob) + 1e-07)
    shared = (frob * inv) * inv * (1.0 / HALF_SPAN)
    for k in range(SQUARE):
        ref = own_ref if k == 0 else got[k - 1]
        value, diag = ref[pl.ds(0, body_rows), :], ref[pl.ds(body_rows, 1), :]
        if k == 0:
            value, diag = (value * inv) * inv, (diag * inv) * inv
        else:
            value, diag = value * shared, diag * shared
        piece_ref[quad ^ k] = value
        diag_ref[quad ^ k] = jnp.broadcast_to(diag, diag_ref.shape[1:])
    row_id = lax.broadcasted_iota(jnp.int32, (BLOCK, BLOCK), 0)
    col_id = lax.broadcasted_iota(jnp.int32, (BLOCK, BLOCK), 1)

    def place(i, j, value):
        gram_ref[pl.ds(i * BLOCK, BLOCK), pl.ds(j * BLOCK, BLOCK)] = value

    for p, entries in enumerate(block_plan(columns)):
        for n, (i, j) in enumerate(entries):
            value = piece_ref[p, pl.ds(n * BLOCK, BLOCK), :]
            flipped = value.T
            if i == j:
                diag = diag_ref[p][0:1]
                upper = jnp.where(row_id < col_id, value, jnp.where(row_id > col_id, flipped, diag))
                place(i, i, upper)
                place(i + 1, i + 1, jnp.where(row_id < col_id, flipped, value))
            else:
                place(i, j, value)
                place(j, i, flipped)

    def dot(x, y):
        return jnp.dot(x, y, preferred_element_type=F32)

    gram = gram_ref[...]
    iterate = (comb_ref[...] * inv).astype(jnp.bfloat16)
    for step in range(NS_ITERS):
        gram_low = gram.astype(jnp.bfloat16)
        square = dot(gram_low, gram_low)
        poly = (COEF_B * gram + COEF_C * square).astype(jnp.bfloat16)
        iterate = (COEF_A * iterate.astype(F32) + dot(iterate, poly)).astype(jnp.bfloat16)
        if step + 1 < NS_ITERS:
            half = COEF_A * gram + dot(gram_low, poly)
            half_high = half.astype(jnp.bfloat16)
            half_low = (half - half_high.astype(F32)).astype(jnp.bfloat16)
            gram = COEF_A * half + dot(poly, half_high) + dot(poly, half_low)
    done_ref[...] = iterate


def call(kernel, out_shape, args, spaces, scratch=(), flops=0):
    size = sum(math.prod(a.shape) * a.dtype.itemsize for a in (*args, *out_shape))
    return pl.pallas_call(
        kernel,
        out_shape=tuple(out_shape),
        in_specs=[pl.BlockSpec(memory_space=s) for s in spaces],
        out_specs=tuple(pl.BlockSpec(memory_space=pltpu.VMEM) for _ in out_shape),
        scratch_shapes=list(scratch),
        cost_estimate=pl.CostEstimate(flops=flops, bytes_accessed=size, transcendentals=0),
    )(*args)


def body(gradients, row_counts, domain_ids, domain_weights):
    domains = lax.axis_size("domain")
    shards = lax.axis_size("fsdp")
    matrices, rows, columns = gradients.shape[1:]
    lanes = matrices // domains
    sets = shards // lanes
    members = domains * lanes
    full_rows = rows * shards
    domain_pos = lax.axis_index("domain")
    shard_pos = lax.axis_index("fsdp")
    lane_pos = shard_pos % lanes
    set_pos = shard_pos // lanes
    member = domain_pos * lanes + lane_pos
    quad = set_pos % SQUARE
    flip = [(k // lanes) * shards + k % lanes for k in range(members)]

    def exchange(value, mask):
        return lax.ppermute(value, AXES, [(i, i ^ mask) for i in range(domains * shards)])

    def piece(index):
        return lax.dynamic_index_in_dim(gradients[0], index, 0, keepdims=False)

    if members <= 8:
        order = sorted(range(1, members), key=lambda k: k // lanes == 0)
        got = {0: piece(member)}
        for k in order:
            got[k] = exchange(piece(member ^ k), flip[k])
        blocks = [got[k] for k in range(members)]
    else:
        teams = [
            [d * shards + s * lanes + l for d in range(domains) for l in range(lanes)]
            for s in range(sets)
        ]
        moved = lax.all_to_all(
            gradients[0], AXES, split_axis=0, concat_axis=0, axis_index_groups=teams, tiled=True
        )
        blocks = [
            lax.dynamic_index_in_dim(moved, member ^ k, 0, keepdims=False) for k in range(members)
        ]

    weight_share, onehot, counts, group_mix = group_mixing(
        domain_ids, domain_weights, domain_weights.shape[0]
    )
    mix = jnp.take(group_mix, domain_pos ^ jnp.arange(domains, dtype=jnp.int32))
    lane_row = (set_pos * lanes + (lane_pos ^ jnp.arange(lanes, dtype=jnp.int32))) * rows
    limits = lax.dynamic_index_in_dim(row_counts, member, 0, keepdims=False) - lane_row
    position = jnp.stack([domain_pos, quad]).astype(jnp.int32)

    per_piece = sum(1 for _ in block_plan(columns)[0]) * BLOCK
    packed = per_piece + TAIL
    vmem, smem = pltpu.VMEM, pltpu.SMEM
    pieces_scratch = [
        pltpu.VMEM((SQUARE, per_piece, BLOCK), F32),
        pltpu.VMEM((SQUARE, 8, BLOCK), F32),
    ]
    combined, payload, own = call(
        functools.partial(gram_kernel, lanes, domains),
        [
            jax.ShapeDtypeStruct((lanes * rows, columns), F32),
            jax.ShapeDtypeStruct((SQUARE - 1, packed, BLOCK), F32),
            jax.ShapeDtypeStruct((packed, BLOCK), F32),
        ],
        [mix, limits, position, *blocks],
        [smem] * 3 + [vmem] * members,
        pieces_scratch,
        flops=2 * lanes * rows * columns * columns,
    )
    scalar_lane = 2 * domains

    def add_up(own, got):
        return call(
            functools.partial(sum_kernel, scalar_lane, len(got)),
            [jax.ShapeDtypeStruct((packed, BLOCK), F32)] * 2,
            [own, *got],
            [vmem] * (1 + len(got)),
        )

    def half_width(value, mask):
        return exchange(value.astype(jnp.float16), mask).astype(F32)

    got = [half_width(payload[k - 1], k * lanes) for k in range(1, SQUARE)]
    own, packet = add_up(own, got)
    stride = SQUARE * lanes
    while stride < shards:
        own, packet = add_up(own, [half_width(packet, stride)])
        stride *= 2
    got = [half_width(packet, k * lanes) for k in range(1, SQUARE)]

    (finished,) = call(
        functools.partial(newton_kernel, scalar_lane),
        [jax.ShapeDtypeStruct((lanes * rows, columns), jnp.bfloat16)],
        [position, combined, own, *got],
        [smem] + [vmem] * (1 + SQUARE),
        pieces_scratch + [pltpu.VMEM((columns, columns), F32)],
        flops=13 * 2 * columns**3,
    )

    finished = finished.reshape(lanes, rows, columns)
    returned = [finished[0]] + [exchange(finished[k], k) for k in range(1, lanes)]
    if lanes == 2:
        first = lane_pos == 0
        ordered = [
            jnp.where(first, returned[0], returned[1]),
            jnp.where(first, returned[1], returned[0]),
        ]
    else:
        stacked = jnp.stack(returned)
        ordered = [
            lax.dynamic_index_in_dim(stacked, lane_pos ^ k, 0, keepdims=False)
            for k in range(lanes)
        ]
    updates = jnp.stack(ordered).astype(F32) * (MUON_SCALE * math.sqrt(full_rows))

    sums = own[per_piece : per_piece + 8]
    stride = 1
    while stride < members:
        sums = sums + exchange(sums, flip[stride])
        stride *= 2
    aligned, squares = sums[1, :domains], sums[1, domains : 2 * domains]
    total_sq = sums[1, scalar_lane]
    cosine = aligned / (jnp.sqrt(squares) * jnp.sqrt(total_sq) + 1e-06)
    score = jnp.sum(onehot * cosine[:, None], axis=0) / jnp.maximum(counts, 1.0)
    raised = weight_share * jnp.exp(ETA * score)
    return (updates, raised / jnp.sum(raised))


def solution(mesh):
    placed = (P("domain", None, "fsdp", None), P(), P(), P())
    return jax.shard_map(
        body,
        mesh=mesh,
        in_specs=placed,
        out_specs=(P("domain", "fsdp", None), P()),
        check_vma=False,
    )
```

```python
import functools
import math

import jax
import jax.numpy as jnp
from jax import lax
from jax.experimental import pallas as pl
from jax.experimental.pallas import tpu as pltpu
from jax.sharding import PartitionSpec as P

NS_ITERS = 3
COEF_A = 3.4445
COEF_B = -4.775
COEF_C = 2.0315
MUON_SCALE = 0.2
ETA = 4.0

AXES = ("domain", "fsdp")
BLOCK = 128
SQUARE = 4
TAIL = 16
HALF_SPAN = 16384.0
TINY = 1e-30
VMEM_GRANT = 16 * 1024 * 1024
F32 = jnp.float32


def group_mixing(domain_ids, domain_weights, kind_count):
    weight_share = domain_weights / jnp.sum(domain_weights)
    onehot = (domain_ids[:, None] == jnp.arange(kind_count, dtype=jnp.int32)[None, :]).astype(F32)
    counts = jnp.sum(onehot, axis=0)
    per_member = weight_share / jnp.maximum(counts, 1.0)
    group_mix = jnp.sum(onehot * per_member[None, :], axis=1)
    return (weight_share, onehot, counts, group_mix)


def block_plan(columns):
    count = columns // BLOCK
    off = [(i, j) for i in range(count) for j in range(i + 1, count)]
    folded = [(i, i) for i in range(0, count, 2)]
    per_piece = (len(off) + len(folded)) // SQUARE
    pieces = []
    for p in range(SQUARE):
        take = per_piece - (1 if p >= SQUARE - len(folded) else 0)
        pieces.append([off.pop(0) for _ in range(take)])
    for n, pair in enumerate(folded):
        pieces[SQUARE - len(folded) + n].append(pair)
    return pieces


def lane_pick(row, index):
    lanes = lax.broadcasted_iota(jnp.int32, row.shape, 1)
    return jnp.sum(jnp.where(lanes == index, row, 0.0), axis=1, keepdims=True)


def encode_row(row):
    power = jnp.clip(jnp.floor(jnp.log2(jnp.abs(row))), -120.0, 120.0)
    scaled = row * jnp.exp2(-power)
    high = scaled.astype(jnp.bfloat16).astype(F32)
    rest = scaled - high
    mid = rest.astype(jnp.bfloat16).astype(F32)
    low = (rest - mid).astype(jnp.bfloat16).astype(F32)
    return (high, mid * 256.0, low * 65536.0, power)


def decode_row(parts):
    high, mid, low, power = parts
    return ((high + mid * (1.0 / 256.0)) + low * (1.0 / 65536.0)) * jnp.exp2(power)


def tail_rows(rows):
    index = lax.broadcasted_iota(jnp.int32, (TAIL, BLOCK), 0)
    out = jnp.zeros((TAIL, BLOCK), F32)
    for n, row in enumerate(rows):
        out = jnp.where(index == n, row, out)
    return out


def gram_kernel(lanes, domains, mix_ref, lim_ref, pos_ref, *refs):
    blocks = refs[: domains * lanes]
    comb_ref, pay_ref, own_ref, piece_ref, diag_ref = refs[domains * lanes :]
    rows, columns = blocks[0].shape
    domain_pos, quad = pos_ref[0], pos_ref[1]
    aligned = [jnp.zeros((1, 1), F32)] * domains
    squares = [jnp.zeros((1, 1), F32)] * domains
    frob = jnp.zeros((1, 1), F32)
    row_index = lax.broadcasted_iota(jnp.int32, (rows, 1), 0)

    def total(v):
        return jnp.sum(jnp.sum(v, axis=0, keepdims=True), axis=1, keepdims=True)

    for kl in range(lanes):
        keep = row_index < lim_ref[kl]
        masked = [
            jnp.where(keep, blocks[kd * lanes + kl][...].astype(F32), 0.0)
            for kd in range(domains)
        ]
        combined = mix_ref[0] * masked[0]
        for kd in range(1, domains):
            combined = combined + mix_ref[kd] * masked[kd]
        for kd in range(domains):
            aligned[kd] = aligned[kd] + total(masked[kd] * combined)
            squares[kd] = squares[kd] + total(masked[kd] * masked[kd])
        frob = frob + total(combined * combined)
        comb_ref[pl.ds(kl * rows, rows), :] = combined
    rounded = comb_ref[...].astype(jnp.bfloat16)
    gram = lax.dot_general(
        rounded, rounded, (((0,), (0,)), ((), ())), preferred_element_type=F32
    )

    lane = lax.broadcasted_iota(jnp.int32, (1, BLOCK), 1)
    scal = jnp.where(lane == 2 * domains, frob, 0.0)
    for kd in range(domains):
        group = domain_pos ^ kd
        scal = jnp.where(lane == group, aligned[kd], scal)
        scal = jnp.where(lane == domains + group, squares[kd], scal)
    parts = encode_row(scal)
    scal = decode_row(parts)
    frob = lane_pick(scal, 2 * domains)
    scale = jnp.where(frob > TINY, HALF_SPAN / jnp.maximum(frob, TINY), 0.0)

    row_id = lax.broadcasted_iota(jnp.int32, (BLOCK, BLOCK), 0)
    col_id = lax.broadcasted_iota(jnp.int32, (BLOCK, BLOCK), 1)

    def part(i, j):
        return gram[i * BLOCK : (i + 1) * BLOCK, j * BLOCK : (j + 1) * BLOCK]

    for p, entries in enumerate(block_plan(columns)):
        diag = jnp.zeros((1, BLOCK), F32)
        for n, (i, j) in enumerate(entries):
            if i == j:
                upper, lower = part(i, i), part(i + 1, i + 1)
                value = jnp.where(row_id < col_id, upper, lower)
                diag = jnp.sum(jnp.where(row_id == col_id, upper, 0.0), axis=0, keepdims=True)
            else:
                value = part(i, j)
            piece_ref[p, pl.ds(n * BLOCK, BLOCK), :] = value
        diag_ref[p] = jnp.broadcast_to(diag, diag_ref.shape[1:])
    body_rows = piece_ref.shape[1]
    for k in range(SQUARE):
        value = piece_ref[quad ^ k]
        diag = diag_ref[quad ^ k][0:1]
        if k == 0:
            own_ref[pl.ds(0, body_rows), :] = value
            own_ref[pl.ds(body_rows, TAIL), :] = tail_rows([diag, scal])
        else:
            pay_ref[k - 1, pl.ds(0, body_rows), :] = value * scale
            pay_ref[k - 1, pl.ds(body_rows, TAIL), :] = tail_rows([diag * scale, *parts])


def sum_kernel(scalar_lane, count, *refs):
    own_ref, got, (out_ref, pay_ref) = refs[0], refs[1 : 1 + count], refs[1 + count :]
    body_rows = own_ref.shape[0] - TAIL
    terms = []
    for ref in (None, *got):
        if ref is None:
            terms.append(
                (
                    own_ref[pl.ds(0, body_rows), :],
                    own_ref[pl.ds(body_rows, 1), :],
                    own_ref[pl.ds(body_rows + 1, 1), :],
                )
            )
            continue
        scal = decode_row([ref[pl.ds(body_rows + 1 + n, 1), :] for n in range(4)])
        scale = lane_pick(scal, scalar_lane) * (1.0 / HALF_SPAN)
        terms.append(
            (ref[pl.ds(0, body_rows), :] * scale, ref[pl.ds(body_rows, 1), :] * scale, scal)
        )
    while len(terms) > 1:
        terms = [
            tuple(x + y for x, y in zip(terms[n], terms[n + 1])) for n in range(0, len(terms), 2)
        ]
    value, diag, scal = terms[0]
    parts = encode_row(scal)
    scal = decode_row(parts)
    frob = lane_pick(scal, scalar_lane)
    scale = jnp.where(frob > TINY, HALF_SPAN / jnp.maximum(frob, TINY), 0.0)
    out_ref[pl.ds(0, body_rows), :] = value
    out_ref[pl.ds(body_rows, TAIL), :] = tail_rows([diag, scal])
    pay_ref[pl.ds(0, body_rows), :] = value * scale
    pay_ref[pl.ds(body_rows, TAIL), :] = tail_rows([diag * scale, *parts])


def newton_kernel(scalar_lane, pos_ref, comb_ref, own_ref, *refs):
    got, (done_ref, piece_ref, diag_ref, gram_ref) = refs[: SQUARE - 1], refs[SQUARE - 1 :]
    quad = pos_ref[1]
    body_rows = own_ref.shape[0] - TAIL
    columns = comb_ref.shape[1]
    scal = own_ref[pl.ds(body_rows + 1, 1), :]
    frob = lane_pick(scal, scalar_lane)
    inv = 1.0 / (jnp.sqrt(frob) + 1e-07)
    shared = (frob * inv) * inv * (1.0 / HALF_SPAN)
    for k in range(SQUARE):
        ref = own_ref if k == 0 else got[k - 1]
        value, diag = ref[pl.ds(0, body_rows), :], ref[pl.ds(body_rows, 1), :]
        if k == 0:
            value, diag = (value * inv) * inv, (diag * inv) * inv
        else:
            value, diag = value * shared, diag * shared
        piece_ref[quad ^ k] = value
        diag_ref[quad ^ k] = jnp.broadcast_to(diag, diag_ref.shape[1:])
    row_id = lax.broadcasted_iota(jnp.int32, (BLOCK, BLOCK), 0)
    col_id = lax.broadcasted_iota(jnp.int32, (BLOCK, BLOCK), 1)

    def place(i, j, value):
        gram_ref[pl.ds(i * BLOCK, BLOCK), pl.ds(j * BLOCK, BLOCK)] = value

    for p, entries in enumerate(block_plan(columns)):
        for n, (i, j) in enumerate(entries):
            value = piece_ref[p, pl.ds(n * BLOCK, BLOCK), :]
            flipped = value.T
            if i == j:
                diag = diag_ref[p][0:1]
                upper = jnp.where(row_id < col_id, value, jnp.where(row_id > col_id, flipped, diag))
                place(i, i, upper)
                place(i + 1, i + 1, jnp.where(row_id < col_id, flipped, value))
            else:
                place(i, j, value)
                place(j, i, flipped)

    def dot(x, y):
        return jnp.dot(x, y, preferred_element_type=F32)

    gram = gram_ref[...]
    iterate = (comb_ref[...] * inv).astype(jnp.bfloat16)
    for step in range(NS_ITERS):
        gram_low = gram.astype(jnp.bfloat16)
        square = dot(gram_low, gram_low)
        poly = (COEF_B * gram + COEF_C * square).astype(jnp.bfloat16)
        iterate = (COEF_A * iterate.astype(F32) + dot(iterate, poly)).astype(jnp.bfloat16)
        if step + 1 < NS_ITERS:
            half = COEF_A * gram + dot(gram_low, poly)
            half_high = half.astype(jnp.bfloat16)
            half_low = (half - half_high.astype(F32)).astype(jnp.bfloat16)
            gram = COEF_A * half + dot(poly, half_high) + dot(poly, half_low)
    done_ref[...] = iterate


def call(kernel, out_shape, args, spaces, scratch=(), flops=0):
    size = sum(math.prod(a.shape) * a.dtype.itemsize for a in (*args, *out_shape))
    return pl.pallas_call(
        kernel,
        out_shape=tuple(out_shape),
        in_specs=[pl.BlockSpec(memory_space=s) for s in spaces],
        out_specs=tuple(pl.BlockSpec(memory_space=pltpu.VMEM) for _ in out_shape),
        scratch_shapes=list(scratch),
        cost_estimate=pl.CostEstimate(flops=flops, bytes_accessed=size, transcendentals=0),
        compiler_params=pltpu.CompilerParams(vmem_limit_bytes=VMEM_GRANT),
    )(*args)


def body(gradients, row_counts, domain_ids, domain_weights):
    domains = lax.axis_size("domain")
    shards = lax.axis_size("fsdp")
    matrices, rows, columns = gradients.shape[1:]
    lanes = matrices // domains
    sets = shards // lanes
    members = domains * lanes
    full_rows = rows * shards
    domain_pos = lax.axis_index("domain")
    shard_pos = lax.axis_index("fsdp")
    lane_pos = shard_pos % lanes
    set_pos = shard_pos // lanes
    member = domain_pos * lanes + lane_pos
    quad = set_pos % SQUARE
    flip = [(k // lanes) * shards + k % lanes for k in range(members)]

    def exchange(value, mask):
        return lax.ppermute(value, AXES, [(i, i ^ mask) for i in range(domains * shards)])

    def piece(index):
        return lax.dynamic_index_in_dim(gradients[0], index, 0, keepdims=False)

    if members <= 8:
        order = sorted(range(1, members), key=lambda k: k // lanes == 0)
        got = {0: piece(member)}
        for k in order:
            got[k] = exchange(piece(member ^ k), flip[k])
        blocks = [got[k] for k in range(members)]
    else:
        teams = [
            [d * shards + s * lanes + l for d in range(domains) for l in range(lanes)]
            for s in range(sets)
        ]
        moved = lax.all_to_all(
            gradients[0], AXES, split_axis=0, concat_axis=0, axis_index_groups=teams, tiled=True
        )
        blocks = [
            lax.dynamic_index_in_dim(moved, member ^ k, 0, keepdims=False) for k in range(members)
        ]

    weight_share, onehot, counts, group_mix = group_mixing(
        domain_ids, domain_weights, domain_weights.shape[0]
    )
    mix = jnp.take(group_mix, domain_pos ^ jnp.arange(domains, dtype=jnp.int32))
    lane_row = (set_pos * lanes + (lane_pos ^ jnp.arange(lanes, dtype=jnp.int32))) * rows
    limits = lax.dynamic_index_in_dim(row_counts, member, 0, keepdims=False) - lane_row
    position = jnp.stack([domain_pos, quad]).astype(jnp.int32)

    per_piece = sum(1 for _ in block_plan(columns)[0]) * BLOCK
    packed = per_piece + TAIL
    vmem, smem = pltpu.VMEM, pltpu.SMEM
    pieces_scratch = [
        pltpu.VMEM((SQUARE, per_piece, BLOCK), F32),
        pltpu.VMEM((SQUARE, 8, BLOCK), F32),
    ]
    combined, payload, own = call(
        functools.partial(gram_kernel, lanes, domains),
        [
            jax.ShapeDtypeStruct((lanes * rows, columns), F32),
            jax.ShapeDtypeStruct((SQUARE - 1, packed, BLOCK), F32),
            jax.ShapeDtypeStruct((packed, BLOCK), F32),
        ],
        [mix, limits, position, *blocks],
        [smem] * 3 + [vmem] * members,
        pieces_scratch,
        flops=2 * lanes * rows * columns * columns,
    )
    scalar_lane = 2 * domains

    def add_up(own, got):
        return call(
            functools.partial(sum_kernel, scalar_lane, len(got)),
            [jax.ShapeDtypeStruct((packed, BLOCK), F32)] * 2,
            [own, *got],
            [vmem] * (1 + len(got)),
        )

    def half_width(value, mask):
        return exchange(value.astype(jnp.float16), mask).astype(F32)

    got = [half_width(payload[k - 1], k * lanes) for k in range(1, SQUARE)]
    own, packet = add_up(own, got)
    stride = SQUARE * lanes
    while stride < shards:
        own, packet = add_up(own, [half_width(packet, stride)])
        stride *= 2
    got = [half_width(packet, k * lanes) for k in range(1, SQUARE)]

    (finished,) = call(
        functools.partial(newton_kernel, scalar_lane),
        [jax.ShapeDtypeStruct((lanes * rows, columns), jnp.bfloat16)],
        [position, combined, own, *got],
        [smem] + [vmem] * (1 + SQUARE),
        pieces_scratch + [pltpu.VMEM((columns, columns), F32)],
        flops=13 * 2 * columns**3,
    )

    finished = finished.reshape(lanes, rows, columns)
    returned = [finished[0]] + [exchange(finished[k], k) for k in range(1, lanes)]
    if lanes == 2:
        first = lane_pos == 0
        ordered = [
            jnp.where(first, returned[0], returned[1]),
            jnp.where(first, returned[1], returned[0]),
        ]
    else:
        stacked = jnp.stack(returned)
        ordered = [
            lax.dynamic_index_in_dim(stacked, lane_pos ^ k, 0, keepdims=False)
            for k in range(lanes)
        ]
    updates = jnp.stack(ordered).astype(F32) * (MUON_SCALE * math.sqrt(full_rows))

    sums = own[per_piece : per_piece + 8]
    stride = 1
    while stride < members:
        sums = sums + exchange(sums, flip[stride])
        stride *= 2
    aligned, squares = sums[1, :domains], sums[1, domains : 2 * domains]
    total_sq = sums[1, scalar_lane]
    cosine = aligned / (jnp.sqrt(squares) * jnp.sqrt(total_sq) + 1e-06)
    score = jnp.sum(onehot * cosine[:, None], axis=0) / jnp.maximum(counts, 1.0)
    raised = weight_share * jnp.exp(ETA * score)
    return (updates, raised / jnp.sum(raised))


def solution(mesh):
    placed = (P("domain", None, "fsdp", None), P(), P(), P())
    return jax.shard_map(
        body,
        mesh=mesh,
        in_specs=placed,
        out_specs=(P("domain", "fsdp", None), P()),
        check_vma=False,
    )
```

```python
import functools
import math

import jax
import jax.numpy as jnp
from jax import lax
from jax.experimental import pallas as pl
from jax.experimental.pallas import tpu as pltpu
from jax.sharding import PartitionSpec as P


NS_ITERS = 3
COEF_A = 3.4445
COEF_B = -4.775
COEF_C = 2.0315
MUON_SCALE = 0.2
ETA = 4.0

AXES = ("domain", "fsdp")
BLOCK = 128
SQUARE = 4
TAIL = 16
HALF_SPAN = 16384.0
TINY = 1e-30
VMEM_GRANT = 16 * 1024 * 1024
F32 = jnp.float32


def group_mixing(domain_ids, domain_weights, kind_count):
    weight_share = domain_weights / jnp.sum(domain_weights)
    onehot = (domain_ids[:, None] == jnp.arange(kind_count, dtype=jnp.int32)[None, :]).astype(F32)
    counts = jnp.sum(onehot, axis=0)
    per_member = weight_share / jnp.maximum(counts, 1.0)
    group_mix = jnp.sum(onehot * per_member[None, :], axis=1)
    return (weight_share, onehot, counts, group_mix)


def block_plan(columns):
    count = columns // BLOCK
    off = [(i, j) for i in range(count) for j in range(i + 1, count)]
    folded = [(i, i) for i in range(0, count, 2)]
    per_piece = (len(off) + len(folded)) // SQUARE
    pieces = []
    for p in range(SQUARE):
        take = per_piece - (1 if p >= SQUARE - len(folded) else 0)
        pieces.append([off.pop(0) for _ in range(take)])
    for n, pair in enumerate(folded):
        pieces[SQUARE - len(folded) + n].append(pair)
    return pieces


def lane_pick(row, index):
    lanes = lax.broadcasted_iota(jnp.int32, row.shape, 1)
    return jnp.sum(jnp.where(lanes == index, row, 0.0), axis=1, keepdims=True)


def encode_row(row):
    power = jnp.clip(jnp.floor(jnp.log2(jnp.abs(row))), -120.0, 120.0)
    scaled = row * jnp.exp2(-power)
    high = scaled.astype(jnp.bfloat16).astype(F32)
    rest = scaled - high
    mid = rest.astype(jnp.bfloat16).astype(F32)
    low = (rest - mid).astype(jnp.bfloat16).astype(F32)
    return (high, mid * 256.0, low * 65536.0, power)


def decode_row(parts):
    high, mid, low, power = parts
    return ((high + mid * (1.0 / 256.0)) + low * (1.0 / 65536.0)) * jnp.exp2(power)


def tail_rows(rows):
    index = lax.broadcasted_iota(jnp.int32, (TAIL, BLOCK), 0)
    out = jnp.zeros((TAIL, BLOCK), F32)
    for n, row in enumerate(rows):
        out = jnp.where(index == n, row, out)
    return out


def gram_kernel(lanes, domains, mix_ref, lim_ref, pos_ref, *refs):
    blocks = refs[: domains * lanes]
    comb_ref, pay_ref, own_ref, piece_ref, diag_ref = refs[domains * lanes :]
    rows, columns = blocks[0].shape
    domain_pos, quad = pos_ref[0], pos_ref[1]
    aligned = [jnp.zeros((1, 1), F32)] * domains
    squares = [jnp.zeros((1, 1), F32)] * domains
    frob = jnp.zeros((1, 1), F32)
    row_index = lax.broadcasted_iota(jnp.int32, (rows, 1), 0)

    def total(v):
        return jnp.sum(jnp.sum(v, axis=0, keepdims=True), axis=1, keepdims=True)

    for kl in range(lanes):
        keep = row_index < lim_ref[kl]
        masked = [
            jnp.where(keep, blocks[kd * lanes + kl][...].astype(F32), 0.0)
            for kd in range(domains)
        ]
        combined = mix_ref[0] * masked[0]
        for kd in range(1, domains):
            combined = combined + mix_ref[kd] * masked[kd]
        for kd in range(domains):
            aligned[kd] = aligned[kd] + total(masked[kd] * combined)
            squares[kd] = squares[kd] + total(masked[kd] * masked[kd])
        frob = frob + total(combined * combined)
        comb_ref[pl.ds(kl * rows, rows), :] = combined
    rounded = comb_ref[...].astype(jnp.bfloat16)
    gram = lax.dot_general(
        rounded, rounded, (((0,), (0,)), ((), ())), preferred_element_type=F32
    )

    lane = lax.broadcasted_iota(jnp.int32, (1, BLOCK), 1)
    scal = jnp.where(lane == 2 * domains, frob, 0.0)
    for kd in range(domains):
        group = domain_pos ^ kd
        scal = jnp.where(lane == group, aligned[kd], scal)
        scal = jnp.where(lane == domains + group, squares[kd], scal)
    parts = encode_row(scal)
    scal = decode_row(parts)
    frob = lane_pick(scal, 2 * domains)
    scale = jnp.where(frob > TINY, HALF_SPAN / jnp.maximum(frob, TINY), 0.0)

    row_id = lax.broadcasted_iota(jnp.int32, (BLOCK, BLOCK), 0)
    col_id = lax.broadcasted_iota(jnp.int32, (BLOCK, BLOCK), 1)

    def part(i, j):
        return gram[i * BLOCK : (i + 1) * BLOCK, j * BLOCK : (j + 1) * BLOCK]

    for p, entries in enumerate(block_plan(columns)):
        diag = jnp.zeros((1, BLOCK), F32)
        for n, (i, j) in enumerate(entries):
            if i == j:
                upper, lower = part(i, i), part(i + 1, i + 1)
                value = jnp.where(row_id < col_id, upper, lower)
                diag = jnp.sum(jnp.where(row_id == col_id, upper, 0.0), axis=0, keepdims=True)
            else:
                value = part(i, j)
            piece_ref[p, pl.ds(n * BLOCK, BLOCK), :] = value
        diag_ref[p] = jnp.broadcast_to(diag, diag_ref.shape[1:])
    body_rows = piece_ref.shape[1]
    for k in range(SQUARE):
        value = piece_ref[quad ^ k]
        diag = diag_ref[quad ^ k][0:1]
        if k == 0:
            own_ref[pl.ds(0, body_rows), :] = value
            own_ref[pl.ds(body_rows, TAIL), :] = tail_rows([diag, scal])
        else:
            pay_ref[k - 1, pl.ds(0, body_rows), :] = value * scale
            pay_ref[k - 1, pl.ds(body_rows, TAIL), :] = tail_rows([diag * scale, *parts])


def sum_kernel(scalar_lane, count, *refs):
    own_ref, got, (out_ref, pay_ref) = refs[0], refs[1 : 1 + count], refs[1 + count :]
    body_rows = own_ref.shape[0] - TAIL
    terms = []
    for ref in (None, *got):
        if ref is None:
            terms.append(
                (
                    own_ref[pl.ds(0, body_rows), :],
                    own_ref[pl.ds(body_rows, 1), :],
                    own_ref[pl.ds(body_rows + 1, 1), :],
                )
            )
            continue
        scal = decode_row([ref[pl.ds(body_rows + 1 + n, 1), :] for n in range(4)])
        scale = lane_pick(scal, scalar_lane) * (1.0 / HALF_SPAN)
        terms.append(
            (ref[pl.ds(0, body_rows), :] * scale, ref[pl.ds(body_rows, 1), :] * scale, scal)
        )
    while len(terms) > 1:
        terms = [
            tuple(x + y for x, y in zip(terms[n], terms[n + 1])) for n in range(0, len(terms), 2)
        ]
    value, diag, scal = terms[0]
    parts = encode_row(scal)
    scal = decode_row(parts)
    frob = lane_pick(scal, scalar_lane)
    scale = jnp.where(frob > TINY, HALF_SPAN / jnp.maximum(frob, TINY), 0.0)
    out_ref[pl.ds(0, body_rows), :] = value
    out_ref[pl.ds(body_rows, TAIL), :] = tail_rows([diag, scal])
    pay_ref[pl.ds(0, body_rows), :] = value * scale
    pay_ref[pl.ds(body_rows, TAIL), :] = tail_rows([diag * scale, *parts])


def newton_kernel(scalar_lane, pos_ref, comb_ref, own_ref, *refs):
    got, (done_ref, piece_ref, diag_ref, gram_ref) = refs[: SQUARE - 1], refs[SQUARE - 1 :]
    quad = pos_ref[1]
    body_rows = own_ref.shape[0] - TAIL
    columns = comb_ref.shape[1]
    scal = own_ref[pl.ds(body_rows + 1, 1), :]
    frob = lane_pick(scal, scalar_lane)
    inv = 1.0 / (jnp.sqrt(frob) + 1e-07)
    shared = (frob * inv) * inv * (1.0 / HALF_SPAN)
    for k in range(SQUARE):
        ref = own_ref if k == 0 else got[k - 1]
        value, diag = ref[pl.ds(0, body_rows), :], ref[pl.ds(body_rows, 1), :]
        if k == 0:
            value, diag = (value * inv) * inv, (diag * inv) * inv
        else:
            value, diag = value * shared, diag * shared
        piece_ref[quad ^ k] = value
        diag_ref[quad ^ k] = jnp.broadcast_to(diag, diag_ref.shape[1:])
    row_id = lax.broadcasted_iota(jnp.int32, (BLOCK, BLOCK), 0)
    col_id = lax.broadcasted_iota(jnp.int32, (BLOCK, BLOCK), 1)

    def place(i, j, value):
        gram_ref[pl.ds(i * BLOCK, BLOCK), pl.ds(j * BLOCK, BLOCK)] = value

    for p, entries in enumerate(block_plan(columns)):
        for n, (i, j) in enumerate(entries):
            value = piece_ref[p, pl.ds(n * BLOCK, BLOCK), :]
            flipped = value.T
            if i == j:
                diag = diag_ref[p][0:1]
                upper = jnp.where(row_id < col_id, value, jnp.where(row_id > col_id, flipped, diag))
                place(i, i, upper)
                place(i + 1, i + 1, jnp.where(row_id < col_id, flipped, value))
            else:
                place(i, j, value)
                place(j, i, flipped)

    def dot(x, y):
        return jnp.dot(x, y, preferred_element_type=F32)

    gram = gram_ref[...]
    iterate = (comb_ref[...] * inv).astype(jnp.bfloat16)
    for step in range(NS_ITERS):
        gram_low = gram.astype(jnp.bfloat16)
        square = dot(gram_low, gram_low)
        poly = (COEF_B * gram + COEF_C * square).astype(jnp.bfloat16)
        iterate = (COEF_A * iterate.astype(F32) + dot(iterate, poly)).astype(jnp.bfloat16)
        if step + 1 < NS_ITERS:
            half = COEF_A * gram + dot(gram_low, poly)
            half_high = half.astype(jnp.bfloat16)
            half_low = (half - half_high.astype(F32)).astype(jnp.bfloat16)
            gram = COEF_A * half + dot(poly, half_high) + dot(poly, half_low)
    done_ref[...] = iterate


def weight_kernel(domains, count, *refs):
    tiles, (share_ref, onehot_ref, counts_ref, out_ref) = refs[:count], refs[count:]
    rows = [ref[1:2, :] for ref in tiles]
    while len(rows) > 1:
        rows = [rows[n] + rows[n + 1] for n in range(0, len(rows), 2)]
    norm = jnp.sqrt(lane_pick(rows[0], 2 * domains))
    score = jnp.zeros(share_ref.shape, F32)
    for g in range(domains):
        aligned, squares = lane_pick(rows[0], g), lane_pick(rows[0], domains + g)
        cosine = aligned / (jnp.sqrt(squares) * norm + 1e-06)
        score = score + onehot_ref[g : g + 1, :] * cosine
    score = score / jnp.maximum(counts_ref[...], 1.0)
    raised = share_ref[...] * jnp.exp(ETA * score)
    out_ref[...] = raised / jnp.sum(raised, axis=1, keepdims=True)


def call(kernel, out_shape, args, spaces, scratch=(), flops=0):
    size = sum(math.prod(a.shape) * a.dtype.itemsize for a in (*args, *out_shape))
    return pl.pallas_call(
        kernel,
        out_shape=tuple(out_shape),
        in_specs=[pl.BlockSpec(memory_space=s) for s in spaces],
        out_specs=tuple(pl.BlockSpec(memory_space=pltpu.VMEM) for _ in out_shape),
        scratch_shapes=list(scratch),
        cost_estimate=pl.CostEstimate(flops=flops, bytes_accessed=size, transcendentals=0),
        compiler_params=pltpu.CompilerParams(vmem_limit_bytes=VMEM_GRANT),
    )(*args)


def body(gradients, row_counts, domain_ids, domain_weights):
    domains = lax.axis_size("domain")
    shards = lax.axis_size("fsdp")
    matrices, rows, columns = gradients.shape[1:]
    lanes = matrices // domains
    sets = shards // lanes
    members = domains * lanes
    full_rows = rows * shards
    domain_pos = lax.axis_index("domain")
    shard_pos = lax.axis_index("fsdp")
    lane_pos = shard_pos % lanes
    set_pos = shard_pos // lanes
    member = domain_pos * lanes + lane_pos
    quad = set_pos % SQUARE
    flip = [(k // lanes) * shards + k % lanes for k in range(members)]

    def exchange(value, mask):
        return lax.ppermute(value, AXES, [(i, i ^ mask) for i in range(domains * shards)])

    def piece(source, index):
        return lax.dynamic_index_in_dim(source[0], index, 0, keepdims=False)

    if members <= 8:
        order = sorted(range(1, members), key=lambda k: k // lanes == 0)
        got, held = {}, gradients
        for k in order:
            part, held = lax.optimization_barrier((piece(held, member ^ k), held))
            got[k] = exchange(part, flip[k])
        got[0] = piece(held, member)
        blocks = [got[k] for k in range(members)]
    else:
        teams = [
            [d * shards + s * lanes + l for d in range(domains) for l in range(lanes)]
            for s in range(sets)
        ]
        moved = lax.all_to_all(
            gradients[0], AXES, split_axis=0, concat_axis=0, axis_index_groups=teams, tiled=True
        )
        blocks = [
            lax.dynamic_index_in_dim(moved, member ^ k, 0, keepdims=False) for k in range(members)
        ]

    weight_share, onehot, counts, group_mix = group_mixing(
        domain_ids, domain_weights, domain_weights.shape[0]
    )
    mix = jnp.take(group_mix, domain_pos ^ jnp.arange(domains, dtype=jnp.int32))
    lane_row = (set_pos * lanes + (lane_pos ^ jnp.arange(lanes, dtype=jnp.int32))) * rows
    limits = lax.dynamic_index_in_dim(row_counts, member, 0, keepdims=False) - lane_row
    position = jnp.stack([domain_pos, quad]).astype(jnp.int32)

    per_piece = sum(1 for _ in block_plan(columns)[0]) * BLOCK
    packed = per_piece + TAIL
    vmem, smem = pltpu.VMEM, pltpu.SMEM
    pieces_scratch = [
        pltpu.VMEM((SQUARE, per_piece, BLOCK), F32),
        pltpu.VMEM((SQUARE, 8, BLOCK), F32),
    ]
    combined, payload, own = call(
        functools.partial(gram_kernel, lanes, domains),
        [
            jax.ShapeDtypeStruct((lanes * rows, columns), F32),
            jax.ShapeDtypeStruct((SQUARE - 1, packed, BLOCK), F32),
            jax.ShapeDtypeStruct((packed, BLOCK), F32),
        ],
        [mix, limits, position, *blocks],
        [smem] * 3 + [vmem] * members,
        pieces_scratch,
        flops=2 * lanes * rows * columns * columns,
    )
    scalar_lane = 2 * domains

    def add_up(own, got):
        return call(
            functools.partial(sum_kernel, scalar_lane, len(got)),
            [jax.ShapeDtypeStruct((packed, BLOCK), F32)] * 2,
            [own, *got],
            [vmem] * (1 + len(got)),
        )

    def half_width(value, mask):
        return exchange(value.astype(jnp.float16), mask).astype(F32)

    got = [half_width(payload[k - 1], k * lanes) for k in range(1, SQUARE)]
    own, packet = add_up(own, got)
    stride = SQUARE * lanes
    while stride < shards:
        own, packet = add_up(own, [half_width(packet, stride)])
        stride *= 2
    got = [half_width(packet, k * lanes) for k in range(1, SQUARE)]

    (finished,) = call(
        functools.partial(newton_kernel, scalar_lane),
        [jax.ShapeDtypeStruct((lanes * rows, columns), jnp.bfloat16)],
        [position, combined, own, *got],
        [smem] + [vmem] * (1 + SQUARE),
        pieces_scratch + [pltpu.VMEM((columns, columns), F32)],
        flops=13 * 2 * columns**3,
    )

    finished = finished.reshape(lanes, rows, columns)
    returned = [finished[0]] + [exchange(finished[k], k) for k in range(1, lanes)]
    if lanes == 2:
        first = lane_pos == 0
        ordered = [
            jnp.where(first, returned[0], returned[1]),
            jnp.where(first, returned[1], returned[0]),
        ]
    else:
        stacked = jnp.stack(returned)
        ordered = [
            lax.dynamic_index_in_dim(stacked, lane_pos ^ k, 0, keepdims=False)
            for k in range(lanes)
        ]
    updates = jnp.stack(ordered).astype(F32) * (MUON_SCALE * math.sqrt(full_rows))

    tiles = [own[per_piece : per_piece + 8]]
    if members <= 8:
        tiles += [exchange(tiles[0], flip[k]) for k in range(1, members)]
    else:
        stride = 1
        while stride < members:
            tiles = [tiles[0] + exchange(tiles[0], flip[stride])]
            stride *= 2
    (weights,) = call(
        functools.partial(weight_kernel, domains, len(tiles)),
        [jax.ShapeDtypeStruct((1, weight_share.shape[0]), F32)],
        [*tiles, weight_share[None], onehot, counts[None]],
        [vmem] * (len(tiles) + 3),
    )
    return (updates, weights[0])


def solution(mesh):
    placed = (P("domain", None, "fsdp", None), P(), P(), P())

    return jax.shard_map(
        body,
        mesh=mesh,
        in_specs=placed,
        out_specs=(P("domain", "fsdp", None), P()),
        check_vma=False,
    )
```

```python
import functools
import math

import jax
import jax.numpy as jnp
from jax import lax
from jax.experimental import pallas as pl
from jax.experimental.pallas import tpu as pltpu
from jax.sharding import PartitionSpec as P


NS_ITERS = 3
COEF_A = 3.4445
COEF_B = -4.775
COEF_C = 2.0315
MUON_SCALE = 0.2
ETA = 4.0

AXES = ("domain", "fsdp")
BLOCK = 128
SQUARE = 4
TAIL = 16
HALF_SPAN = 16384.0
TINY = 1e-30
VMEM_GRANT = 16 * 1024 * 1024
F32 = jnp.float32


def group_mixing(domain_ids, domain_weights, kind_count):
    weight_share = domain_weights / jnp.sum(domain_weights)
    onehot = (domain_ids[:, None] == jnp.arange(kind_count, dtype=jnp.int32)[None, :]).astype(F32)
    counts = jnp.sum(onehot, axis=0)
    per_member = weight_share / jnp.maximum(counts, 1.0)
    group_mix = jnp.sum(onehot * per_member[None, :], axis=1)
    return (weight_share, onehot, counts, group_mix)


def block_plan(columns):
    count = columns // BLOCK
    off = [(i, j) for i in range(count) for j in range(i + 1, count)]
    folded = [(i, i) for i in range(0, count, 2)]
    per_piece = (len(off) + len(folded)) // SQUARE
    pieces = []
    for p in range(SQUARE):
        take = per_piece - (1 if p >= SQUARE - len(folded) else 0)
        pieces.append([off.pop(0) for _ in range(take)])
    for n, pair in enumerate(folded):
        pieces[SQUARE - len(folded) + n].append(pair)
    return pieces


def lane_pick(row, index):
    lanes = lax.broadcasted_iota(jnp.int32, row.shape, 1)
    return jnp.sum(jnp.where(lanes == index, row, 0.0), axis=1, keepdims=True)


def encode_row(row):
    power = jnp.clip(jnp.floor(jnp.log2(jnp.abs(row))), -120.0, 120.0)
    scaled = row * jnp.exp2(-power)
    high = scaled.astype(jnp.bfloat16).astype(F32)
    rest = scaled - high
    mid = rest.astype(jnp.bfloat16).astype(F32)
    low = (rest - mid).astype(jnp.bfloat16).astype(F32)
    return (high, mid * 256.0, low * 65536.0, power)


def decode_row(parts):
    high, mid, low, power = parts
    return ((high + mid * (1.0 / 256.0)) + low * (1.0 / 65536.0)) * jnp.exp2(power)


def tail_rows(rows):
    index = lax.broadcasted_iota(jnp.int32, (TAIL, BLOCK), 0)
    out = jnp.zeros((TAIL, BLOCK), F32)
    for n, row in enumerate(rows):
        out = jnp.where(index == n, row, out)
    return out


def fetch_kernel(count, index_ref, source_ref, *refs):
    outs, sems = refs[:count], refs[count]
    copies = [
        pltpu.make_async_copy(source_ref.at[index_ref[n]], outs[n], sems.at[n])
        for n in range(count)
    ]
    for copy in copies:
        copy.start()
    for copy in copies:
        copy.wait()


def gram_kernel(domains, stage, last, mix_ref, lim_ref, pos_ref, *refs):
    blocks, refs = refs[:domains], refs[domains:]
    if stage:
        sofar_ref, scal_ref, refs = refs[0], refs[1], refs[2:]
    comb_ref, refs = refs[0], refs[1:]
    rows, columns = blocks[0].shape
    domain_pos, quad = pos_ref[0], pos_ref[1]

    def total(v):
        return jnp.sum(jnp.sum(v, axis=0, keepdims=True), axis=1, keepdims=True)

    keep = lax.broadcasted_iota(jnp.int32, (rows, 1), 0) < lim_ref[stage]
    masked = [jnp.where(keep, ref[...].astype(F32), 0.0) for ref in blocks]
    combined = mix_ref[0] * masked[0]
    for kd in range(1, domains):
        combined = combined + mix_ref[kd] * masked[kd]
    comb_ref[...] = combined
    rounded = combined.astype(jnp.bfloat16)
    gram = lax.dot_general(
        rounded, rounded, (((0,), (0,)), ((), ())), preferred_element_type=F32
    )
    lane = lax.broadcasted_iota(jnp.int32, (1, BLOCK), 1)
    scal = jnp.where(lane == 2 * domains, total(combined * combined), 0.0)
    for kd in range(domains):
        group = domain_pos ^ kd
        scal = jnp.where(lane == group, total(masked[kd] * combined), scal)
        scal = jnp.where(lane == domains + group, total(masked[kd] * masked[kd]), scal)
    if stage:
        scal = scal + scal_ref[0:1, :]
    if not last:
        gram_ref, sums_ref = refs
        gram_ref[...] = gram + sofar_ref[...] if stage else gram
        sums_ref[...] = jnp.broadcast_to(scal, sums_ref.shape)
        return

    pay_ref, own_ref, piece_ref, diag_ref = refs
    parts = encode_row(scal)
    scal = decode_row(parts)
    frob = lane_pick(scal, 2 * domains)
    scale = jnp.where(frob > TINY, HALF_SPAN / jnp.maximum(frob, TINY), 0.0)
    row_id = lax.broadcasted_iota(jnp.int32, (BLOCK, BLOCK), 0)
    col_id = lax.broadcasted_iota(jnp.int32, (BLOCK, BLOCK), 1)

    def part(i, j):
        value = gram[i * BLOCK : (i + 1) * BLOCK, j * BLOCK : (j + 1) * BLOCK]
        if stage:
            value = value + sofar_ref[pl.ds(i * BLOCK, BLOCK), pl.ds(j * BLOCK, BLOCK)]
        return value

    for p, entries in enumerate(block_plan(columns)):
        diag = jnp.zeros((1, BLOCK), F32)
        for n, (i, j) in enumerate(entries):
            if i == j:
                upper, lower = part(i, i), part(i + 1, i + 1)
                value = jnp.where(row_id < col_id, upper, lower)
                diag = jnp.sum(jnp.where(row_id == col_id, upper, 0.0), axis=0, keepdims=True)
            else:
                value = part(i, j)
            piece_ref[p, pl.ds(n * BLOCK, BLOCK), :] = value
        diag_ref[p] = jnp.broadcast_to(diag, diag_ref.shape[1:])
    body_rows = piece_ref.shape[1]
    for k in range(SQUARE):
        value = piece_ref[quad ^ k]
        diag = diag_ref[quad ^ k][0:1]
        if k == 0:
            own_ref[pl.ds(0, body_rows), :] = value
            own_ref[pl.ds(body_rows, TAIL), :] = tail_rows([diag, scal])
        else:
            pay_ref[k - 1, pl.ds(0, body_rows), :] = value * scale
            pay_ref[k - 1, pl.ds(body_rows, TAIL), :] = tail_rows([diag * scale, *parts])


def tree_sum(terms):
    while len(terms) > 1:
        terms = [terms[n] + terms[n + 1] for n in range(0, len(terms), 2)]
    return terms[0]


def sum_kernel(scalar_lane, count, tile_count, *refs):
    own_ref, got, refs = refs[0], refs[1 : 1 + count], refs[1 + count :]
    tiles, (out_ref, pay_ref) = refs[:tile_count], refs[tile_count:]
    body_rows = own_ref.shape[0] - TAIL

    def row(ref, n):
        return ref[pl.ds(body_rows + n, 1), :]

    scals = [row(own_ref, 1)] + [decode_row([row(ref, 1 + n) for n in range(4)]) for ref in got]
    scales = [1.0] + [lane_pick(scal, scalar_lane) * (1.0 / HALF_SPAN) for scal in scals[1:]]
    refs = (own_ref, *got)
    value = tree_sum([ref[pl.ds(0, body_rows), :] * x for ref, x in zip(refs, scales)])
    diag = tree_sum([row(ref, 0) * x for ref, x in zip(refs, scales)])
    scal = tree_sum(scals)
    if tile_count:
        every = tree_sum([ref[1:2, :] for ref in tiles])
    else:
        every = tree_sum(
            [row(own_ref, 2)] + [decode_row([row(ref, 5 + n) for n in range(4)]) for ref in got]
        )
    parts, every_parts = encode_row(scal), encode_row(every)
    scal, every = decode_row(parts), decode_row(every_parts)
    frob = lane_pick(scal, scalar_lane)
    scale = jnp.where(frob > TINY, HALF_SPAN / jnp.maximum(frob, TINY), 0.0)
    out_ref[pl.ds(0, body_rows), :] = value
    out_ref[pl.ds(body_rows, TAIL), :] = tail_rows([diag, scal, every])
    pay_ref[pl.ds(0, body_rows), :] = value * scale
    pay_ref[pl.ds(body_rows, TAIL), :] = tail_rows([diag * scale, *parts, *every_parts])


def newton_kernel(scalar_lane, lanes, pos_ref, own_ref, *refs):
    got, refs = refs[: SQUARE - 1], refs[SQUARE - 1 :]
    combs, (away_ref, stay_ref, poly_ref, piece_ref, diag_ref, gram_ref, start_ref) = (
        refs[:lanes],
        refs[lanes:],
    )
    quad = pos_ref[1]
    body_rows = own_ref.shape[0] - TAIL
    rows, columns = combs[0].shape
    scal = own_ref[pl.ds(body_rows + 1, 1), :]
    frob = lane_pick(scal, scalar_lane)
    inv = 1.0 / (jnp.sqrt(frob) + 1e-07)
    shared = (frob * inv) * inv * (1.0 / HALF_SPAN)
    for k in range(SQUARE):
        ref = own_ref if k == 0 else got[k - 1]
        value, diag = ref[pl.ds(0, body_rows), :], ref[pl.ds(body_rows, 1), :]
        if k == 0:
            value, diag = (value * inv) * inv, (diag * inv) * inv
        else:
            value, diag = value * shared, diag * shared
        piece_ref[quad ^ k] = value
        diag_ref[quad ^ k] = jnp.broadcast_to(diag, diag_ref.shape[1:])
    row_id = lax.broadcasted_iota(jnp.int32, (BLOCK, BLOCK), 0)
    col_id = lax.broadcasted_iota(jnp.int32, (BLOCK, BLOCK), 1)

    def place(i, j, value):
        gram_ref[pl.ds(i * BLOCK, BLOCK), pl.ds(j * BLOCK, BLOCK)] = value

    for p, entries in enumerate(block_plan(columns)):
        for n, (i, j) in enumerate(entries):
            value = piece_ref[p, pl.ds(n * BLOCK, BLOCK), :]
            flipped = value.T
            if i == j:
                diag = diag_ref[p][0:1]
                upper = jnp.where(row_id < col_id, value, jnp.where(row_id > col_id, flipped, diag))
                place(i, i, upper)
                place(i + 1, i + 1, jnp.where(row_id < col_id, flipped, value))
            else:
                place(i, j, value)
                place(j, i, flipped)

    def dot(x, y):
        return jnp.dot(x, y, preferred_element_type=F32)

    for kl in range(lanes):
        start_ref[pl.ds(kl * rows, rows), :] = (combs[kl][...] * inv).astype(jnp.bfloat16)
    gram = gram_ref[...]
    iterate = start_ref[...]
    for step in range(NS_ITERS):
        gram_low = gram.astype(jnp.bfloat16)
        square = dot(gram_low, gram_low)
        poly = (COEF_B * gram + COEF_C * square).astype(jnp.bfloat16)
        if step + 1 == NS_ITERS:
            away_ref[...] = newton_rows(iterate[rows:], poly)
            stay_ref[...] = iterate[:rows]
            poly_ref[...] = poly
            return
        iterate = newton_rows(iterate, poly)
        half = COEF_A * gram + dot(gram_low, poly)
        half_high = half.astype(jnp.bfloat16)
        half_low = (half - half_high.astype(F32)).astype(jnp.bfloat16)
        gram = COEF_A * half + dot(poly, half_high) + dot(poly, half_low)


def newton_rows(iterate, poly):
    moved = jnp.dot(iterate, poly, preferred_element_type=F32)
    return (COEF_A * iterate.astype(F32) + moved).astype(jnp.bfloat16)


def own_rows_kernel(stay_ref, poly_ref, out_ref):
    out_ref[...] = newton_rows(stay_ref[...], poly_ref[...])


def weight_kernel(domains, own_ref, *refs):
    got, (share_ref, onehot_ref, counts_ref, out_ref) = refs[:-4], refs[-4:]
    body_rows = own_ref.shape[0] - TAIL
    sums = tree_sum(
        [own_ref[pl.ds(body_rows + 2, 1), :]]
        + [decode_row([ref[pl.ds(body_rows + 5 + n, 1), :] for n in range(4)]) for ref in got]
    )
    norm = jnp.sqrt(lane_pick(sums, 2 * domains))
    score = jnp.zeros(share_ref.shape, F32)
    for g in range(domains):
        aligned, squares = lane_pick(sums, g), lane_pick(sums, domains + g)
        cosine = aligned / (jnp.sqrt(squares) * norm + 1e-06)
        score = score + onehot_ref[g : g + 1, :] * cosine
    score = score / jnp.maximum(counts_ref[...], 1.0)
    raised = share_ref[...] * jnp.exp(ETA * score)
    out_ref[...] = raised / jnp.sum(raised, axis=1, keepdims=True)


def call(kernel, out_shape, args, spaces, scratch=(), flops=0, grant=VMEM_GRANT):
    size = sum(math.prod(a.shape) * a.dtype.itemsize for a in (*args, *out_shape))
    return pl.pallas_call(
        kernel,
        out_shape=tuple(out_shape),
        in_specs=[pl.BlockSpec(memory_space=s) for s in spaces],
        out_specs=tuple(pl.BlockSpec(memory_space=pltpu.VMEM) for _ in out_shape),
        scratch_shapes=list(scratch),
        cost_estimate=pl.CostEstimate(flops=flops, bytes_accessed=size, transcendentals=0),
        compiler_params=pltpu.CompilerParams(vmem_limit_bytes=grant),
    )(*args)


def spread_order(members, lanes):
    return sorted(range(1, members), key=lambda k: k // lanes == 0)


def body(gradients, row_counts, domain_ids, domain_weights):
    domains = lax.axis_size("domain")
    shards = lax.axis_size("fsdp")
    matrices, rows, columns = gradients.shape[1:]
    lanes = matrices // domains
    sets = shards // lanes
    members = domains * lanes
    full_rows = rows * shards
    domain_pos = lax.axis_index("domain")
    shard_pos = lax.axis_index("fsdp")
    lane_pos = shard_pos % lanes
    set_pos = shard_pos // lanes
    member = domain_pos * lanes + lane_pos
    quad = set_pos % SQUARE
    flip = [(k // lanes) * shards + k % lanes for k in range(members)]

    def exchange(value, mask):
        return lax.ppermute(value, AXES, [(i, i ^ mask) for i in range(domains * shards)])

    vmem, smem, hbm = pltpu.VMEM, pltpu.SMEM, pltpu.HBM
    tile = jax.ShapeDtypeStruct((rows, columns), gradients.dtype)

    def fetch(wanted):
        index = jnp.stack([member ^ k for k in wanted]).astype(jnp.int32)
        return call(
            functools.partial(fetch_kernel, len(wanted)),
            [tile] * len(wanted),
            [index, gradients[0]],
            [smem, hbm],
            [pltpu.SemaphoreType.DMA((len(wanted),))],
        )

    if members <= 8:
        order = spread_order(members, lanes)
        ahead = lax.dynamic_index_in_dim(gradients[0], member ^ order[0], 0, keepdims=False)
        fetched = (ahead, *fetch(order[1:] + [0]))
        pieces = dict(zip(order + [0], fetched))
        got = {k: exchange(pieces[k], flip[k]) for k in order}
        got[0] = pieces[0]
        blocks = [got[k] for k in range(members)]
    else:
        teams = [
            [d * shards + s * lanes + l for d in range(domains) for l in range(lanes)]
            for s in range(sets)
        ]
        moved = lax.all_to_all(
            gradients[0], AXES, split_axis=0, concat_axis=0, axis_index_groups=teams, tiled=True
        )
        blocks = [
            lax.dynamic_index_in_dim(moved, member ^ k, 0, keepdims=False) for k in range(members)
        ]

    weight_share, onehot, counts, group_mix = group_mixing(
        domain_ids, domain_weights, domain_weights.shape[0]
    )
    mix = jnp.take(group_mix, domain_pos ^ jnp.arange(domains, dtype=jnp.int32))
    lane_row = (set_pos * lanes + (lane_pos ^ jnp.arange(lanes, dtype=jnp.int32))) * rows
    limits = lax.dynamic_index_in_dim(row_counts, member, 0, keepdims=False) - lane_row
    position = jnp.stack([domain_pos, quad, lane_pos]).astype(jnp.int32)

    per_piece = len(block_plan(columns)[0]) * BLOCK
    packed = per_piece + TAIL
    pieces_scratch = [
        pltpu.VMEM((SQUARE, per_piece, BLOCK), F32),
        pltpu.VMEM((SQUARE, 8, BLOCK), F32),
    ]
    square = jax.ShapeDtypeStruct((columns, columns), F32)
    combs, carried = [], []
    for kl in range(lanes):
        last = kl == lanes - 1
        results = [jax.ShapeDtypeStruct((rows, columns), F32)]
        if last:
            results += [
                jax.ShapeDtypeStruct((SQUARE - 1, packed, BLOCK), F32),
                jax.ShapeDtypeStruct((packed, BLOCK), F32),
            ]
        else:
            results += [square, jax.ShapeDtypeStruct((8, BLOCK), F32)]
        comb, *carried = call(
            functools.partial(gram_kernel, domains, kl, last),
            results,
            [mix, limits, position, *blocks[kl::lanes], *carried],
            [smem] * 3 + [vmem] * (domains + len(carried)),
            pieces_scratch if last else (),
            flops=2 * rows * columns * columns,
        )
        combs.append(comb)
    payload, own = carried
    scalar_lane = 2 * domains

    def add_up(own, got, tiles=()):
        return call(
            functools.partial(sum_kernel, scalar_lane, len(got), len(tiles)),
            [jax.ShapeDtypeStruct((packed, BLOCK), F32)] * 2,
            [own, *got, *tiles],
            [vmem] * (1 + len(got) + len(tiles)),
        )

    def half_width(value, mask):
        return exchange(value.astype(jnp.float16), mask).astype(F32)

    got = [half_width(payload[k - 1], k * lanes) for k in range(1, SQUARE)]
    tiles = [own[per_piece : per_piece + 8]]
    if members <= 8:
        tiles += [exchange(tiles[0], flip[k]) for k in range(1, members)]
    else:
        stride = 1
        while stride < members:
            tiles = [tiles[0] + exchange(tiles[0], flip[stride])]
            stride *= 2
    own, packet = add_up(own, got, tiles)
    stride = SQUARE * lanes
    while stride < shards:
        own, packet = add_up(own, [half_width(packet, stride)])
        stride *= 2
    got = [half_width(packet, k * lanes) for k in range(1, SQUARE)]

    away, stay, poly = call(
        functools.partial(newton_kernel, scalar_lane, lanes),
        [
            jax.ShapeDtypeStruct(((lanes - 1) * rows, columns), jnp.bfloat16),
            jax.ShapeDtypeStruct((rows, columns), jnp.bfloat16),
            jax.ShapeDtypeStruct((columns, columns), jnp.bfloat16),
        ],
        [position, own, *got, *combs],
        [smem] + [vmem] * (SQUARE + lanes),
        pieces_scratch
        + [pltpu.VMEM((columns, columns), F32), pltpu.VMEM((lanes * rows, columns), jnp.bfloat16)],
        flops=12 * 2 * columns**3,
    )
    away = away.reshape(lanes - 1, rows, columns)
    returned = [exchange(away[k - 1], k) for k in range(1, lanes)]
    (kept,) = call(
        own_rows_kernel,
        [jax.ShapeDtypeStruct((rows, columns), jnp.bfloat16)],
        [stay, poly],
        [vmem, vmem],
        flops=2 * rows * columns * columns,
    )
    (weights,) = call(
        functools.partial(weight_kernel, domains),
        [jax.ShapeDtypeStruct((1, weight_share.shape[0]), F32)],
        [own, *got, weight_share[None], onehot, counts[None]],
        [vmem] * (SQUARE + 3),
    )
    returned = [kept, *returned]
    if lanes == 2:
        first = lane_pos == 0
        ordered = [
            jnp.where(first, returned[0], returned[1]),
            jnp.where(first, returned[1], returned[0]),
        ]
    else:
        stacked = jnp.stack(returned)
        ordered = [
            lax.dynamic_index_in_dim(stacked, lane_pos ^ k, 0, keepdims=False)
            for k in range(lanes)
        ]
    updates = jnp.stack(ordered).astype(F32) * (MUON_SCALE * math.sqrt(full_rows))
    return (updates, weights[0])


def solution(mesh):
    placed = (P("domain", None, "fsdp", None), P(), P(), P())

    return jax.shard_map(
        body,
        mesh=mesh,
        in_specs=placed,
        out_specs=(P("domain", "fsdp", None), P()),
        check_vma=False,
    )
```

```python
import functools
import math

import jax
import jax.numpy as jnp
from jax import lax
from jax.experimental import pallas as pl
from jax.experimental.pallas import tpu as pltpu
from jax.sharding import PartitionSpec as P


NS_ITERS = 3
COEF_A = 3.4445
COEF_B = -4.775
COEF_C = 2.0315
MUON_SCALE = 0.2
ETA = 4.0

AXES = ("domain", "fsdp")
BLOCK = 128
SQUARE = 4
TAIL = 16
HALF_SPAN = 16384.0
TINY = 1e-30
VMEM_GRANT = 16 * 1024 * 1024
F32 = jnp.float32


def group_mixing(domain_ids, domain_weights, kind_count):
    weight_share = domain_weights / jnp.sum(domain_weights)
    onehot = (domain_ids[:, None] == jnp.arange(kind_count, dtype=jnp.int32)[None, :]).astype(F32)
    counts = jnp.sum(onehot, axis=0)
    per_member = weight_share / jnp.maximum(counts, 1.0)
    group_mix = jnp.sum(onehot * per_member[None, :], axis=1)
    return (weight_share, onehot, counts, group_mix)


def block_plan(columns):
    count = columns // BLOCK
    off = [(i, j) for i in range(count) for j in range(i + 1, count)]
    folded = [(i, i) for i in range(0, count, 2)]
    per_piece = (len(off) + len(folded)) // SQUARE
    pieces = []
    for p in range(SQUARE):
        take = per_piece - (1 if p >= SQUARE - len(folded) else 0)
        pieces.append([off.pop(0) for _ in range(take)])
    for n, pair in enumerate(folded):
        pieces[SQUARE - len(folded) + n].append(pair)
    return pieces


def lane_pick(row, index):
    lanes = lax.broadcasted_iota(jnp.int32, row.shape, 1)
    return jnp.sum(jnp.where(lanes == index, row, 0.0), axis=1, keepdims=True)


def encode_row(row):
    power = jnp.clip(jnp.floor(jnp.log2(jnp.abs(row))), -120.0, 120.0)
    scaled = row * jnp.exp2(-power)
    high = scaled.astype(jnp.bfloat16).astype(F32)
    rest = scaled - high
    mid = rest.astype(jnp.bfloat16).astype(F32)
    low = (rest - mid).astype(jnp.bfloat16).astype(F32)
    return (high, mid * 256.0, low * 65536.0, power)


def decode_row(parts):
    high, mid, low, power = parts
    return ((high + mid * (1.0 / 256.0)) + low * (1.0 / 65536.0)) * jnp.exp2(power)


def tail_rows(rows):
    index = lax.broadcasted_iota(jnp.int32, (TAIL, BLOCK), 0)
    out = jnp.zeros((TAIL, BLOCK), F32)
    for n, row in enumerate(rows):
        out = jnp.where(index == n, row, out)
    return out


def fetch_kernel(count, index_ref, source_ref, *refs):
    outs, sems = refs[:count], refs[count]
    copies = [
        pltpu.make_async_copy(source_ref.at[index_ref[n]], outs[n], sems.at[n])
        for n in range(count)
    ]
    for copy in copies:
        copy.start()
    for copy in copies:
        copy.wait()


def gram_kernel(domains, stage, last, mix_ref, lim_ref, pos_ref, *refs):
    blocks, refs = refs[:domains], refs[domains:]
    if stage:
        sofar_ref, scal_ref, refs = refs[0], refs[1], refs[2:]
    comb_ref, refs = refs[0], refs[1:]
    rows, columns = blocks[0].shape
    domain_pos, quad = pos_ref[0], pos_ref[1]

    def total(v):
        return jnp.sum(jnp.sum(v, axis=0, keepdims=True), axis=1, keepdims=True)

    keep = lax.broadcasted_iota(jnp.int32, (rows, 1), 0) < lim_ref[stage]
    masked = [jnp.where(keep, ref[...].astype(F32), 0.0) for ref in blocks]
    combined = mix_ref[0] * masked[0]
    for kd in range(1, domains):
        combined = combined + mix_ref[kd] * masked[kd]
    comb_ref[...] = combined
    rounded = combined.astype(jnp.bfloat16)
    gram = lax.dot_general(
        rounded, rounded, (((0,), (0,)), ((), ())), preferred_element_type=F32
    )
    lane = lax.broadcasted_iota(jnp.int32, (1, BLOCK), 1)
    scal = jnp.where(lane == 2 * domains, total(combined * combined), 0.0)
    for kd in range(domains):
        group = domain_pos ^ kd
        scal = jnp.where(lane == group, total(masked[kd] * combined), scal)
        scal = jnp.where(lane == domains + group, total(masked[kd] * masked[kd]), scal)
    if stage:
        scal = scal + scal_ref[0:1, :]
    if not last:
        gram_ref, sums_ref = refs
        gram_ref[...] = gram + sofar_ref[...] if stage else gram
        sums_ref[...] = jnp.broadcast_to(scal, sums_ref.shape)
        return

    pay_ref, own_ref, piece_ref, diag_ref = refs
    parts = encode_row(scal)
    scal = decode_row(parts)
    frob = lane_pick(scal, 2 * domains)
    scale = jnp.where(frob > TINY, HALF_SPAN / jnp.maximum(frob, TINY), 0.0)
    row_id = lax.broadcasted_iota(jnp.int32, (BLOCK, BLOCK), 0)
    col_id = lax.broadcasted_iota(jnp.int32, (BLOCK, BLOCK), 1)

    def part(i, j):
        value = gram[i * BLOCK : (i + 1) * BLOCK, j * BLOCK : (j + 1) * BLOCK]
        if stage:
            value = value + sofar_ref[pl.ds(i * BLOCK, BLOCK), pl.ds(j * BLOCK, BLOCK)]
        return value

    for p, entries in enumerate(block_plan(columns)):
        diag = jnp.zeros((1, BLOCK), F32)
        for n, (i, j) in enumerate(entries):
            if i == j:
                upper, lower = part(i, i), part(i + 1, i + 1)
                value = jnp.where(row_id < col_id, upper, lower)
                diag = jnp.sum(jnp.where(row_id == col_id, upper, 0.0), axis=0, keepdims=True)
            else:
                value = part(i, j)
            piece_ref[p, pl.ds(n * BLOCK, BLOCK), :] = value
        diag_ref[p] = jnp.broadcast_to(diag, diag_ref.shape[1:])
    body_rows = piece_ref.shape[1]
    for k in range(SQUARE):
        value = piece_ref[quad ^ k]
        diag = diag_ref[quad ^ k][0:1]
        if k == 0:
            own_ref[pl.ds(0, body_rows), :] = value
            own_ref[pl.ds(body_rows, TAIL), :] = tail_rows([diag, scal])
        else:
            pay_ref[k - 1, pl.ds(0, body_rows), :] = value * scale
            pay_ref[k - 1, pl.ds(body_rows, TAIL), :] = tail_rows([diag * scale, *parts])


def tree_sum(terms):
    while len(terms) > 1:
        terms = [terms[n] + terms[n + 1] for n in range(0, len(terms), 2)]
    return terms[0]


def sum_kernel(scalar_lane, count, tile_count, *refs):
    own_ref, got, refs = refs[0], refs[1 : 1 + count], refs[1 + count :]
    tiles, (out_ref, pay_ref) = refs[:tile_count], refs[tile_count:]
    body_rows = own_ref.shape[0] - TAIL

    def row(ref, n):
        return ref[pl.ds(body_rows + n, 1), :]

    scals = [row(own_ref, 1)] + [decode_row([row(ref, 1 + n) for n in range(4)]) for ref in got]
    scales = [1.0] + [lane_pick(scal, scalar_lane) * (1.0 / HALF_SPAN) for scal in scals[1:]]
    refs = (own_ref, *got)
    value = tree_sum([ref[pl.ds(0, body_rows), :] * x for ref, x in zip(refs, scales)])
    diag = tree_sum([row(ref, 0) * x for ref, x in zip(refs, scales)])
    scal = tree_sum(scals)
    if tile_count:
        every = tree_sum([ref[1:2, :] for ref in tiles])
    else:
        every = tree_sum(
            [row(own_ref, 2)] + [decode_row([row(ref, 5 + n) for n in range(4)]) for ref in got]
        )
    parts, every_parts = encode_row(scal), encode_row(every)
    scal, every = decode_row(parts), decode_row(every_parts)
    frob = lane_pick(scal, scalar_lane)
    scale = jnp.where(frob > TINY, HALF_SPAN / jnp.maximum(frob, TINY), 0.0)
    out_ref[pl.ds(0, body_rows), :] = value
    out_ref[pl.ds(body_rows, TAIL), :] = tail_rows([diag, scal, every])
    pay_ref[pl.ds(0, body_rows), :] = value * scale
    pay_ref[pl.ds(body_rows, TAIL), :] = tail_rows([diag * scale, *parts, *every_parts])


def newton_kernel(scalar_lane, lanes, pos_ref, own_ref, *refs):
    got, refs = refs[: SQUARE - 1], refs[SQUARE - 1 :]
    combs, (away_ref, stay_ref, poly_ref, piece_ref, diag_ref, gram_ref, start_ref) = (
        refs[:lanes],
        refs[lanes:],
    )
    quad = pos_ref[1]
    body_rows = own_ref.shape[0] - TAIL
    rows, columns = combs[0].shape
    scal = own_ref[pl.ds(body_rows + 1, 1), :]
    frob = lane_pick(scal, scalar_lane)
    inv = 1.0 / (jnp.sqrt(frob) + 1e-07)
    shared = (frob * inv) * inv * (1.0 / HALF_SPAN)
    for k in range(SQUARE):
        ref = own_ref if k == 0 else got[k - 1]
        value, diag = ref[pl.ds(0, body_rows), :], ref[pl.ds(body_rows, 1), :]
        if k == 0:
            value, diag = (value * inv) * inv, (diag * inv) * inv
        else:
            value, diag = value * shared, diag * shared
        piece_ref[quad ^ k] = value
        diag_ref[quad ^ k] = jnp.broadcast_to(diag, diag_ref.shape[1:])
    row_id = lax.broadcasted_iota(jnp.int32, (BLOCK, BLOCK), 0)
    col_id = lax.broadcasted_iota(jnp.int32, (BLOCK, BLOCK), 1)

    def place(i, j, value):
        gram_ref[pl.ds(i * BLOCK, BLOCK), pl.ds(j * BLOCK, BLOCK)] = value

    for p, entries in enumerate(block_plan(columns)):
        for n, (i, j) in enumerate(entries):
            value = piece_ref[p, pl.ds(n * BLOCK, BLOCK), :]
            flipped = value.T
            if i == j:
                diag = diag_ref[p][0:1]
                upper = jnp.where(row_id < col_id, value, jnp.where(row_id > col_id, flipped, diag))
                place(i, i, upper)
                place(i + 1, i + 1, jnp.where(row_id < col_id, flipped, value))
            else:
                place(i, j, value)
                place(j, i, flipped)

    def dot(x, y):
        return jnp.dot(x, y, preferred_element_type=F32)

    for kl in range(lanes):
        start_ref[pl.ds(kl * rows, rows), :] = (combs[kl][...] * inv).astype(jnp.bfloat16)
    gram = gram_ref[...]
    iterate = start_ref[...]
    for step in range(NS_ITERS):
        gram_low = gram.astype(jnp.bfloat16)
        square = dot(gram_low, gram_low)
        poly = (COEF_B * gram + COEF_C * square).astype(jnp.bfloat16)
        if step + 1 == NS_ITERS:
            away_ref[...] = newton_rows(iterate[rows:], poly)
            stay_ref[...] = iterate[:rows]
            poly_ref[...] = poly
            return
        iterate = newton_rows(iterate, poly)
        half = COEF_A * gram + dot(gram_low, poly)
        half_high = half.astype(jnp.bfloat16)
        half_low = (half - half_high.astype(F32)).astype(jnp.bfloat16)
        gram = COEF_A * half + dot(poly, half_high) + dot(poly, half_low)


def newton_rows(iterate, poly):
    moved = jnp.dot(iterate, poly, preferred_element_type=F32)
    return (COEF_A * iterate.astype(F32) + moved).astype(jnp.bfloat16)


def own_rows_kernel(stay_ref, poly_ref, out_ref):
    out_ref[...] = newton_rows(stay_ref[...], poly_ref[...])


def every_kernel(own_ref, *refs):
    got, out_ref = refs[:-1], refs[-1]
    body_rows = own_ref.shape[0] - TAIL
    sums = tree_sum(
        [own_ref[pl.ds(body_rows + 2, 1), :]]
        + [decode_row([ref[pl.ds(body_rows + 5 + n, 1), :] for n in range(4)]) for ref in got]
    )
    out_ref[...] = jnp.broadcast_to(sums, out_ref.shape)


def weight_kernel(domains, *refs):
    tiles, (share_ref, onehot_ref, counts_ref, out_ref) = refs[:-4], refs[-4:]
    sums = tree_sum([ref[0:1, :] for ref in tiles])
    norm = jnp.sqrt(lane_pick(sums, 2 * domains))
    score = jnp.zeros(share_ref.shape, F32)
    for g in range(domains):
        aligned, squares = lane_pick(sums, g), lane_pick(sums, domains + g)
        cosine = aligned / (jnp.sqrt(squares) * norm + 1e-06)
        score = score + onehot_ref[g : g + 1, :] * cosine
    score = score / jnp.maximum(counts_ref[...], 1.0)
    raised = share_ref[...] * jnp.exp(ETA * score)
    out_ref[...] = raised / jnp.sum(raised, axis=1, keepdims=True)


def call(kernel, out_shape, args, spaces, scratch=(), flops=0, grant=VMEM_GRANT):
    size = sum(math.prod(a.shape) * a.dtype.itemsize for a in (*args, *out_shape))
    return pl.pallas_call(
        kernel,
        out_shape=tuple(out_shape),
        in_specs=[pl.BlockSpec(memory_space=s) for s in spaces],
        out_specs=tuple(pl.BlockSpec(memory_space=pltpu.VMEM) for _ in out_shape),
        scratch_shapes=list(scratch),
        cost_estimate=pl.CostEstimate(flops=flops, bytes_accessed=size, transcendentals=0),
        compiler_params=pltpu.CompilerParams(vmem_limit_bytes=grant),
    )(*args)


def spread_order(members, lanes):
    return sorted(range(1, members), key=lambda k: k // lanes == 0)


def body(gradients, row_counts, domain_ids, domain_weights):
    domains = lax.axis_size("domain")
    shards = lax.axis_size("fsdp")
    matrices, rows, columns = gradients.shape[1:]
    lanes = matrices // domains
    sets = shards // lanes
    members = domains * lanes
    full_rows = rows * shards
    domain_pos = lax.axis_index("domain")
    shard_pos = lax.axis_index("fsdp")
    lane_pos = shard_pos % lanes
    set_pos = shard_pos // lanes
    member = domain_pos * lanes + lane_pos
    quad = set_pos % SQUARE
    flip = [(k // lanes) * shards + k % lanes for k in range(members)]

    def exchange(value, mask):
        return lax.ppermute(value, AXES, [(i, i ^ mask) for i in range(domains * shards)])

    vmem, smem, hbm = pltpu.VMEM, pltpu.SMEM, pltpu.HBM
    tile = jax.ShapeDtypeStruct((rows, columns), gradients.dtype)

    def fetch(wanted):
        index = jnp.stack([member ^ k for k in wanted]).astype(jnp.int32)
        return call(
            functools.partial(fetch_kernel, len(wanted)),
            [tile] * len(wanted),
            [index, gradients[0]],
            [smem, hbm],
            [pltpu.SemaphoreType.DMA((len(wanted),))],
        )

    if members <= 8:
        order = spread_order(members, lanes)
        ahead = lax.dynamic_index_in_dim(gradients[0], member ^ order[0], 0, keepdims=False)
        fetched = (ahead, *fetch(order[1:] + [0]))
        pieces = dict(zip(order + [0], fetched))
        got = {k: exchange(pieces[k], flip[k]) for k in order}
        got[0] = pieces[0]
        blocks = [got[k] for k in range(members)]
    else:
        teams = [
            [d * shards + s * lanes + l for d in range(domains) for l in range(lanes)]
            for s in range(sets)
        ]
        moved = lax.all_to_all(
            gradients[0], AXES, split_axis=0, concat_axis=0, axis_index_groups=teams, tiled=True
        )
        blocks = [
            lax.dynamic_index_in_dim(moved, member ^ k, 0, keepdims=False) for k in range(members)
        ]

    weight_share, onehot, counts, group_mix = group_mixing(
        domain_ids, domain_weights, domain_weights.shape[0]
    )
    mix = jnp.take(group_mix, domain_pos ^ jnp.arange(domains, dtype=jnp.int32))
    lane_row = (set_pos * lanes + (lane_pos ^ jnp.arange(lanes, dtype=jnp.int32))) * rows
    limits = lax.dynamic_index_in_dim(row_counts, member, 0, keepdims=False) - lane_row
    position = jnp.stack([domain_pos, quad, lane_pos]).astype(jnp.int32)

    per_piece = len(block_plan(columns)[0]) * BLOCK
    packed = per_piece + TAIL
    pieces_scratch = [
        pltpu.VMEM((SQUARE, per_piece, BLOCK), F32),
        pltpu.VMEM((SQUARE, 8, BLOCK), F32),
    ]
    square = jax.ShapeDtypeStruct((columns, columns), F32)
    combs, carried = [], []
    for kl in range(lanes):
        last = kl == lanes - 1
        results = [jax.ShapeDtypeStruct((rows, columns), F32)]
        if last:
            results += [
                jax.ShapeDtypeStruct((SQUARE - 1, packed, BLOCK), F32),
                jax.ShapeDtypeStruct((packed, BLOCK), F32),
            ]
        else:
            results += [square, jax.ShapeDtypeStruct((8, BLOCK), F32)]
        comb, *carried = call(
            functools.partial(gram_kernel, domains, kl, last),
            results,
            [mix, limits, position, *blocks[kl::lanes], *carried],
            [smem] * 3 + [vmem] * (domains + len(carried)),
            pieces_scratch if last else (),
            flops=2 * rows * columns * columns,
        )
        combs.append(comb)
    payload, own = carried
    scalar_lane = 2 * domains

    def add_up(own, got, tiles=()):
        return call(
            functools.partial(sum_kernel, scalar_lane, len(got), len(tiles)),
            [jax.ShapeDtypeStruct((packed, BLOCK), F32)] * 2,
            [own, *got, *tiles],
            [vmem] * (1 + len(got) + len(tiles)),
        )

    def half_width(value, mask):
        return exchange(value.astype(jnp.float16), mask).astype(F32)

    got = [half_width(payload[k - 1], k * lanes) for k in range(1, SQUARE)]
    tiles = [own[per_piece : per_piece + 8]]
    if domains <= 4:
        tiles += [exchange(tiles[0], kd * shards) for kd in range(1, domains)]
    else:
        stride = 1
        while stride < domains:
            tiles = [tiles[0] + exchange(tiles[0], stride * shards)]
            stride *= 2
    own, packet = add_up(own, got, tiles)
    stride = SQUARE * lanes
    while stride < shards:
        own, packet = add_up(own, [half_width(packet, stride)])
        stride *= 2
    got = [half_width(packet, k * lanes) for k in range(1, SQUARE)]

    (every,) = call(
        every_kernel, [jax.ShapeDtypeStruct((8, BLOCK), F32)], [own, *got], [vmem] * SQUARE
    )
    tiles, stride = [every], 1
    while stride < lanes:
        every = tree_sum(tiles)
        tiles = [every, exchange(every, stride)]
        stride *= 2

    away, stay, poly = call(
        functools.partial(newton_kernel, scalar_lane, lanes),
        [
            jax.ShapeDtypeStruct(((lanes - 1) * rows, columns), jnp.bfloat16),
            jax.ShapeDtypeStruct((rows, columns), jnp.bfloat16),
            jax.ShapeDtypeStruct((columns, columns), jnp.bfloat16),
        ],
        [position, own, *got, *combs],
        [smem] + [vmem] * (SQUARE + lanes),
        pieces_scratch
        + [pltpu.VMEM((columns, columns), F32), pltpu.VMEM((lanes * rows, columns), jnp.bfloat16)],
        flops=12 * 2 * columns**3,
    )
    away = away.reshape(lanes - 1, rows, columns)
    returned = [exchange(away[k - 1], k) for k in range(1, lanes)]
    (kept,) = call(
        own_rows_kernel,
        [jax.ShapeDtypeStruct((rows, columns), jnp.bfloat16)],
        [stay, poly],
        [vmem, vmem],
        flops=2 * rows * columns * columns,
    )
    (weights,) = call(
        functools.partial(weight_kernel, domains),
        [jax.ShapeDtypeStruct((1, weight_share.shape[0]), F32)],
        [*tiles, weight_share[None], onehot, counts[None]],
        [vmem] * (len(tiles) + 3),
    )
    returned = [kept, *returned]
    if lanes == 2:
        first = lane_pos == 0
        ordered = [
            jnp.where(first, returned[0], returned[1]),
            jnp.where(first, returned[1], returned[0]),
        ]
    else:
        stacked = jnp.stack(returned)
        ordered = [
            lax.dynamic_index_in_dim(stacked, lane_pos ^ k, 0, keepdims=False)
            for k in range(lanes)
        ]
    updates = jnp.stack(ordered).astype(F32) * (MUON_SCALE * math.sqrt(full_rows))
    return (updates, weights[0])


def solution(mesh):
    placed = (P("domain", None, "fsdp", None), P(), P(), P())

    return jax.shard_map(
        body,
        mesh=mesh,
        in_specs=placed,
        out_specs=(P("domain", "fsdp", None), P()),
        check_vma=False,
    )
```

```python
import functools
import math

import jax
import jax.numpy as jnp
from jax import lax
from jax.experimental import pallas as pl
from jax.experimental.pallas import tpu as pltpu
from jax.sharding import PartitionSpec as P


NS_ITERS = 3
COEF_A = 3.4445
COEF_B = -4.775
COEF_C = 2.0315
MUON_SCALE = 0.2
ETA = 4.0

AXES = ("domain", "fsdp")
BLOCK = 128
SQUARE = 4
TAIL = 16
HALF_SPAN = 16384.0
TINY = 1e-30
VMEM_GRANT = 16 * 1024 * 1024
F32 = jnp.float32


def group_mixing(domain_ids, domain_weights, kind_count):
    weight_share = domain_weights / jnp.sum(domain_weights)
    onehot = (domain_ids[:, None] == jnp.arange(kind_count, dtype=jnp.int32)[None, :]).astype(F32)
    counts = jnp.sum(onehot, axis=0)
    per_member = weight_share / jnp.maximum(counts, 1.0)
    group_mix = jnp.sum(onehot * per_member[None, :], axis=1)
    return (weight_share, onehot, counts, group_mix)


def block_plan(columns):
    count = columns // BLOCK
    off = [(i, j) for i in range(count) for j in range(i + 1, count)]
    folded = [(i, i) for i in range(0, count, 2)]
    per_piece = (len(off) + len(folded)) // SQUARE
    pieces = []
    for p in range(SQUARE):
        take = per_piece - (1 if p >= SQUARE - len(folded) else 0)
        pieces.append([off.pop(0) for _ in range(take)])
    for n, pair in enumerate(folded):
        pieces[SQUARE - len(folded) + n].append(pair)
    return pieces


def lane_pick(row, index):
    lanes = lax.broadcasted_iota(jnp.int32, row.shape, 1)
    return jnp.sum(jnp.where(lanes == index, row, 0.0), axis=1, keepdims=True)


def encode_row(row):
    power = jnp.clip(jnp.floor(jnp.log2(jnp.abs(row))), -120.0, 120.0)
    scaled = row * jnp.exp2(-power)
    high = scaled.astype(jnp.bfloat16).astype(F32)
    rest = scaled - high
    mid = rest.astype(jnp.bfloat16).astype(F32)
    low = (rest - mid).astype(jnp.bfloat16).astype(F32)
    return (high, mid * 256.0, low * 65536.0, power)


def decode_row(parts):
    high, mid, low, power = parts
    return ((high + mid * (1.0 / 256.0)) + low * (1.0 / 65536.0)) * jnp.exp2(power)


def tail_rows(rows):
    index = lax.broadcasted_iota(jnp.int32, (TAIL, BLOCK), 0)
    out = jnp.zeros((TAIL, BLOCK), F32)
    for n, row in enumerate(rows):
        out = jnp.where(index == n, row, out)
    return out


def fetch_kernel(count, index_ref, source_ref, *refs):
    outs, sems = refs[:count], refs[count]
    copies = [
        pltpu.make_async_copy(source_ref.at[index_ref[n]], outs[n], sems.at[n])
        for n in range(count)
    ]
    for copy in copies:
        copy.start()
    for copy in copies:
        copy.wait()


def gram_kernel(domains, stage, last, mix_ref, lim_ref, pos_ref, *refs):
    blocks, refs = refs[:domains], refs[domains:]
    if stage:
        sofar_ref, scal_ref, refs = refs[0], refs[1], refs[2:]
    comb_ref, refs = refs[0], refs[1:]
    _, columns = blocks[0].shape
    domain_pos, quad = pos_ref[0], pos_ref[1]

    def total(v):
        return jnp.sum(jnp.sum(v, axis=0, keepdims=True), axis=1, keepdims=True)

    keep = lim_ref[stage] > 0
    values = [ref[...].astype(F32) for ref in blocks]
    weights = [jnp.where(keep, mix_ref[kd], 0.0) for kd in range(domains)]
    combined = weights[0] * values[0]
    for kd in range(1, domains):
        combined = combined + weights[kd] * values[kd]
    comb_ref[...] = combined
    rounded = combined.astype(jnp.bfloat16)
    gram = lax.dot_general(
        rounded, rounded, (((0,), (0,)), ((), ())), preferred_element_type=F32
    )
    lane = lax.broadcasted_iota(jnp.int32, (1, BLOCK), 1)
    scal = jnp.where(lane == 2 * domains, total(combined * combined), 0.0)
    for kd in range(domains):
        group = domain_pos ^ kd
        square = jnp.where(keep, total(values[kd] * values[kd]), 0.0)
        scal = jnp.where(lane == group, total(values[kd] * combined), scal)
        scal = jnp.where(lane == domains + group, square, scal)
    if stage:
        scal = scal + scal_ref[0:1, :]
    if not last:
        gram_ref, sums_ref = refs
        gram_ref[...] = gram + sofar_ref[...] if stage else gram
        sums_ref[...] = jnp.broadcast_to(scal, sums_ref.shape)
        return

    (pay_ref,) = refs
    body_rows = pay_ref.shape[1] - TAIL
    parts = encode_row(scal)
    scal = decode_row(parts)
    frob = lane_pick(scal, 2 * domains)
    scale = jnp.where(frob > TINY, HALF_SPAN / jnp.maximum(frob, TINY), 0.0)
    row_id = lax.broadcasted_iota(jnp.int32, (BLOCK, BLOCK), 0)
    col_id = lax.broadcasted_iota(jnp.int32, (BLOCK, BLOCK), 1)

    def part(i, j):
        value = gram[i * BLOCK : (i + 1) * BLOCK, j * BLOCK : (j + 1) * BLOCK]
        if stage:
            value = value + sofar_ref[pl.ds(i * BLOCK, BLOCK), pl.ds(j * BLOCK, BLOCK)]
        return value

    for p, entries in enumerate(block_plan(columns)):
        slot = quad ^ p
        factor = jnp.where(slot == 0, 1.0, scale)
        diag = jnp.zeros((1, BLOCK), F32)
        for n, (i, j) in enumerate(entries):
            if i == j:
                upper, lower = part(i, i), part(i + 1, i + 1)
                value = jnp.where(row_id < col_id, upper, lower)
                diag = jnp.sum(jnp.where(row_id == col_id, upper, 0.0), axis=0, keepdims=True)
            else:
                value = part(i, j)
            pay_ref[slot, pl.ds(n * BLOCK, BLOCK), :] = value * factor
        own_tail = tail_rows([diag, scal])
        sent_tail = tail_rows([diag * scale, *parts])
        pay_ref[slot, pl.ds(body_rows, TAIL), :] = jnp.where(slot == 0, own_tail, sent_tail)


def tree_sum(terms):
    while len(terms) > 1:
        terms = [terms[n] + terms[n + 1] for n in range(0, len(terms), 2)]
    return terms[0]


def sum_kernel(scalar_lane, count, tile_count, *refs):
    own_ref, got, refs = refs[0], refs[1 : 1 + count], refs[1 + count :]
    tiles, (out_ref, pay_ref) = refs[:tile_count], refs[tile_count:]
    body_rows = own_ref.shape[0] - TAIL

    def row(ref, n):
        return ref[pl.ds(body_rows + n, 1), :]

    scals = [row(own_ref, 1)] + [decode_row([row(ref, 1 + n) for n in range(4)]) for ref in got]
    scales = [1.0] + [lane_pick(scal, scalar_lane) * (1.0 / HALF_SPAN) for scal in scals[1:]]
    refs = (own_ref, *got)
    value = tree_sum([ref[pl.ds(0, body_rows), :] * x for ref, x in zip(refs, scales)])
    diag = tree_sum([row(ref, 0) * x for ref, x in zip(refs, scales)])
    scal = tree_sum(scals)
    if tile_count:
        every = tree_sum([ref[1:2, :] for ref in tiles])
    else:
        every = tree_sum(
            [row(own_ref, 2)] + [decode_row([row(ref, 5 + n) for n in range(4)]) for ref in got]
        )
    parts, every_parts = encode_row(scal), encode_row(every)
    scal, every = decode_row(parts), decode_row(every_parts)
    frob = lane_pick(scal, scalar_lane)
    scale = jnp.where(frob > TINY, HALF_SPAN / jnp.maximum(frob, TINY), 0.0)
    out_ref[pl.ds(0, body_rows), :] = value
    out_ref[pl.ds(body_rows, TAIL), :] = tail_rows([diag, scal, every])
    pay_ref[pl.ds(0, body_rows), :] = value * scale
    pay_ref[pl.ds(body_rows, TAIL), :] = tail_rows([diag * scale, *parts, *every_parts])


def newton_kernel(scalar_lane, lanes, pos_ref, own_ref, *refs):
    got, refs = refs[: SQUARE - 1], refs[SQUARE - 1 :]
    combs, refs = refs[: lanes - 1], refs[lanes - 1 :]
    away_ref, poly_ref, inv_ref, piece_ref, diag_ref, gram_ref, start_ref = refs
    quad = pos_ref[1]
    body_rows = own_ref.shape[0] - TAIL
    rows, columns = combs[0].shape
    scal = own_ref[pl.ds(body_rows + 1, 1), :]
    frob = lane_pick(scal, scalar_lane)
    inv = 1.0 / (jnp.sqrt(frob) + 1e-07)
    shared = (frob * inv) * inv * (1.0 / HALF_SPAN)
    for k in range(SQUARE):
        ref = own_ref if k == 0 else got[k - 1]
        value, diag = ref[pl.ds(0, body_rows), :], ref[pl.ds(body_rows, 1), :]
        if k == 0:
            value, diag = (value * inv) * inv, (diag * inv) * inv
        else:
            value, diag = value * shared, diag * shared
        piece_ref[quad ^ k] = value
        diag_ref[quad ^ k] = jnp.broadcast_to(diag, diag_ref.shape[1:])
    row_id = lax.broadcasted_iota(jnp.int32, (BLOCK, BLOCK), 0)
    col_id = lax.broadcasted_iota(jnp.int32, (BLOCK, BLOCK), 1)

    def place(i, j, value):
        gram_ref[pl.ds(i * BLOCK, BLOCK), pl.ds(j * BLOCK, BLOCK)] = value

    for p, entries in enumerate(block_plan(columns)):
        for n, (i, j) in enumerate(entries):
            value = piece_ref[p, pl.ds(n * BLOCK, BLOCK), :]
            flipped = value.T
            if i == j:
                diag = diag_ref[p][0:1]
                upper = jnp.where(row_id < col_id, value, jnp.where(row_id > col_id, flipped, diag))
                place(i, i, upper)
                place(i + 1, i + 1, jnp.where(row_id < col_id, flipped, value))
            else:
                place(i, j, value)
                place(j, i, flipped)

    def dot(x, y):
        return jnp.dot(x, y, preferred_element_type=F32)

    inv_ref[...] = jnp.broadcast_to(inv, inv_ref.shape)
    for n, ref in enumerate(combs):
        start_ref[pl.ds(n * rows, rows), :] = (ref[...] * inv).astype(jnp.bfloat16)
    gram = gram_ref[...]
    iterate = start_ref[...]
    for step in range(NS_ITERS):
        gram_low = gram.astype(jnp.bfloat16)
        square = dot(gram_low, gram_low)
        poly = (COEF_B * gram + COEF_C * square).astype(jnp.bfloat16)
        poly_ref[step] = poly
        iterate = newton_rows(iterate, poly)
        if step + 1 == NS_ITERS:
            away_ref[...] = iterate
            return
        half = COEF_A * gram + dot(gram_low, poly)
        half_high = half.astype(jnp.bfloat16)
        half_low = (half - half_high.astype(F32)).astype(jnp.bfloat16)
        gram = COEF_A * half + dot(poly, half_high) + dot(poly, half_low)


def newton_rows(iterate, poly):
    moved = jnp.dot(iterate, poly, preferred_element_type=F32)
    return (COEF_A * iterate.astype(F32) + moved).astype(jnp.bfloat16)


def every_kernel(own_ref, *refs):
    got, out_ref = refs[:-1], refs[-1]
    body_rows = own_ref.shape[0] - TAIL
    sums = tree_sum(
        [own_ref[pl.ds(body_rows + 2, 1), :]]
        + [decode_row([ref[pl.ds(body_rows + 5 + n, 1), :] for n in range(4)]) for ref in got]
    )
    out_ref[...] = jnp.broadcast_to(sums, out_ref.shape)


def finish_kernel(domains, count, comb_ref, inv_ref, poly_ref, *refs):
    tiles, refs = refs[:count], refs[count:]
    share_ref, onehot_ref, counts_ref, rows_ref, out_ref, held_ref, sem = refs
    sums = tree_sum([ref[0:1, :] for ref in tiles])
    norm = jnp.sqrt(lane_pick(sums, 2 * domains))
    score = jnp.zeros(share_ref.shape, F32)
    for g in range(domains):
        aligned, squares = lane_pick(sums, g), lane_pick(sums, domains + g)
        cosine = aligned / (jnp.sqrt(squares) * norm + 1e-06)
        score = score + onehot_ref[g : g + 1, :] * cosine
    score = score / jnp.maximum(counts_ref[...], 1.0)
    raised = share_ref[...] * jnp.exp(ETA * score)
    held_ref[...] = raised / jnp.sum(raised, axis=1, keepdims=True)
    copy = pltpu.make_async_copy(held_ref, out_ref, sem)
    copy.start()
    iterate = (comb_ref[...] * inv_ref[0:1, 0:1]).astype(jnp.bfloat16)
    for step in range(NS_ITERS):
        iterate = newton_rows(iterate, poly_ref[step])
    rows_ref[...] = iterate
    copy.wait()


def call(kernel, out_shape, args, spaces, scratch=(), flops=0, outs=None):
    size = sum(math.prod(a.shape) * a.dtype.itemsize for a in (*args, *out_shape))
    outs = outs or [pltpu.VMEM] * len(out_shape)
    return pl.pallas_call(
        kernel,
        out_shape=tuple(out_shape),
        in_specs=[pl.BlockSpec(memory_space=s) for s in spaces],
        out_specs=tuple(pl.BlockSpec(memory_space=s) for s in outs),
        scratch_shapes=list(scratch),
        cost_estimate=pl.CostEstimate(flops=flops, bytes_accessed=size, transcendentals=0),
        compiler_params=pltpu.CompilerParams(vmem_limit_bytes=VMEM_GRANT),
    )(*args)


def spread_order(members, lanes):
    return sorted(range(1, members), key=lambda k: k // lanes == 0)


def body(gradients, row_counts, domain_ids, domain_weights):
    domains = lax.axis_size("domain")
    shards = lax.axis_size("fsdp")
    matrices, rows, columns = gradients.shape[1:]
    lanes = matrices // domains
    sets = shards // lanes
    members = domains * lanes
    full_rows = rows * shards
    domain_pos = lax.axis_index("domain")
    shard_pos = lax.axis_index("fsdp")
    lane_pos = shard_pos % lanes
    set_pos = shard_pos // lanes
    member = domain_pos * lanes + lane_pos
    quad = set_pos % SQUARE
    flip = [(k // lanes) * shards + k % lanes for k in range(members)]

    def exchange(value, mask):
        return lax.ppermute(value, AXES, [(i, i ^ mask) for i in range(domains * shards)])

    vmem, smem, hbm = pltpu.VMEM, pltpu.SMEM, pltpu.HBM
    tile = jax.ShapeDtypeStruct((rows, columns), gradients.dtype)

    def fetch(wanted):
        index = jnp.stack([member ^ k for k in wanted]).astype(jnp.int32)
        return call(
            functools.partial(fetch_kernel, len(wanted)),
            [tile] * len(wanted),
            [index, gradients[0]],
            [smem, hbm],
            [pltpu.SemaphoreType.DMA((len(wanted),))],
        )

    if members <= 8:
        order = spread_order(members, lanes)
        ahead = lax.dynamic_index_in_dim(gradients[0], member ^ order[0], 0, keepdims=False)
        fetched = (ahead, *fetch(order[1:] + [0]))
        pieces = dict(zip(order + [0], fetched))
        got = {k: exchange(pieces[k], flip[k]) for k in order}
        got[0] = pieces[0]
        blocks = [got[k] for k in range(members)]
    else:
        teams = [
            [d * shards + s * lanes + l for d in range(domains) for l in range(lanes)]
            for s in range(sets)
        ]
        moved = lax.all_to_all(
            gradients[0], AXES, split_axis=0, concat_axis=0, axis_index_groups=teams, tiled=True
        )
        blocks = [
            lax.dynamic_index_in_dim(moved, member ^ k, 0, keepdims=False) for k in range(members)
        ]

    weight_share, onehot, counts, group_mix = group_mixing(
        domain_ids, domain_weights, domain_weights.shape[0]
    )
    mix = jnp.take(group_mix, domain_pos ^ jnp.arange(domains, dtype=jnp.int32))
    lane_row = (set_pos * lanes + (lane_pos ^ jnp.arange(lanes, dtype=jnp.int32))) * rows
    limits = lax.dynamic_index_in_dim(row_counts, member, 0, keepdims=False) - lane_row
    position = jnp.stack([domain_pos, quad, lane_pos]).astype(jnp.int32)

    per_piece = len(block_plan(columns)[0]) * BLOCK
    packed = per_piece + TAIL
    pieces_scratch = [
        pltpu.VMEM((SQUARE, per_piece, BLOCK), F32),
        pltpu.VMEM((SQUARE, 8, BLOCK), F32),
    ]
    square = jax.ShapeDtypeStruct((columns, columns), F32)
    combs, carried = [], []
    for kl in range(lanes):
        last = kl == lanes - 1
        results = [jax.ShapeDtypeStruct((rows, columns), F32)]
        if last:
            results += [jax.ShapeDtypeStruct((SQUARE, packed, BLOCK), F32)]
        else:
            results += [square, jax.ShapeDtypeStruct((8, BLOCK), F32)]
        comb, *carried = call(
            functools.partial(gram_kernel, domains, kl, last),
            results,
            [mix, limits, position, *blocks[kl::lanes], *carried],
            [smem] * 3 + [vmem] * (domains + len(carried)),
            flops=2 * rows * columns * columns,
        )
        combs.append(comb)
    (payload,) = carried
    own = payload[0]
    scalar_lane = 2 * domains

    def add_up(own, got, tiles=()):
        return call(
            functools.partial(sum_kernel, scalar_lane, len(got), len(tiles)),
            [jax.ShapeDtypeStruct((packed, BLOCK), F32)] * 2,
            [own, *got, *tiles],
            [vmem] * (1 + len(got) + len(tiles)),
        )

    def half_width(value, mask):
        return exchange(value.astype(jnp.float16), mask).astype(F32)

    got = [half_width(payload[k], k * lanes) for k in range(1, SQUARE)]
    tiles = [own[per_piece : per_piece + 8]]
    if domains <= 4:
        tiles += [exchange(tiles[0], kd * shards) for kd in range(1, domains)]
    else:
        stride = 1
        while stride < domains:
            tiles = [tiles[0] + exchange(tiles[0], stride * shards)]
            stride *= 2
    own, packet = add_up(own, got, tiles)
    stride = SQUARE * lanes
    while stride < shards:
        own, packet = add_up(own, [half_width(packet, stride)])
        stride *= 2
    got = [half_width(packet, k * lanes) for k in range(1, SQUARE)]

    (every,) = call(
        every_kernel, [jax.ShapeDtypeStruct((8, BLOCK), F32)], [own, *got], [vmem] * SQUARE
    )
    tiles, stride = [every], 1
    while stride < lanes:
        every = tree_sum(tiles)
        tiles = [every, exchange(every, stride)]
        stride *= 2

    away, poly, inv = call(
        functools.partial(newton_kernel, scalar_lane, lanes),
        [
            jax.ShapeDtypeStruct(((lanes - 1) * rows, columns), jnp.bfloat16),
            jax.ShapeDtypeStruct((NS_ITERS, columns, columns), jnp.bfloat16),
            jax.ShapeDtypeStruct((8, BLOCK), F32),
        ],
        [position, own, *got, *combs[1:]],
        [smem] + [vmem] * (SQUARE + lanes - 1),
        pieces_scratch
        + [
            pltpu.VMEM((columns, columns), F32),
            pltpu.VMEM(((lanes - 1) * rows, columns), jnp.bfloat16),
        ],
        flops=10 * 2 * columns**3,
    )
    away = away.reshape(lanes - 1, rows, columns)
    returned = [exchange(away[k - 1], k) for k in range(1, lanes)]
    kinds = jax.ShapeDtypeStruct((1, weight_share.shape[0]), F32)
    kept, weights = call(
        functools.partial(finish_kernel, domains, len(tiles)),
        [jax.ShapeDtypeStruct((rows, columns), jnp.bfloat16), kinds],
        [combs[0], inv, poly, *tiles, weight_share[None], onehot, counts[None]],
        [vmem] * (6 + len(tiles)),
        [pltpu.VMEM(kinds.shape, F32), pltpu.SemaphoreType.DMA],
        flops=NS_ITERS * 2 * rows * columns * columns,
        outs=[vmem, hbm],
    )
    returned = [kept, *returned]
    if lanes == 2:
        first = lane_pos == 0
        ordered = [
            jnp.where(first, returned[0], returned[1]),
            jnp.where(first, returned[1], returned[0]),
        ]
    else:
        stacked = jnp.stack(returned)
        ordered = [
            lax.dynamic_index_in_dim(stacked, lane_pos ^ k, 0, keepdims=False)
            for k in range(lanes)
        ]
    updates = jnp.stack(ordered).astype(F32) * (MUON_SCALE * math.sqrt(full_rows))
    return (updates, weights[0])


def solution(mesh):
    placed = (P("domain", None, "fsdp", None), P(), P(), P())

    return jax.shard_map(
        body,
        mesh=mesh,
        in_specs=placed,
        out_specs=(P("domain", "fsdp", None), P()),
        check_vma=False,
    )
```

```python
import functools
import math

import jax
import jax.numpy as jnp
from jax import lax
from jax.experimental import pallas as pl
from jax.experimental.pallas import tpu as pltpu
from jax.sharding import PartitionSpec as P


NS_ITERS = 3
COEF_A = 3.4445
COEF_B = -4.775
COEF_C = 2.0315
MUON_SCALE = 0.2
ETA = 4.0

AXES = ("domain", "fsdp")
BLOCK = 128
SQUARE = 4
TAIL = 16
HALF_SPAN = 16384.0
TINY = 1e-30
VMEM_GRANT = 16 * 1024 * 1024
F32 = jnp.float32


def group_mixing(domain_ids, domain_weights, kind_count):
    weight_share = domain_weights / jnp.sum(domain_weights)
    onehot = (domain_ids[:, None] == jnp.arange(kind_count, dtype=jnp.int32)[None, :]).astype(F32)
    counts = jnp.sum(onehot, axis=0)
    per_member = weight_share / jnp.maximum(counts, 1.0)
    group_mix = jnp.sum(onehot * per_member[None, :], axis=1)
    return (weight_share, onehot, counts, group_mix)


def block_plan(columns):
    count = columns // BLOCK
    off = [(i, j) for i in range(count) for j in range(i + 1, count)]
    folded = [(i, i) for i in range(0, count, 2)]
    per_piece = (len(off) + len(folded)) // SQUARE
    pieces = []
    for p in range(SQUARE):
        take = per_piece - (1 if p >= SQUARE - len(folded) else 0)
        pieces.append([off.pop(0) for _ in range(take)])
    for n, pair in enumerate(folded):
        pieces[SQUARE - len(folded) + n].append(pair)
    return pieces


def lane_pick(row, index):
    lanes = lax.broadcasted_iota(jnp.int32, row.shape, 1)
    return jnp.sum(jnp.where(lanes == index, row, 0.0), axis=1, keepdims=True)


def encode_row(row):
    power = jnp.clip(jnp.floor(jnp.log2(jnp.abs(row))), -120.0, 120.0)
    scaled = row * jnp.exp2(-power)
    high = scaled.astype(jnp.bfloat16).astype(F32)
    rest = scaled - high
    mid = rest.astype(jnp.bfloat16).astype(F32)
    low = (rest - mid).astype(jnp.bfloat16).astype(F32)
    return (high, mid * 256.0, low * 65536.0, power)


def decode_row(parts):
    high, mid, low, power = parts
    return ((high + mid * (1.0 / 256.0)) + low * (1.0 / 65536.0)) * jnp.exp2(power)


def tail_rows(rows):
    index = lax.broadcasted_iota(jnp.int32, (TAIL, BLOCK), 0)
    out = jnp.zeros((TAIL, BLOCK), F32)
    for n, row in enumerate(rows):
        out = jnp.where(index == n, row, out)
    return out


def fetch_kernel(count, index_ref, source_ref, *refs):
    outs, sems = refs[:count], refs[count]
    copies = [
        pltpu.make_async_copy(source_ref.at[index_ref[n]], outs[n], sems.at[n])
        for n in range(count)
    ]
    for copy in copies:
        copy.start()
    for copy in copies:
        copy.wait()


def gram_kernel(domains, stage, last, mix_ref, lim_ref, pos_ref, *refs):
    blocks, refs = refs[:domains], refs[domains:]
    if stage:
        sofar_ref, scal_ref, refs = refs[0], refs[1], refs[2:]
    comb_ref, refs = refs[0], refs[1:]
    _, columns = blocks[0].shape
    domain_pos, quad = pos_ref[0], pos_ref[1]

    def total(v):
        return jnp.sum(jnp.sum(v, axis=0, keepdims=True), axis=1, keepdims=True)

    keep = lim_ref[stage] > 0
    values = [ref[...].astype(F32) for ref in blocks]
    weights = [jnp.where(keep, mix_ref[kd], 0.0) for kd in range(domains)]
    combined = weights[0] * values[0]
    for kd in range(1, domains):
        combined = combined + weights[kd] * values[kd]
    comb_ref[...] = combined
    rounded = combined.astype(jnp.bfloat16)
    half_width = columns // 2

    def inner(x, y):
        return lax.dot_general(x, y, (((0,), (0,)), ((), ())), preferred_element_type=F32)

    gram_top = inner(rounded[:, :half_width], rounded)
    gram_low = inner(rounded[:, half_width:], rounded[:, half_width:])
    lane = lax.broadcasted_iota(jnp.int32, (1, BLOCK), 1)
    frob = total(combined * combined)
    scal = jnp.where(lane == 2 * domains, frob, 0.0)
    for kd in range(domains):
        group = domain_pos ^ kd
        square = jnp.where(keep, total(values[kd] * values[kd]), 0.0)
        scal = jnp.where(lane == group, total(values[kd] * combined), scal)
        scal = jnp.where(lane == domains + group, square, scal)
    if stage:
        frob = frob + lane_pick(scal_ref[0:1, :], 2 * domains)
        scal = scal + scal_ref[0:1, :]
    if not last:
        gram_ref, sums_ref = refs
        top, low = pl.ds(0, half_width), pl.ds(half_width, half_width)
        gram_ref[top, :] = gram_top + sofar_ref[top, :] if stage else gram_top
        gram_ref[low, low] = gram_low + sofar_ref[low, low] if stage else gram_low
        sums_ref[...] = jnp.broadcast_to(scal, sums_ref.shape)
        return

    (pay_ref,) = refs
    body_rows = pay_ref.shape[1] - TAIL
    parts = encode_row(scal)
    scal = decode_row(parts)
    scale = jnp.where(frob > TINY, HALF_SPAN / jnp.maximum(frob, TINY), 0.0)
    row_id = lax.broadcasted_iota(jnp.int32, (BLOCK, BLOCK), 0)
    col_id = lax.broadcasted_iota(jnp.int32, (BLOCK, BLOCK), 1)

    def part(i, j):
        source, shift = (gram_top, 0) if i * BLOCK < half_width else (gram_low, half_width)
        row, column = i * BLOCK - shift, j * BLOCK - shift
        value = source[row : row + BLOCK, column : column + BLOCK]
        if stage:
            value = value + sofar_ref[pl.ds(i * BLOCK, BLOCK), pl.ds(j * BLOCK, BLOCK)]
        return value

    for p, entries in enumerate(block_plan(columns)):
        slot = quad ^ p
        factor = jnp.where(slot == 0, 1.0, scale)
        diag = jnp.zeros((1, BLOCK), F32)
        for n, (i, j) in enumerate(entries):
            if i == j:
                upper, lower = part(i, i), part(i + 1, i + 1)
                value = jnp.where(row_id < col_id, upper, lower)
                diag = jnp.sum(jnp.where(row_id == col_id, upper, 0.0), axis=0, keepdims=True)
            else:
                value = part(i, j)
            pay_ref[slot, pl.ds(n * BLOCK, BLOCK), :] = value * factor
        own_tail = tail_rows([diag, scal])
        sent_tail = tail_rows([diag * scale, *parts])
        pay_ref[slot, pl.ds(body_rows, TAIL), :] = jnp.where(slot == 0, own_tail, sent_tail)


def tree_sum(terms):
    while len(terms) > 1:
        terms = [terms[n] + terms[n + 1] for n in range(0, len(terms), 2)]
    return terms[0]


def sum_kernel(scalar_lane, count, tile_count, *refs):
    own_ref, got, refs = refs[0], refs[1 : 1 + count], refs[1 + count :]
    tiles, (out_ref, pay_ref) = refs[:tile_count], refs[tile_count:]
    body_rows = own_ref.shape[0] - TAIL

    def row(ref, n):
        return ref[pl.ds(body_rows + n, 1), :]

    scals = [row(own_ref, 1)] + [decode_row([row(ref, 1 + n) for n in range(4)]) for ref in got]
    scales = [1.0] + [lane_pick(scal, scalar_lane) * (1.0 / HALF_SPAN) for scal in scals[1:]]
    refs = (own_ref, *got)
    value = tree_sum([ref[pl.ds(0, body_rows), :] * x for ref, x in zip(refs, scales)])
    diag = tree_sum([row(ref, 0) * x for ref, x in zip(refs, scales)])
    scal = tree_sum(scals)
    if tile_count:
        every = tree_sum([ref[1:2, :] for ref in tiles])
    else:
        every = tree_sum(
            [row(own_ref, 2)] + [decode_row([row(ref, 5 + n) for n in range(4)]) for ref in got]
        )
    frob = lane_pick(scal, scalar_lane)
    parts, every_parts = encode_row(scal), encode_row(every)
    scal, every = decode_row(parts), decode_row(every_parts)
    scale = jnp.where(frob > TINY, HALF_SPAN / jnp.maximum(frob, TINY), 0.0)
    out_ref[pl.ds(0, body_rows), :] = value
    out_ref[pl.ds(body_rows, TAIL), :] = tail_rows([diag, scal, every])
    pay_ref[pl.ds(0, body_rows), :] = value * scale
    pay_ref[pl.ds(body_rows, TAIL), :] = tail_rows([diag * scale, *parts, *every_parts])


def newton_kernel(scalar_lane, lanes, pos_ref, own_ref, *refs):
    got, refs = refs[: SQUARE - 1], refs[SQUARE - 1 :]
    combs, refs = refs[: lanes - 1], refs[lanes - 1 :]
    away_ref, poly_ref, inv_ref, piece_ref, diag_ref, gram_ref, start_ref, near_ref = refs
    quad = pos_ref[1]
    body_rows = own_ref.shape[0] - TAIL
    rows, columns = combs[0].shape
    scal = own_ref[pl.ds(body_rows + 1, 1), :]
    frob = lane_pick(scal, scalar_lane)
    inv = 1.0 / (jnp.sqrt(frob) + 1e-07)
    shared = (frob * inv) * inv * (1.0 / HALF_SPAN)
    for k in range(SQUARE):
        ref = own_ref if k == 0 else got[k - 1]
        value, diag = ref[pl.ds(0, body_rows), :], ref[pl.ds(body_rows, 1), :]
        if k == 0:
            value, diag = (value * inv) * inv, (diag * inv) * inv
        else:
            value, diag = value * shared, diag * shared
        piece_ref[quad ^ k] = value
        diag_ref[quad ^ k] = jnp.broadcast_to(diag, diag_ref.shape[1:])
    row_id = lax.broadcasted_iota(jnp.int32, (BLOCK, BLOCK), 0)
    col_id = lax.broadcasted_iota(jnp.int32, (BLOCK, BLOCK), 1)

    def place(i, j, value):
        gram_ref[pl.ds(i * BLOCK, BLOCK), pl.ds(j * BLOCK, BLOCK)] = value

    for p, entries in enumerate(block_plan(columns)):
        for n, (i, j) in enumerate(entries):
            value = piece_ref[p, pl.ds(n * BLOCK, BLOCK), :]
            flipped = value.T
            if i == j:
                diag = diag_ref[p][0:1]
                upper = jnp.where(row_id < col_id, value, jnp.where(row_id > col_id, flipped, diag))
                place(i, i, upper)
                place(i + 1, i + 1, jnp.where(row_id < col_id, flipped, value))
            else:
                place(i, j, value)
                place(j, i, flipped)

    def dot(x, y):
        return jnp.dot(x, y, preferred_element_type=F32)

    inv_ref[...] = jnp.broadcast_to(inv, inv_ref.shape)
    for n, ref in enumerate(combs):
        start_ref[pl.ds(n * rows, rows), :] = (ref[...] * inv).astype(jnp.bfloat16)
    half_width = columns // 2
    top, low = pl.ds(0, half_width), pl.ds(half_width, half_width)
    iterate = start_ref[...]
    gram_top, gram_low = gram_ref[top, :], gram_ref[low, low]
    for step in range(NS_ITERS):
        mirror(near_ref.at[step], gram_top.astype(jnp.bfloat16), gram_low.astype(jnp.bfloat16))
        near = near_ref[step]
        square_top = dot(near[:half_width], near)
        square_low = dot(near[half_width:], near[:, half_width:])
        mirror(
            poly_ref.at[step],
            (COEF_B * gram_top + COEF_C * square_top).astype(jnp.bfloat16),
            (COEF_B * gram_low + COEF_C * square_low).astype(jnp.bfloat16),
        )
        if step:
            iterate = newton_rows(iterate, poly)
        poly = poly_ref[step]
        if step + 1 == NS_ITERS:
            away_ref[...] = newton_rows(iterate, poly)
            return
        moved = dot(near, poly)
        left = gram_top[:, half_width:].T
        half_top = COEF_A * gram_top + moved[:half_width]
        half_low = COEF_A * jnp.concatenate([left, gram_low], axis=1) + moved[half_width:]
        half = jnp.concatenate([half_top, half_low], axis=0)
        high = half.astype(jnp.bfloat16)
        rest = (half - high.astype(F32)).astype(jnp.bfloat16)
        gram_top = COEF_A * half_top + dot(poly[:half_width], high) + dot(poly[:half_width], rest)
        gram_low = (
            COEF_A * half_low[:, half_width:]
            + dot(poly[half_width:], high[:, half_width:])
            + dot(poly[half_width:], rest[:, half_width:])
        )


def mirror(ref, top_value, low_value):
    half_width = low_value.shape[0]
    top, low = pl.ds(0, half_width), pl.ds(half_width, half_width)
    ref[top, :] = top_value
    ref[low, top] = top_value[:, half_width:].T
    ref[low, low] = low_value


def newton_rows(iterate, poly):
    moved = jnp.dot(iterate, poly, preferred_element_type=F32)
    return (COEF_A * iterate.astype(F32) + moved).astype(jnp.bfloat16)


def every_kernel(own_ref, *refs):
    got, out_ref = refs[:-1], refs[-1]
    body_rows = own_ref.shape[0] - TAIL
    sums = tree_sum(
        [own_ref[pl.ds(body_rows + 2, 1), :]]
        + [decode_row([ref[pl.ds(body_rows + 5 + n, 1), :] for n in range(4)]) for ref in got]
    )
    out_ref[...] = jnp.broadcast_to(sums, out_ref.shape)


def finish_kernel(domains, count, comb_ref, inv_ref, poly_ref, *refs):
    tiles, refs = refs[:count], refs[count:]
    share_ref, onehot_ref, counts_ref, rows_ref, out_ref, held_ref, sem = refs
    sums = tree_sum([ref[0:1, :] for ref in tiles])
    norm = jnp.sqrt(lane_pick(sums, 2 * domains))
    score = jnp.zeros(share_ref.shape, F32)
    for g in range(domains):
        aligned, squares = lane_pick(sums, g), lane_pick(sums, domains + g)
        cosine = aligned / (jnp.sqrt(squares) * norm + 1e-06)
        score = score + onehot_ref[g : g + 1, :] * cosine
    score = score / jnp.maximum(counts_ref[...], 1.0)
    raised = share_ref[...] * jnp.exp(ETA * score)
    held_ref[...] = raised / jnp.sum(raised, axis=1, keepdims=True)
    copy = pltpu.make_async_copy(held_ref, out_ref, sem)
    copy.start()
    iterate = (comb_ref[...] * inv_ref[0:1, 0:1]).astype(jnp.bfloat16)
    for step in range(NS_ITERS):
        iterate = newton_rows(iterate, poly_ref[step])
    rows_ref[...] = iterate
    copy.wait()


def call(kernel, out_shape, args, spaces, scratch=(), flops=0, outs=None):
    size = sum(math.prod(a.shape) * a.dtype.itemsize for a in (*args, *out_shape))
    outs = outs or [pltpu.VMEM] * len(out_shape)
    return pl.pallas_call(
        kernel,
        out_shape=tuple(out_shape),
        in_specs=[pl.BlockSpec(memory_space=s) for s in spaces],
        out_specs=tuple(pl.BlockSpec(memory_space=s) for s in outs),
        scratch_shapes=list(scratch),
        cost_estimate=pl.CostEstimate(flops=flops, bytes_accessed=size, transcendentals=0),
        compiler_params=pltpu.CompilerParams(vmem_limit_bytes=VMEM_GRANT),
    )(*args)


def spread_order(members, lanes):
    return sorted(range(1, members), key=lambda k: k // lanes == 0)


def body(gradients, row_counts, domain_ids, domain_weights):
    domains = lax.axis_size("domain")
    shards = lax.axis_size("fsdp")
    matrices, rows, columns = gradients.shape[1:]
    lanes = matrices // domains
    sets = shards // lanes
    members = domains * lanes
    full_rows = rows * shards
    domain_pos = lax.axis_index("domain")
    shard_pos = lax.axis_index("fsdp")
    lane_pos = shard_pos % lanes
    set_pos = shard_pos // lanes
    member = domain_pos * lanes + lane_pos
    quad = set_pos % SQUARE
    flip = [(k // lanes) * shards + k % lanes for k in range(members)]

    def exchange(value, mask):
        return lax.ppermute(value, AXES, [(i, i ^ mask) for i in range(domains * shards)])

    vmem, smem, hbm = pltpu.VMEM, pltpu.SMEM, pltpu.HBM
    tile = jax.ShapeDtypeStruct((rows, columns), gradients.dtype)

    def fetch(wanted):
        index = jnp.stack([member ^ k for k in wanted]).astype(jnp.int32)
        return call(
            functools.partial(fetch_kernel, len(wanted)),
            [tile] * len(wanted),
            [index, gradients[0]],
            [smem, hbm],
            [pltpu.SemaphoreType.DMA((len(wanted),))],
        )

    if members <= 8:
        order = spread_order(members, lanes)
        ahead = lax.dynamic_index_in_dim(gradients[0], member ^ order[0], 0, keepdims=False)
        fetched = (ahead, *fetch(order[1:] + [0]))
        pieces = dict(zip(order + [0], fetched))
        got = {k: exchange(pieces[k], flip[k]) for k in order}
        got[0] = pieces[0]
        blocks = [got[k] for k in range(members)]
    else:
        teams = [
            [d * shards + s * lanes + l for d in range(domains) for l in range(lanes)]
            for s in range(sets)
        ]
        moved = lax.all_to_all(
            gradients[0], AXES, split_axis=0, concat_axis=0, axis_index_groups=teams, tiled=True
        )
        blocks = [
            lax.dynamic_index_in_dim(moved, member ^ k, 0, keepdims=False) for k in range(members)
        ]

    weight_share, onehot, counts, group_mix = group_mixing(
        domain_ids, domain_weights, domain_weights.shape[0]
    )
    mix = jnp.take(group_mix, domain_pos ^ jnp.arange(domains, dtype=jnp.int32))
    lane_row = (set_pos * lanes + (lane_pos ^ jnp.arange(lanes, dtype=jnp.int32))) * rows
    limits = lax.dynamic_index_in_dim(row_counts, member, 0, keepdims=False) - lane_row
    position = jnp.stack([domain_pos, quad, lane_pos]).astype(jnp.int32)

    per_piece = len(block_plan(columns)[0]) * BLOCK
    packed = per_piece + TAIL
    pieces_scratch = [
        pltpu.VMEM((SQUARE, per_piece, BLOCK), F32),
        pltpu.VMEM((SQUARE, 8, BLOCK), F32),
    ]
    square = jax.ShapeDtypeStruct((columns, columns), F32)
    combs, carried = [], []
    for kl in range(lanes):
        last = kl == lanes - 1
        results = [jax.ShapeDtypeStruct((rows, columns), F32)]
        if last:
            results += [jax.ShapeDtypeStruct((SQUARE, packed, BLOCK), F32)]
        else:
            results += [square, jax.ShapeDtypeStruct((8, BLOCK), F32)]
        comb, *carried = call(
            functools.partial(gram_kernel, domains, kl, last),
            results,
            [mix, limits, position, *blocks[kl::lanes], *carried],
            [smem] * 3 + [vmem] * (domains + len(carried)),
            flops=2 * rows * columns * columns,
        )
        combs.append(comb)
    (payload,) = carried
    own = payload[0]
    scalar_lane = 2 * domains

    def add_up(own, got, tiles=()):
        return call(
            functools.partial(sum_kernel, scalar_lane, len(got), len(tiles)),
            [jax.ShapeDtypeStruct((packed, BLOCK), F32)] * 2,
            [own, *got, *tiles],
            [vmem] * (1 + len(got) + len(tiles)),
        )

    def half_width(value, mask):
        return exchange(value.astype(jnp.float16), mask).astype(F32)

    got = [half_width(payload[k], k * lanes) for k in range(1, SQUARE)]
    tiles = [own[per_piece : per_piece + 8]]
    if domains <= 4:
        tiles += [exchange(tiles[0], kd * shards) for kd in range(1, domains)]
    else:
        stride = 1
        while stride < domains:
            tiles = [tiles[0] + exchange(tiles[0], stride * shards)]
            stride *= 2
    own, packet = add_up(own, got, tiles)
    stride = SQUARE * lanes
    while stride < shards:
        own, packet = add_up(own, [half_width(packet, stride)])
        stride *= 2
    got = [half_width(packet, k * lanes) for k in range(1, SQUARE)]

    (every,) = call(
        every_kernel, [jax.ShapeDtypeStruct((8, BLOCK), F32)], [own, *got], [vmem] * SQUARE
    )
    tiles, stride = [every], 1
    while stride < lanes:
        every = tree_sum(tiles)
        tiles = [every, exchange(every, stride)]
        stride *= 2

    away, poly, inv = call(
        functools.partial(newton_kernel, scalar_lane, lanes),
        [
            jax.ShapeDtypeStruct(((lanes - 1) * rows, columns), jnp.bfloat16),
            jax.ShapeDtypeStruct((NS_ITERS, columns, columns), jnp.bfloat16),
            jax.ShapeDtypeStruct((8, BLOCK), F32),
        ],
        [position, own, *got, *combs[1:]],
        [smem] + [vmem] * (SQUARE + lanes - 1),
        pieces_scratch
        + [
            pltpu.VMEM((columns, columns), F32),
            pltpu.VMEM(((lanes - 1) * rows, columns), jnp.bfloat16),
            pltpu.VMEM((NS_ITERS, columns, columns), jnp.bfloat16),
        ],
        flops=9 * 2 * columns**3,
    )
    away = away.reshape(lanes - 1, rows, columns)
    returned = [exchange(away[k - 1], k) for k in range(1, lanes)]
    kinds = jax.ShapeDtypeStruct((1, weight_share.shape[0]), F32)
    kept, weights = call(
        functools.partial(finish_kernel, domains, len(tiles)),
        [jax.ShapeDtypeStruct((rows, columns), jnp.bfloat16), kinds],
        [combs[0], inv, poly, *tiles, weight_share[None], onehot, counts[None]],
        [vmem] * (6 + len(tiles)),
        [pltpu.VMEM(kinds.shape, F32), pltpu.SemaphoreType.DMA],
        flops=NS_ITERS * 2 * rows * columns * columns,
        outs=[vmem, hbm],
    )
    returned = [kept, *returned]
    if lanes == 2:
        first = lane_pos == 0
        ordered = [
            jnp.where(first, returned[0], returned[1]),
            jnp.where(first, returned[1], returned[0]),
        ]
    else:
        stacked = jnp.stack(returned)
        ordered = [
            lax.dynamic_index_in_dim(stacked, lane_pos ^ k, 0, keepdims=False)
            for k in range(lanes)
        ]
    updates = jnp.stack(ordered).astype(F32) * (MUON_SCALE * math.sqrt(full_rows))
    return (updates, weights[0])


def solution(mesh):
    placed = (P("domain", None, "fsdp", None), P(), P(), P())

    return jax.shard_map(
        body,
        mesh=mesh,
        in_specs=placed,
        out_specs=(P("domain", "fsdp", None), P()),
        check_vma=False,
    )
```

```python
import functools
import math

import jax
import jax.numpy as jnp
from jax import lax
from jax.experimental import pallas as pl
from jax.experimental.pallas import tpu as pltpu
from jax.sharding import PartitionSpec as P


NS_ITERS = 3
COEF_A = 3.4445
COEF_B = -4.775
COEF_C = 2.0315
MUON_SCALE = 0.2
ETA = 4.0

AXES = ("domain", "fsdp")
BLOCK = 128
SQUARE = 4
TAIL = 16
HALF_SPAN = 16384.0
TINY = 1e-30
VMEM_GRANT = 16 * 1024 * 1024
F32 = jnp.float32


def group_mixing(domain_ids, domain_weights, kind_count):
    weight_share = domain_weights / jnp.sum(domain_weights)
    onehot = (domain_ids[:, None] == jnp.arange(kind_count, dtype=jnp.int32)[None, :]).astype(F32)
    counts = jnp.sum(onehot, axis=0)
    per_member = weight_share / jnp.maximum(counts, 1.0)
    group_mix = jnp.sum(onehot * per_member[None, :], axis=1)
    return (weight_share, onehot, counts, group_mix)


def block_plan(columns):
    count = columns // BLOCK
    off = [(i, j) for i in range(count) for j in range(i + 1, count)]
    folded = [(i, i) for i in range(0, count, 2)]
    per_piece = (len(off) + len(folded)) // SQUARE
    pieces = []
    for p in range(SQUARE):
        take = per_piece - (1 if p >= SQUARE - len(folded) else 0)
        pieces.append([off.pop(0) for _ in range(take)])
    for n, pair in enumerate(folded):
        pieces[SQUARE - len(folded) + n].append(pair)
    return pieces


def lane_pick(row, index):
    lanes = lax.broadcasted_iota(jnp.int32, row.shape, 1)
    return jnp.sum(jnp.where(lanes == index, row, 0.0), axis=1, keepdims=True)


def encode_row(row):
    power = jnp.clip(jnp.floor(jnp.log2(jnp.abs(row))), -120.0, 120.0)
    scaled = row * jnp.exp2(-power)
    high = scaled.astype(jnp.bfloat16).astype(F32)
    rest = scaled - high
    mid = rest.astype(jnp.bfloat16).astype(F32)
    low = (rest - mid).astype(jnp.bfloat16).astype(F32)
    return (high, mid * 256.0, low * 65536.0, power)


def decode_row(parts):
    high, mid, low, power = parts
    return ((high + mid * (1.0 / 256.0)) + low * (1.0 / 65536.0)) * jnp.exp2(power)


def tail_rows(rows):
    index = lax.broadcasted_iota(jnp.int32, (TAIL, BLOCK), 0)
    out = jnp.zeros((TAIL, BLOCK), F32)
    for n, row in enumerate(rows):
        out = jnp.where(index == n, row, out)
    return out


def fetch_kernel(count, index_ref, source_ref, *refs):
    outs, sems = refs[:count], refs[count]
    copies = [
        pltpu.make_async_copy(source_ref.at[index_ref[n]], outs[n], sems.at[n])
        for n in range(count)
    ]
    for copy in copies:
        copy.start()
    for copy in copies:
        copy.wait()


def gram_kernel(domains, stage, last, mix_ref, lim_ref, pos_ref, *refs):
    blocks, refs = refs[:domains], refs[domains:]
    if stage:
        sofar_ref, scal_ref, refs = refs[0], refs[1], refs[2:]
    comb_ref, refs = refs[0], refs[1:]
    _, columns = blocks[0].shape
    domain_pos, quad = pos_ref[0], pos_ref[1]

    def total(v):
        return jnp.sum(jnp.sum(v, axis=0, keepdims=True), axis=1, keepdims=True)

    keep = lim_ref[stage] > 0
    values = [ref[...].astype(F32) for ref in blocks]
    weights = [jnp.where(keep, mix_ref[kd], 0.0) for kd in range(domains)]
    combined = weights[0] * values[0]
    for kd in range(1, domains):
        combined = combined + weights[kd] * values[kd]
    comb_ref[...] = combined
    rounded = combined.astype(jnp.bfloat16)
    half_width = columns // 2

    def inner(x, y):
        return lax.dot_general(x, y, (((0,), (0,)), ((), ())), preferred_element_type=F32)

    gram_top = inner(rounded[:, :half_width], rounded)
    gram_low = inner(rounded[:, half_width:], rounded[:, half_width:])
    lane = lax.broadcasted_iota(jnp.int32, (1, BLOCK), 1)
    frob = total(combined * combined)
    scal = jnp.where(lane == 2 * domains, frob, 0.0)
    for kd in range(domains):
        group = domain_pos ^ kd
        square = jnp.where(keep, total(values[kd] * values[kd]), 0.0)
        scal = jnp.where(lane == group, total(values[kd] * combined), scal)
        scal = jnp.where(lane == domains + group, square, scal)
    if stage:
        frob = frob + lane_pick(scal_ref[0:1, :], 2 * domains)
        scal = scal + scal_ref[0:1, :]
    if not last:
        gram_ref, sums_ref = refs
        top, low = pl.ds(0, half_width), pl.ds(half_width, half_width)
        gram_ref[top, :] = gram_top + sofar_ref[top, :] if stage else gram_top
        gram_ref[low, low] = gram_low + sofar_ref[low, low] if stage else gram_low
        sums_ref[...] = jnp.broadcast_to(scal, sums_ref.shape)
        return

    (pay_ref,) = refs
    body_rows = pay_ref.shape[1] - TAIL
    parts = encode_row(scal)
    scal = decode_row(parts)
    scale = jnp.where(frob > TINY, HALF_SPAN / jnp.maximum(frob, TINY), 0.0)
    row_id = lax.broadcasted_iota(jnp.int32, (BLOCK, BLOCK), 0)
    col_id = lax.broadcasted_iota(jnp.int32, (BLOCK, BLOCK), 1)

    def part(i, j):
        source, shift = (gram_top, 0) if i * BLOCK < half_width else (gram_low, half_width)
        row, column = i * BLOCK - shift, j * BLOCK - shift
        value = source[row : row + BLOCK, column : column + BLOCK]
        if stage:
            value = value + sofar_ref[pl.ds(i * BLOCK, BLOCK), pl.ds(j * BLOCK, BLOCK)]
        return value

    for p, entries in enumerate(block_plan(columns)):
        slot = quad ^ p
        factor = jnp.where(slot == 0, 1.0, scale)
        diag = jnp.zeros((1, BLOCK), F32)
        for n, (i, j) in enumerate(entries):
            if i == j:
                upper, lower = part(i, i), part(i + 1, i + 1)
                value = jnp.where(row_id < col_id, upper, lower)
                diag = jnp.sum(jnp.where(row_id == col_id, upper, 0.0), axis=0, keepdims=True)
            else:
                value = part(i, j)
            pay_ref[slot, pl.ds(n * BLOCK, BLOCK), :] = value * factor
        own_tail = tail_rows([diag, scal])
        sent_tail = tail_rows([diag * scale, *parts])
        pay_ref[slot, pl.ds(body_rows, TAIL), :] = jnp.where(slot == 0, own_tail, sent_tail)


def tree_sum(terms):
    while len(terms) > 1:
        terms = [terms[n] + terms[n + 1] for n in range(0, len(terms), 2)]
    return terms[0]


def sum_kernel(scalar_lane, count, tile_count, *refs):
    own_ref, got, refs = refs[0], refs[1 : 1 + count], refs[1 + count :]
    tiles, (out_ref, pay_ref) = refs[:tile_count], refs[tile_count:]
    body_rows = own_ref.shape[0] - TAIL

    def row(ref, n):
        return ref[pl.ds(body_rows + n, 1), :]

    scals = [row(own_ref, 1)] + [decode_row([row(ref, 1 + n) for n in range(4)]) for ref in got]
    scales = [1.0] + [lane_pick(scal, scalar_lane) * (1.0 / HALF_SPAN) for scal in scals[1:]]
    refs = (own_ref, *got)
    value = tree_sum([ref[pl.ds(0, body_rows), :] * x for ref, x in zip(refs, scales)])
    diag = tree_sum([row(ref, 0) * x for ref, x in zip(refs, scales)])
    scal = tree_sum(scals)
    if tile_count:
        every = tree_sum([ref[1:2, :] for ref in tiles])
    else:
        every = tree_sum(
            [row(own_ref, 2)] + [decode_row([row(ref, 5 + n) for n in range(4)]) for ref in got]
        )
    frob = lane_pick(scal, scalar_lane)
    parts, every_parts = encode_row(scal), encode_row(every)
    scal, every = decode_row(parts), decode_row(every_parts)
    scale = jnp.where(frob > TINY, HALF_SPAN / jnp.maximum(frob, TINY), 0.0)
    out_ref[pl.ds(0, body_rows), :] = value
    out_ref[pl.ds(body_rows, TAIL), :] = tail_rows([diag, scal, every])
    pay_ref[pl.ds(0, body_rows), :] = value * scale
    pay_ref[pl.ds(body_rows, TAIL), :] = tail_rows([diag * scale, *parts, *every_parts])


def newton_kernel(scalar_lane, lanes, pos_ref, own_ref, *refs):
    got, refs = refs[: SQUARE - 1], refs[SQUARE - 1 :]
    combs, refs = refs[: lanes - 1], refs[lanes - 1 :]
    away_ref, poly_ref, inv_ref, piece_ref, diag_ref, gram_ref, start_ref = refs
    quad = pos_ref[1]
    body_rows = own_ref.shape[0] - TAIL
    rows, columns = combs[0].shape
    scal = own_ref[pl.ds(body_rows + 1, 1), :]
    frob = lane_pick(scal, scalar_lane)
    inv = 1.0 / (jnp.sqrt(frob) + 1e-07)
    shared = (frob * inv) * inv * (1.0 / HALF_SPAN)
    for k in range(SQUARE):
        ref = own_ref if k == 0 else got[k - 1]
        value, diag = ref[pl.ds(0, body_rows), :], ref[pl.ds(body_rows, 1), :]
        if k == 0:
            value, diag = (value * inv) * inv, (diag * inv) * inv
        else:
            value, diag = value * shared, diag * shared
        piece_ref[quad ^ k] = value
        diag_ref[quad ^ k] = jnp.broadcast_to(diag, diag_ref.shape[1:])
    row_id = lax.broadcasted_iota(jnp.int32, (BLOCK, BLOCK), 0)
    col_id = lax.broadcasted_iota(jnp.int32, (BLOCK, BLOCK), 1)

    def place(i, j, value):
        gram_ref[pl.ds(i * BLOCK, BLOCK), pl.ds(j * BLOCK, BLOCK)] = value

    for p, entries in enumerate(block_plan(columns)):
        for n, (i, j) in enumerate(entries):
            value = piece_ref[p, pl.ds(n * BLOCK, BLOCK), :]
            flipped = value.T
            if i == j:
                diag = diag_ref[p][0:1]
                upper = jnp.where(row_id < col_id, value, jnp.where(row_id > col_id, flipped, diag))
                place(i, i, upper)
                place(i + 1, i + 1, jnp.where(row_id < col_id, flipped, value))
            else:
                place(i, j, value)
                place(j, i, flipped)

    def dot(x, y):
        return jnp.dot(x, y, preferred_element_type=F32)

    inv_ref[...] = jnp.broadcast_to(inv, inv_ref.shape)
    for n, ref in enumerate(combs):
        start_ref[pl.ds(n * rows, rows), :] = (ref[...] * inv).astype(jnp.bfloat16)
    half_width = columns // 2
    top, low = pl.ds(0, half_width), pl.ds(half_width, half_width)
    iterate = start_ref[...]
    gram = gram_ref[...]
    for step in range(NS_ITERS):
        near = gram.astype(jnp.bfloat16)
        if step:
            iterate = newton_rows(iterate, poly)
        poly = (COEF_B * gram + COEF_C * dot(near, near)).astype(jnp.bfloat16)
        poly_ref[step] = poly
        if step + 1 == NS_ITERS:
            away_ref[...] = newton_rows(iterate, poly)
            return
        half = COEF_A * gram + dot(near, poly)
        high = half.astype(jnp.bfloat16)
        rest = (half - high.astype(F32)).astype(jnp.bfloat16)
        gram_ref[top, :] = (
            COEF_A * half[:half_width]
            + dot(poly[:half_width], high)
            + dot(poly[:half_width], rest)
        )
        gram_ref[low, low] = (
            COEF_A * half[half_width:, half_width:]
            + dot(poly[half_width:], high[:, half_width:])
            + dot(poly[half_width:], rest[:, half_width:])
        )
        gram_ref[low, top] = gram_ref[top, low].T
        gram = gram_ref[...]


def newton_rows(iterate, poly):
    moved = jnp.dot(iterate, poly, preferred_element_type=F32)
    return (COEF_A * iterate.astype(F32) + moved).astype(jnp.bfloat16)


def every_kernel(own_ref, *refs):
    got, out_ref = refs[:-1], refs[-1]
    body_rows = own_ref.shape[0] - TAIL
    sums = tree_sum(
        [own_ref[pl.ds(body_rows + 2, 1), :]]
        + [decode_row([ref[pl.ds(body_rows + 5 + n, 1), :] for n in range(4)]) for ref in got]
    )
    out_ref[...] = jnp.broadcast_to(sums, out_ref.shape)


def finish_kernel(domains, count, comb_ref, inv_ref, poly_ref, *refs):
    tiles, refs = refs[:count], refs[count:]
    share_ref, onehot_ref, counts_ref, rows_ref, out_ref, held_ref, sem = refs
    sums = tree_sum([ref[0:1, :] for ref in tiles])
    norm = jnp.sqrt(lane_pick(sums, 2 * domains))
    score = jnp.zeros(share_ref.shape, F32)
    for g in range(domains):
        aligned, squares = lane_pick(sums, g), lane_pick(sums, domains + g)
        cosine = aligned / (jnp.sqrt(squares) * norm + 1e-06)
        score = score + onehot_ref[g : g + 1, :] * cosine
    score = score / jnp.maximum(counts_ref[...], 1.0)
    raised = share_ref[...] * jnp.exp(ETA * score)
    held_ref[...] = raised / jnp.sum(raised, axis=1, keepdims=True)
    copy = pltpu.make_async_copy(held_ref, out_ref, sem)
    copy.start()
    iterate = (comb_ref[...] * inv_ref[0:1, 0:1]).astype(jnp.bfloat16)
    for step in range(NS_ITERS):
        iterate = newton_rows(iterate, poly_ref[step])
    rows_ref[...] = iterate
    copy.wait()


def call(kernel, out_shape, args, spaces, scratch=(), flops=0, outs=None):
    size = sum(math.prod(a.shape) * a.dtype.itemsize for a in (*args, *out_shape))
    outs = outs or [pltpu.VMEM] * len(out_shape)
    return pl.pallas_call(
        kernel,
        out_shape=tuple(out_shape),
        in_specs=[pl.BlockSpec(memory_space=s) for s in spaces],
        out_specs=tuple(pl.BlockSpec(memory_space=s) for s in outs),
        scratch_shapes=list(scratch),
        cost_estimate=pl.CostEstimate(flops=flops, bytes_accessed=size, transcendentals=0),
        compiler_params=pltpu.CompilerParams(vmem_limit_bytes=VMEM_GRANT),
    )(*args)


def spread_order(members, lanes):
    return sorted(range(1, members), key=lambda k: k // lanes == 0)


def body(gradients, row_counts, domain_ids, domain_weights):
    domains = lax.axis_size("domain")
    shards = lax.axis_size("fsdp")
    matrices, rows, columns = gradients.shape[1:]
    lanes = matrices // domains
    sets = shards // lanes
    members = domains * lanes
    full_rows = rows * shards
    domain_pos = lax.axis_index("domain")
    shard_pos = lax.axis_index("fsdp")
    lane_pos = shard_pos % lanes
    set_pos = shard_pos // lanes
    member = domain_pos * lanes + lane_pos
    quad = set_pos % SQUARE
    flip = [(k // lanes) * shards + k % lanes for k in range(members)]

    def exchange(value, mask):
        return lax.ppermute(value, AXES, [(i, i ^ mask) for i in range(domains * shards)])

    vmem, smem, hbm = pltpu.VMEM, pltpu.SMEM, pltpu.HBM
    tile = jax.ShapeDtypeStruct((rows, columns), gradients.dtype)

    def fetch(wanted):
        index = jnp.stack([member ^ k for k in wanted]).astype(jnp.int32)
        return call(
            functools.partial(fetch_kernel, len(wanted)),
            [tile] * len(wanted),
            [index, gradients[0]],
            [smem, hbm],
            [pltpu.SemaphoreType.DMA((len(wanted),))],
        )

    if members <= 8:
        order = spread_order(members, lanes)
        ahead = lax.dynamic_index_in_dim(gradients[0], member ^ order[0], 0, keepdims=False)
        fetched = (ahead, *fetch(order[1:] + [0]))
        pieces = dict(zip(order + [0], fetched))
        got = {k: exchange(pieces[k], flip[k]) for k in order}
        got[0] = pieces[0]
        blocks = [got[k] for k in range(members)]
    else:
        teams = [
            [d * shards + s * lanes + l for d in range(domains) for l in range(lanes)]
            for s in range(sets)
        ]
        moved = lax.all_to_all(
            gradients[0], AXES, split_axis=0, concat_axis=0, axis_index_groups=teams, tiled=True
        )
        blocks = [
            lax.dynamic_index_in_dim(moved, member ^ k, 0, keepdims=False) for k in range(members)
        ]

    weight_share, onehot, counts, group_mix = group_mixing(
        domain_ids, domain_weights, domain_weights.shape[0]
    )
    mix = jnp.take(group_mix, domain_pos ^ jnp.arange(domains, dtype=jnp.int32))
    lane_row = (set_pos * lanes + (lane_pos ^ jnp.arange(lanes, dtype=jnp.int32))) * rows
    limits = lax.dynamic_index_in_dim(row_counts, member, 0, keepdims=False) - lane_row
    position = jnp.stack([domain_pos, quad, lane_pos]).astype(jnp.int32)

    per_piece = len(block_plan(columns)[0]) * BLOCK
    packed = per_piece + TAIL
    pieces_scratch = [
        pltpu.VMEM((SQUARE, per_piece, BLOCK), F32),
        pltpu.VMEM((SQUARE, 8, BLOCK), F32),
    ]
    square = jax.ShapeDtypeStruct((columns, columns), F32)
    combs, carried = [], []
    for kl in range(lanes):
        last = kl == lanes - 1
        results = [jax.ShapeDtypeStruct((rows, columns), F32)]
        if last:
            results += [jax.ShapeDtypeStruct((SQUARE, packed, BLOCK), F32)]
        else:
            results += [square, jax.ShapeDtypeStruct((8, BLOCK), F32)]
        comb, *carried = call(
            functools.partial(gram_kernel, domains, kl, last),
            results,
            [mix, limits, position, *blocks[kl::lanes], *carried],
            [smem] * 3 + [vmem] * (domains + len(carried)),
            flops=2 * rows * columns * columns,
        )
        combs.append(comb)
    (payload,) = carried
    own = payload[0]
    scalar_lane = 2 * domains

    def add_up(own, got, tiles=()):
        return call(
            functools.partial(sum_kernel, scalar_lane, len(got), len(tiles)),
            [jax.ShapeDtypeStruct((packed, BLOCK), F32)] * 2,
            [own, *got, *tiles],
            [vmem] * (1 + len(got) + len(tiles)),
        )

    def half_width(value, mask):
        return exchange(value.astype(jnp.float16), mask).astype(F32)

    got = [half_width(payload[k], k * lanes) for k in range(1, SQUARE)]
    tiles = [own[per_piece : per_piece + 8]]
    if domains <= 4:
        tiles += [exchange(tiles[0], kd * shards) for kd in range(1, domains)]
    else:
        stride = 1
        while stride < domains:
            tiles = [tiles[0] + exchange(tiles[0], stride * shards)]
            stride *= 2
    own, packet = add_up(own, got, tiles)
    stride = SQUARE * lanes
    while stride < shards:
        own, packet = add_up(own, [half_width(packet, stride)])
        stride *= 2
    got = [half_width(packet, k * lanes) for k in range(1, SQUARE)]

    (every,) = call(
        every_kernel, [jax.ShapeDtypeStruct((8, BLOCK), F32)], [own, *got], [vmem] * SQUARE
    )
    tiles, stride = [every], 1
    while stride < lanes:
        every = tree_sum(tiles)
        tiles = [every, exchange(every, stride)]
        stride *= 2

    away, poly, inv = call(
        functools.partial(newton_kernel, scalar_lane, lanes),
        [
            jax.ShapeDtypeStruct(((lanes - 1) * rows, columns), jnp.bfloat16),
            jax.ShapeDtypeStruct((NS_ITERS, columns, columns), jnp.bfloat16),
            jax.ShapeDtypeStruct((8, BLOCK), F32),
        ],
        [position, own, *got, *combs[1:]],
        [smem] + [vmem] * (SQUARE + lanes - 1),
        pieces_scratch
        + [
            pltpu.VMEM((columns, columns), F32),
            pltpu.VMEM(((lanes - 1) * rows, columns), jnp.bfloat16),
        ],
        flops=9 * 2 * columns**3,
    )
    away = away.reshape(lanes - 1, rows, columns)
    returned = [exchange(away[k - 1], k) for k in range(1, lanes)]
    kinds = jax.ShapeDtypeStruct((1, weight_share.shape[0]), F32)
    kept, weights = call(
        functools.partial(finish_kernel, domains, len(tiles)),
        [jax.ShapeDtypeStruct((rows, columns), jnp.bfloat16), kinds],
        [combs[0], inv, poly, *tiles, weight_share[None], onehot, counts[None]],
        [vmem] * (6 + len(tiles)),
        [pltpu.VMEM(kinds.shape, F32), pltpu.SemaphoreType.DMA],
        flops=NS_ITERS * 2 * rows * columns * columns,
        outs=[vmem, hbm],
    )
    returned = [kept, *returned]
    if lanes == 2:
        first = lane_pos == 0
        ordered = [
            jnp.where(first, returned[0], returned[1]),
            jnp.where(first, returned[1], returned[0]),
        ]
    else:
        stacked = jnp.stack(returned)
        ordered = [
            lax.dynamic_index_in_dim(stacked, lane_pos ^ k, 0, keepdims=False)
            for k in range(lanes)
        ]
    updates = jnp.stack(ordered).astype(F32) * (MUON_SCALE * math.sqrt(full_rows))
    return (updates, weights[0])


def solution(mesh):
    placed = (P("domain", None, "fsdp", None), P(), P(), P())

    return jax.shard_map(
        body,
        mesh=mesh,
        in_specs=placed,
        out_specs=(P("domain", "fsdp", None), P()),
        check_vma=False,
    )
```

```python
import functools
import math

import jax
import jax.numpy as jnp
from jax import lax
from jax.experimental import pallas as pl
from jax.experimental.pallas import tpu as pltpu
from jax.sharding import PartitionSpec as P


NS_ITERS = 3
COEF_A = 3.4445
COEF_B = -4.775
COEF_C = 2.0315
MUON_SCALE = 0.2
ETA = 4.0

AXES = ("domain", "fsdp")
BLOCK = 128
SQUARE = 4
TAIL = 16
HALF_SPAN = 16384.0
TINY = 1e-30
VMEM_GRANT = 16 * 1024 * 1024
F32 = jnp.float32


def group_mixing(domain_ids, domain_weights, kind_count):
    weight_share = domain_weights / jnp.sum(domain_weights)
    onehot = (domain_ids[:, None] == jnp.arange(kind_count, dtype=jnp.int32)[None, :]).astype(F32)
    counts = jnp.sum(onehot, axis=0)
    per_member = weight_share / jnp.maximum(counts, 1.0)
    group_mix = jnp.sum(onehot * per_member[None, :], axis=1)
    return (weight_share, onehot, counts, group_mix)


def block_plan(columns):
    count = columns // BLOCK
    off = [(i, j) for i in range(count) for j in range(i + 1, count)]
    folded = [(i, i) for i in range(0, count, 2)]
    per_piece = (len(off) + len(folded)) // SQUARE
    pieces = []
    for p in range(SQUARE):
        take = per_piece - (1 if p >= SQUARE - len(folded) else 0)
        pieces.append([off.pop(0) for _ in range(take)])
    for n, pair in enumerate(folded):
        pieces[SQUARE - len(folded) + n].append(pair)
    return pieces


def lane_pick(row, index):
    lanes = lax.broadcasted_iota(jnp.int32, row.shape, 1)
    return jnp.sum(jnp.where(lanes == index, row, 0.0), axis=1, keepdims=True)


def encode_row(row):
    power = jnp.clip(jnp.floor(jnp.log2(jnp.abs(row))), -120.0, 120.0)
    scaled = row * jnp.exp2(-power)
    high = scaled.astype(jnp.bfloat16).astype(F32)
    rest = scaled - high
    mid = rest.astype(jnp.bfloat16).astype(F32)
    low = (rest - mid).astype(jnp.bfloat16).astype(F32)
    return (high, mid * 256.0, low * 65536.0, power)


def decode_row(parts):
    high, mid, low, power = parts
    return ((high + mid * (1.0 / 256.0)) + low * (1.0 / 65536.0)) * jnp.exp2(power)


def tail_rows(rows):
    index = lax.broadcasted_iota(jnp.int32, (TAIL, BLOCK), 0)
    out = jnp.zeros((TAIL, BLOCK), F32)
    for n, row in enumerate(rows):
        out = jnp.where(index == n, row, out)
    return out


def fetch_kernel(count, index_ref, source_ref, *refs):
    outs, sems = refs[:count], refs[count]
    copies = [
        pltpu.make_async_copy(source_ref.at[index_ref[n]], outs[n], sems.at[n])
        for n in range(count)
    ]
    for copy in copies:
        copy.start()
    for copy in copies:
        copy.wait()


def gram_kernel(domains, stage, last, mix_ref, lim_ref, pos_ref, *refs):
    blocks, refs = refs[:domains], refs[domains:]
    if stage:
        sofar_ref, scal_ref, refs = refs[0], refs[1], refs[2:]
    comb_ref, refs = refs[0], refs[1:]
    _, columns = blocks[0].shape
    domain_pos, quad = pos_ref[0], pos_ref[1]

    def total(v):
        return jnp.sum(jnp.sum(v, axis=0, keepdims=True), axis=1, keepdims=True)

    keep = lim_ref[stage] > 0
    values = [ref[...].astype(F32) for ref in blocks]
    weights = [jnp.where(keep, mix_ref[kd], 0.0) for kd in range(domains)]
    combined = weights[0] * values[0]
    for kd in range(1, domains):
        combined = combined + weights[kd] * values[kd]
    comb_ref[...] = combined
    rounded = combined.astype(jnp.bfloat16)
    half_width = columns // 2

    def inner(x, y):
        return lax.dot_general(x, y, (((0,), (0,)), ((), ())), preferred_element_type=F32)

    gram_top = inner(rounded[:, :half_width], rounded)
    gram_low = inner(rounded[:, half_width:], rounded[:, half_width:])
    lane = lax.broadcasted_iota(jnp.int32, (1, BLOCK), 1)
    frob = total(combined * combined)
    scal = jnp.where(lane == 2 * domains, frob, 0.0)
    for kd in range(domains):
        group = domain_pos ^ kd
        square = jnp.where(keep, total(values[kd] * values[kd]), 0.0)
        scal = jnp.where(lane == group, total(values[kd] * combined), scal)
        scal = jnp.where(lane == domains + group, square, scal)
    if stage:
        frob = frob + lane_pick(scal_ref[0:1, :], 2 * domains)
        scal = scal + scal_ref[0:1, :]
    if not last:
        gram_ref, sums_ref = refs
        top, low = pl.ds(0, half_width), pl.ds(half_width, half_width)
        gram_ref[top, :] = gram_top + sofar_ref[top, :] if stage else gram_top
        gram_ref[low, low] = gram_low + sofar_ref[low, low] if stage else gram_low
        sums_ref[...] = jnp.broadcast_to(scal, sums_ref.shape)
        return

    (pay_ref,) = refs
    body_rows = pay_ref.shape[1] - TAIL
    parts = encode_row(scal)
    scal = decode_row(parts)
    scale = jnp.where(frob > TINY, HALF_SPAN / jnp.maximum(frob, TINY), 0.0)
    row_id = lax.broadcasted_iota(jnp.int32, (BLOCK, BLOCK), 0)
    col_id = lax.broadcasted_iota(jnp.int32, (BLOCK, BLOCK), 1)

    def part(i, j):
        source, shift = (gram_top, 0) if i * BLOCK < half_width else (gram_low, half_width)
        row, column = i * BLOCK - shift, j * BLOCK - shift
        value = source[row : row + BLOCK, column : column + BLOCK]
        if stage:
            value = value + sofar_ref[pl.ds(i * BLOCK, BLOCK), pl.ds(j * BLOCK, BLOCK)]
        return value

    for p, entries in enumerate(block_plan(columns)):
        slot = quad ^ p
        factor = jnp.where(slot == 0, 1.0, scale)
        diag = jnp.zeros((1, BLOCK), F32)
        for n, (i, j) in enumerate(entries):
            if i == j:
                upper, lower = part(i, i), part(i + 1, i + 1)
                value = jnp.where(row_id < col_id, upper, lower)
                diag = jnp.sum(jnp.where(row_id == col_id, upper, 0.0), axis=0, keepdims=True)
            else:
                value = part(i, j)
            pay_ref[slot, pl.ds(n * BLOCK, BLOCK), :] = value * factor
        own_tail = tail_rows([diag, scal])
        sent_tail = tail_rows([diag * scale, *parts])
        pay_ref[slot, pl.ds(body_rows, TAIL), :] = jnp.where(slot == 0, own_tail, sent_tail)


def tree_sum(terms):
    while len(terms) > 1:
        terms = [terms[n] + terms[n + 1] for n in range(0, len(terms), 2)]
    return terms[0]


def sum_kernel(scalar_lane, count, tile_count, *refs):
    own_ref, got, refs = refs[0], refs[1 : 1 + count], refs[1 + count :]
    tiles, (out_ref, pay_ref) = refs[:tile_count], refs[tile_count:]
    body_rows = own_ref.shape[0] - TAIL

    def row(ref, n):
        return ref[pl.ds(body_rows + n, 1), :]

    scals = [row(own_ref, 1)] + [decode_row([row(ref, 1 + n) for n in range(4)]) for ref in got]
    scales = [1.0] + [lane_pick(scal, scalar_lane) * (1.0 / HALF_SPAN) for scal in scals[1:]]
    refs = (own_ref, *got)
    value = tree_sum([ref[pl.ds(0, body_rows), :] * x for ref, x in zip(refs, scales)])
    diag = tree_sum([row(ref, 0) * x for ref, x in zip(refs, scales)])
    scal = tree_sum(scals)
    if tile_count:
        every = tree_sum([ref[1:2, :] for ref in tiles])
    else:
        every = tree_sum(
            [row(own_ref, 2)] + [decode_row([row(ref, 5 + n) for n in range(4)]) for ref in got]
        )
    frob = lane_pick(scal, scalar_lane)
    parts, every_parts = encode_row(scal), encode_row(every)
    scal, every = decode_row(parts), decode_row(every_parts)
    scale = jnp.where(frob > TINY, HALF_SPAN / jnp.maximum(frob, TINY), 0.0)
    out_ref[pl.ds(0, body_rows), :] = value
    out_ref[pl.ds(body_rows, TAIL), :] = tail_rows([diag, scal, every])
    pay_ref[pl.ds(0, body_rows), :] = value * scale
    pay_ref[pl.ds(body_rows, TAIL), :] = tail_rows([diag * scale, *parts, *every_parts])


def newton_kernel(scalar_lane, lanes, pos_ref, own_ref, *refs):
    got, refs = refs[: SQUARE - 1], refs[SQUARE - 1 :]
    combs, refs = refs[: lanes - 1], refs[lanes - 1 :]
    away_ref, poly_ref, inv_ref, piece_ref, diag_ref, gram_ref, start_ref = refs
    quad = pos_ref[1]
    body_rows = own_ref.shape[0] - TAIL
    rows, columns = combs[0].shape
    scal = own_ref[pl.ds(body_rows + 1, 1), :]
    frob = lane_pick(scal, scalar_lane)
    inv = 1.0 / (jnp.sqrt(frob) + 1e-07)
    shared = (frob * inv) * inv * (1.0 / HALF_SPAN)
    for k in range(SQUARE):
        ref = own_ref if k == 0 else got[k - 1]
        value, diag = ref[pl.ds(0, body_rows), :], ref[pl.ds(body_rows, 1), :]
        if k == 0:
            value, diag = (value * inv) * inv, (diag * inv) * inv
        else:
            value, diag = value * shared, diag * shared
        piece_ref[quad ^ k] = value
        diag_ref[quad ^ k] = jnp.broadcast_to(diag, diag_ref.shape[1:])
    row_id = lax.broadcasted_iota(jnp.int32, (BLOCK, BLOCK), 0)
    col_id = lax.broadcasted_iota(jnp.int32, (BLOCK, BLOCK), 1)

    def place(i, j, value):
        gram_ref[pl.ds(i * BLOCK, BLOCK), pl.ds(j * BLOCK, BLOCK)] = value

    for p, entries in enumerate(block_plan(columns)):
        for n, (i, j) in enumerate(entries):
            value = piece_ref[p, pl.ds(n * BLOCK, BLOCK), :]
            flipped = value.T
            if i == j:
                diag = diag_ref[p][0:1]
                upper = jnp.where(row_id < col_id, value, jnp.where(row_id > col_id, flipped, diag))
                place(i, i, upper)
                place(i + 1, i + 1, jnp.where(row_id < col_id, flipped, value))
            else:
                place(i, j, value)
                place(j, i, flipped)

    def dot(x, y):
        return jnp.dot(x, y, preferred_element_type=F32)

    inv_ref[...] = jnp.broadcast_to(inv, inv_ref.shape)
    for n, ref in enumerate(combs):
        start_ref[pl.ds(n * rows, rows), :] = (ref[...] * inv).astype(jnp.bfloat16)
    half_width = columns // 2
    top, low = pl.ds(0, half_width), pl.ds(half_width, half_width)
    iterate = start_ref[...]
    gram = gram_ref[...]
    for step in range(NS_ITERS):
        near = gram.astype(jnp.bfloat16)
        if step:
            iterate = newton_rows(iterate, poly)
        poly = (COEF_B * gram + COEF_C * dot(near, near)).astype(jnp.bfloat16)
        poly_ref[step] = poly
        if step + 1 == NS_ITERS:
            away_ref[...] = newton_rows(iterate, poly)
            return
        half = COEF_A * gram + dot(near, poly)
        high = half.astype(jnp.bfloat16)
        rest = (half - high.astype(F32)).astype(jnp.bfloat16)
        twice = jnp.concatenate([poly, poly], axis=1)
        both = jnp.concatenate([high, rest], axis=0)
        gram_ref[top, :] = COEF_A * half[:half_width] + dot(twice[:half_width], both)
        gram_ref[low, low] = COEF_A * half[half_width:, half_width:] + dot(
            twice[half_width:], both[:, half_width:]
        )
        gram_ref[low, top] = gram_ref[top, low].T
        gram = gram_ref[...]


def newton_rows(iterate, poly):
    moved = jnp.dot(iterate, poly, preferred_element_type=F32)
    return (COEF_A * iterate.astype(F32) + moved).astype(jnp.bfloat16)


def every_kernel(own_ref, *refs):
    got, out_ref = refs[:-1], refs[-1]
    body_rows = own_ref.shape[0] - TAIL
    sums = tree_sum(
        [own_ref[pl.ds(body_rows + 2, 1), :]]
        + [decode_row([ref[pl.ds(body_rows + 5 + n, 1), :] for n in range(4)]) for ref in got]
    )
    out_ref[...] = jnp.broadcast_to(sums, out_ref.shape)


def finish_kernel(domains, count, comb_ref, inv_ref, poly_ref, *refs):
    tiles, refs = refs[:count], refs[count:]
    share_ref, onehot_ref, counts_ref, rows_ref, out_ref, held_ref, sem = refs
    sums = tree_sum([ref[0:1, :] for ref in tiles])
    norm = jnp.sqrt(lane_pick(sums, 2 * domains))
    score = jnp.zeros(share_ref.shape, F32)
    for g in range(domains):
        aligned, squares = lane_pick(sums, g), lane_pick(sums, domains + g)
        cosine = aligned / (jnp.sqrt(squares) * norm + 1e-06)
        score = score + onehot_ref[g : g + 1, :] * cosine
    score = score / jnp.maximum(counts_ref[...], 1.0)
    raised = share_ref[...] * jnp.exp(ETA * score)
    held_ref[...] = raised / jnp.sum(raised, axis=1, keepdims=True)
    copy = pltpu.make_async_copy(held_ref, out_ref, sem)
    copy.start()
    iterate = (comb_ref[...] * inv_ref[0:1, 0:1]).astype(jnp.bfloat16)
    for step in range(NS_ITERS):
        iterate = newton_rows(iterate, poly_ref[step])
    rows_ref[...] = iterate
    copy.wait()


def call(kernel, out_shape, args, spaces, scratch=(), flops=0, outs=None):
    size = sum(math.prod(a.shape) * a.dtype.itemsize for a in (*args, *out_shape))
    outs = outs or [pltpu.VMEM] * len(out_shape)
    return pl.pallas_call(
        kernel,
        out_shape=tuple(out_shape),
        in_specs=[pl.BlockSpec(memory_space=s) for s in spaces],
        out_specs=tuple(pl.BlockSpec(memory_space=s) for s in outs),
        scratch_shapes=list(scratch),
        cost_estimate=pl.CostEstimate(flops=flops, bytes_accessed=size, transcendentals=0),
        compiler_params=pltpu.CompilerParams(vmem_limit_bytes=VMEM_GRANT),
    )(*args)


def spread_order(members, lanes):
    return sorted(range(1, members), key=lambda k: k // lanes == 0)


def body(gradients, row_counts, domain_ids, domain_weights):
    domains = lax.axis_size("domain")
    shards = lax.axis_size("fsdp")
    matrices, rows, columns = gradients.shape[1:]
    lanes = matrices // domains
    sets = shards // lanes
    members = domains * lanes
    full_rows = rows * shards
    domain_pos = lax.axis_index("domain")
    shard_pos = lax.axis_index("fsdp")
    lane_pos = shard_pos % lanes
    set_pos = shard_pos // lanes
    member = domain_pos * lanes + lane_pos
    quad = set_pos % SQUARE
    flip = [(k // lanes) * shards + k % lanes for k in range(members)]

    def exchange(value, mask):
        return lax.ppermute(value, AXES, [(i, i ^ mask) for i in range(domains * shards)])

    vmem, smem, hbm = pltpu.VMEM, pltpu.SMEM, pltpu.HBM
    tile = jax.ShapeDtypeStruct((rows, columns), gradients.dtype)

    def fetch(wanted):
        index = jnp.stack([member ^ k for k in wanted]).astype(jnp.int32)
        return call(
            functools.partial(fetch_kernel, len(wanted)),
            [tile] * len(wanted),
            [index, gradients[0]],
            [smem, hbm],
            [pltpu.SemaphoreType.DMA((len(wanted),))],
        )

    if members <= 8:
        order = spread_order(members, lanes)
        ahead = lax.dynamic_index_in_dim(gradients[0], member ^ order[0], 0, keepdims=False)
        fetched = (ahead, *fetch(order[1:] + [0]))
        pieces = dict(zip(order + [0], fetched))
        got = {k: exchange(pieces[k], flip[k]) for k in order}
        got[0] = pieces[0]
        blocks = [got[k] for k in range(members)]
    else:
        teams = [
            [d * shards + s * lanes + l for d in range(domains) for l in range(lanes)]
            for s in range(sets)
        ]
        moved = lax.all_to_all(
            gradients[0], AXES, split_axis=0, concat_axis=0, axis_index_groups=teams, tiled=True
        )
        blocks = [
            lax.dynamic_index_in_dim(moved, member ^ k, 0, keepdims=False) for k in range(members)
        ]

    weight_share, onehot, counts, group_mix = group_mixing(
        domain_ids, domain_weights, domain_weights.shape[0]
    )
    mix = jnp.take(group_mix, domain_pos ^ jnp.arange(domains, dtype=jnp.int32))
    lane_row = (set_pos * lanes + (lane_pos ^ jnp.arange(lanes, dtype=jnp.int32))) * rows
    limits = lax.dynamic_index_in_dim(row_counts, member, 0, keepdims=False) - lane_row
    position = jnp.stack([domain_pos, quad, lane_pos]).astype(jnp.int32)

    per_piece = len(block_plan(columns)[0]) * BLOCK
    packed = per_piece + TAIL
    pieces_scratch = [
        pltpu.VMEM((SQUARE, per_piece, BLOCK), F32),
        pltpu.VMEM((SQUARE, 8, BLOCK), F32),
    ]
    square = jax.ShapeDtypeStruct((columns, columns), F32)
    combs, carried = [], []
    for kl in range(lanes):
        last = kl == lanes - 1
        results = [jax.ShapeDtypeStruct((rows, columns), F32)]
        if last:
            results += [jax.ShapeDtypeStruct((SQUARE, packed, BLOCK), F32)]
        else:
            results += [square, jax.ShapeDtypeStruct((8, BLOCK), F32)]
        comb, *carried = call(
            functools.partial(gram_kernel, domains, kl, last),
            results,
            [mix, limits, position, *blocks[kl::lanes], *carried],
            [smem] * 3 + [vmem] * (domains + len(carried)),
            flops=2 * rows * columns * columns,
        )
        combs.append(comb)
    (payload,) = carried
    own = payload[0]
    scalar_lane = 2 * domains

    def add_up(own, got, tiles=()):
        return call(
            functools.partial(sum_kernel, scalar_lane, len(got), len(tiles)),
            [jax.ShapeDtypeStruct((packed, BLOCK), F32)] * 2,
            [own, *got, *tiles],
            [vmem] * (1 + len(got) + len(tiles)),
        )

    def half_width(value, mask):
        return exchange(value.astype(jnp.float16), mask).astype(F32)

    got = [half_width(payload[k], k * lanes) for k in range(1, SQUARE)]
    tiles = [own[per_piece : per_piece + 8]]
    if domains <= 4:
        tiles += [exchange(tiles[0], kd * shards) for kd in range(1, domains)]
    else:
        stride = 1
        while stride < domains:
            tiles = [tiles[0] + exchange(tiles[0], stride * shards)]
            stride *= 2
    own, packet = add_up(own, got, tiles)
    stride = SQUARE * lanes
    while stride < shards:
        own, packet = add_up(own, [half_width(packet, stride)])
        stride *= 2
    got = [half_width(packet, k * lanes) for k in range(1, SQUARE)]

    (every,) = call(
        every_kernel, [jax.ShapeDtypeStruct((8, BLOCK), F32)], [own, *got], [vmem] * SQUARE
    )
    tiles, stride = [every], 1
    while stride < lanes:
        every = tree_sum(tiles)
        tiles = [every, exchange(every, stride)]
        stride *= 2

    away, poly, inv = call(
        functools.partial(newton_kernel, scalar_lane, lanes),
        [
            jax.ShapeDtypeStruct(((lanes - 1) * rows, columns), jnp.bfloat16),
            jax.ShapeDtypeStruct((NS_ITERS, columns, columns), jnp.bfloat16),
            jax.ShapeDtypeStruct((8, BLOCK), F32),
        ],
        [position, own, *got, *combs[1:]],
        [smem] + [vmem] * (SQUARE + lanes - 1),
        pieces_scratch
        + [
            pltpu.VMEM((columns, columns), F32),
            pltpu.VMEM(((lanes - 1) * rows, columns), jnp.bfloat16),
        ],
        flops=9 * 2 * columns**3,
    )
    away = away.reshape(lanes - 1, rows, columns)
    returned = [exchange(away[k - 1], k) for k in range(1, lanes)]
    kinds = jax.ShapeDtypeStruct((1, weight_share.shape[0]), F32)
    kept, weights = call(
        functools.partial(finish_kernel, domains, len(tiles)),
        [jax.ShapeDtypeStruct((rows, columns), jnp.bfloat16), kinds],
        [combs[0], inv, poly, *tiles, weight_share[None], onehot, counts[None]],
        [vmem] * (6 + len(tiles)),
        [pltpu.VMEM(kinds.shape, F32), pltpu.SemaphoreType.DMA],
        flops=NS_ITERS * 2 * rows * columns * columns,
        outs=[vmem, hbm],
    )
    returned = [kept, *returned]
    if lanes == 2:
        first = lane_pos == 0
        ordered = [
            jnp.where(first, returned[0], returned[1]),
            jnp.where(first, returned[1], returned[0]),
        ]
    else:
        stacked = jnp.stack(returned)
        ordered = [
            lax.dynamic_index_in_dim(stacked, lane_pos ^ k, 0, keepdims=False)
            for k in range(lanes)
        ]
    updates = jnp.stack(ordered).astype(F32) * (MUON_SCALE * math.sqrt(full_rows))
    return (updates, weights[0])


def solution(mesh):
    placed = (P("domain", None, "fsdp", None), P(), P(), P())

    return jax.shard_map(
        body,
        mesh=mesh,
        in_specs=placed,
        out_specs=(P("domain", "fsdp", None), P()),
        check_vma=False,
    )
```

```python
import functools
import math

import jax
import jax.numpy as jnp
from jax import lax
from jax.experimental import pallas as pl
from jax.experimental.pallas import tpu as pltpu
from jax.sharding import PartitionSpec as P


NS_ITERS = 3
COEF_A = 3.4445
COEF_B = -4.775
COEF_C = 2.0315
MUON_SCALE = 0.2
ETA = 4.0

AXES = ("domain", "fsdp")
BLOCK = 128
SQUARE = 4
TAIL = 16
HALF_SPAN = 16384.0
TINY = 1e-30
VMEM_GRANT = 16 * 1024 * 1024
F32 = jnp.float32


def group_mixing(domain_ids, domain_weights, kind_count):
    weight_share = domain_weights / jnp.sum(domain_weights)
    onehot = (domain_ids[:, None] == jnp.arange(kind_count, dtype=jnp.int32)[None, :]).astype(F32)
    counts = jnp.sum(onehot, axis=0)
    per_member = weight_share / jnp.maximum(counts, 1.0)
    group_mix = jnp.sum(onehot * per_member[None, :], axis=1)
    return (weight_share, onehot, counts, group_mix)


def block_plan(columns):
    count = columns // BLOCK
    off = [(i, j) for i in range(count) for j in range(i + 1, count)]
    folded = [(i, i) for i in range(0, count, 2)]
    per_piece = (len(off) + len(folded)) // SQUARE
    pieces = []
    for p in range(SQUARE):
        take = per_piece - (1 if p >= SQUARE - len(folded) else 0)
        pieces.append([off.pop(0) for _ in range(take)])
    for n, pair in enumerate(folded):
        pieces[SQUARE - len(folded) + n].append(pair)
    return pieces


def lane_pick(row, index):
    lanes = lax.broadcasted_iota(jnp.int32, row.shape, 1)
    return jnp.sum(jnp.where(lanes == index, row, 0.0), axis=1, keepdims=True)


def encode_row(row):
    power = jnp.clip(jnp.floor(jnp.log2(jnp.abs(row))), -120.0, 120.0)
    scaled = row * jnp.exp2(-power)
    high = scaled.astype(jnp.bfloat16).astype(F32)
    rest = scaled - high
    mid = rest.astype(jnp.bfloat16).astype(F32)
    low = (rest - mid).astype(jnp.bfloat16).astype(F32)
    return (high, mid * 256.0, low * 65536.0, power)


def decode_row(parts):
    high, mid, low, power = parts
    return ((high + mid * (1.0 / 256.0)) + low * (1.0 / 65536.0)) * jnp.exp2(power)


def tail_rows(rows):
    index = lax.broadcasted_iota(jnp.int32, (TAIL, BLOCK), 0)
    out = jnp.zeros((TAIL, BLOCK), F32)
    for n, row in enumerate(rows):
        out = jnp.where(index == n, row, out)
    return out


def fetch_kernel(count, index_ref, source_ref, *refs):
    outs, sems = refs[:count], refs[count]
    copies = [
        pltpu.make_async_copy(source_ref.at[index_ref[n]], outs[n], sems.at[n])
        for n in range(count)
    ]
    for copy in copies:
        copy.start()
    for copy in copies:
        copy.wait()


def gram_kernel(domains, others, stage, last, mix_ref, lim_ref, pos_ref, *refs):
    blocks, refs = refs[:domains], refs[domains:]
    ahead, refs = (refs[:others], refs[others:]) if stage == 0 else ((), refs)
    if stage:
        sofar_ref, scal_ref, refs = refs[0], refs[1], refs[2:]
    comb_ref, refs = refs[0], refs[1:]
    _, columns = blocks[0].shape
    domain_pos, quad = pos_ref[0], pos_ref[1]

    def total(v):
        return jnp.sum(jnp.sum(v, axis=0, keepdims=True), axis=1, keepdims=True)

    keep = lim_ref[stage] > 0
    values = [ref[...].astype(F32) for ref in blocks]
    weights = [jnp.where(keep, mix_ref[kd], 0.0) for kd in range(domains)]
    combined = weights[0] * values[0]
    for kd in range(1, domains):
        combined = combined + weights[kd] * values[kd]
    comb_ref[...] = combined
    rounded = combined.astype(jnp.bfloat16)
    half_width = columns // 2

    def inner(x, y):
        return lax.dot_general(x, y, (((0,), (0,)), ((), ())), preferred_element_type=F32)

    gram_top = inner(rounded[:, :half_width], rounded)
    gram_low = inner(rounded[:, half_width:], rounded[:, half_width:])
    lane = lax.broadcasted_iota(jnp.int32, (1, BLOCK), 1)
    frob = total(combined * combined)
    scal = jnp.where(lane == 2 * domains, frob, 0.0)
    for kd in range(domains):
        group = domain_pos ^ kd
        scal = jnp.where(lane == group, total(values[kd] * combined), scal)
        if kd == 0 and stage:
            continue
        square = jnp.where(keep, total(values[kd] * values[kd]), 0.0)
        for n, ref in enumerate(ahead if kd == 0 else (), 1):
            value = ref[...].astype(F32)
            square = square + jnp.where(lim_ref[n] > 0, total(value * value), 0.0)
        scal = jnp.where(lane == domains + group, square, scal)
    if stage:
        frob = frob + lane_pick(scal_ref[0:1, :], 2 * domains)
        scal = scal + scal_ref[0:1, :]
    if not last:
        gram_ref, sums_ref = refs
        top, low = pl.ds(0, half_width), pl.ds(half_width, half_width)
        gram_ref[top, :] = gram_top + sofar_ref[top, :] if stage else gram_top
        gram_ref[low, low] = gram_low + sofar_ref[low, low] if stage else gram_low
        sums_ref[...] = jnp.broadcast_to(scal, sums_ref.shape)
        return

    (pay_ref,) = refs
    body_rows = pay_ref.shape[1] - TAIL
    parts = encode_row(scal)
    scal = decode_row(parts)
    scale = jnp.where(frob > TINY, HALF_SPAN / jnp.maximum(frob, TINY), 0.0)
    row_id = lax.broadcasted_iota(jnp.int32, (BLOCK, BLOCK), 0)
    col_id = lax.broadcasted_iota(jnp.int32, (BLOCK, BLOCK), 1)

    def part(i, j):
        source, shift = (gram_top, 0) if i * BLOCK < half_width else (gram_low, half_width)
        row, column = i * BLOCK - shift, j * BLOCK - shift
        value = source[row : row + BLOCK, column : column + BLOCK]
        if stage:
            value = value + sofar_ref[pl.ds(i * BLOCK, BLOCK), pl.ds(j * BLOCK, BLOCK)]
        return value

    for p, entries in enumerate(block_plan(columns)):
        slot = quad ^ p
        factor = jnp.where(slot == 0, 1.0, scale)
        diag = jnp.zeros((1, BLOCK), F32)
        for n, (i, j) in enumerate(entries):
            if i == j:
                upper, lower = part(i, i), part(i + 1, i + 1)
                value = jnp.where(row_id < col_id, upper, lower)
                diag = jnp.sum(jnp.where(row_id == col_id, upper, 0.0), axis=0, keepdims=True)
            else:
                value = part(i, j)
            pay_ref[slot, pl.ds(n * BLOCK, BLOCK), :] = value * factor
        own_tail = tail_rows([diag, scal])
        sent_tail = tail_rows([diag * scale, *parts])
        pay_ref[slot, pl.ds(body_rows, TAIL), :] = jnp.where(slot == 0, own_tail, sent_tail)


def tree_sum(terms):
    while len(terms) > 1:
        terms = [terms[n] + terms[n + 1] for n in range(0, len(terms), 2)]
    return terms[0]


def sum_kernel(scalar_lane, count, tile_count, *refs):
    own_ref, got, refs = refs[0], refs[1 : 1 + count], refs[1 + count :]
    tiles, (out_ref, pay_ref) = refs[:tile_count], refs[tile_count:]
    body_rows = own_ref.shape[0] - TAIL

    def row(ref, n):
        return ref[pl.ds(body_rows + n, 1), :]

    scals = [row(own_ref, 1)] + [decode_row([row(ref, 1 + n) for n in range(4)]) for ref in got]
    scales = [1.0] + [lane_pick(scal, scalar_lane) * (1.0 / HALF_SPAN) for scal in scals[1:]]
    refs = (own_ref, *got)
    value = tree_sum([ref[pl.ds(0, body_rows), :] * x for ref, x in zip(refs, scales)])
    diag = tree_sum([row(ref, 0) * x for ref, x in zip(refs, scales)])
    scal = tree_sum(scals)
    if tile_count:
        every = tree_sum([ref[1:2, :] for ref in tiles])
    else:
        every = tree_sum(
            [row(own_ref, 2)] + [decode_row([row(ref, 5 + n) for n in range(4)]) for ref in got]
        )
    frob = lane_pick(scal, scalar_lane)
    parts, every_parts = encode_row(scal), encode_row(every)
    scal, every = decode_row(parts), decode_row(every_parts)
    scale = jnp.where(frob > TINY, HALF_SPAN / jnp.maximum(frob, TINY), 0.0)
    out_ref[pl.ds(0, body_rows), :] = value
    out_ref[pl.ds(body_rows, TAIL), :] = tail_rows([diag, scal, every])
    pay_ref[pl.ds(0, body_rows), :] = value * scale
    pay_ref[pl.ds(body_rows, TAIL), :] = tail_rows([diag * scale, *parts, *every_parts])


def newton_kernel(scalar_lane, lanes, pos_ref, own_ref, *refs):
    got, refs = refs[: SQUARE - 1], refs[SQUARE - 1 :]
    combs, refs = refs[: lanes - 1], refs[lanes - 1 :]
    away_ref, poly_ref, inv_ref, piece_ref, diag_ref, gram_ref, start_ref = refs
    quad = pos_ref[1]
    body_rows = own_ref.shape[0] - TAIL
    rows, columns = combs[0].shape
    scal = own_ref[pl.ds(body_rows + 1, 1), :]
    frob = lane_pick(scal, scalar_lane)
    inv = 1.0 / (jnp.sqrt(frob) + 1e-07)
    shared = (frob * inv) * inv * (1.0 / HALF_SPAN)
    for k in range(SQUARE):
        ref = own_ref if k == 0 else got[k - 1]
        value, diag = ref[pl.ds(0, body_rows), :], ref[pl.ds(body_rows, 1), :]
        if k == 0:
            value, diag = (value * inv) * inv, (diag * inv) * inv
        else:
            value, diag = value * shared, diag * shared
        piece_ref[quad ^ k] = value
        diag_ref[quad ^ k] = jnp.broadcast_to(diag, diag_ref.shape[1:])
    row_id = lax.broadcasted_iota(jnp.int32, (BLOCK, BLOCK), 0)
    col_id = lax.broadcasted_iota(jnp.int32, (BLOCK, BLOCK), 1)

    def place(i, j, value):
        gram_ref[pl.ds(i * BLOCK, BLOCK), pl.ds(j * BLOCK, BLOCK)] = value

    for p, entries in enumerate(block_plan(columns)):
        for n, (i, j) in enumerate(entries):
            value = piece_ref[p, pl.ds(n * BLOCK, BLOCK), :]
            flipped = value.T
            if i == j:
                diag = diag_ref[p][0:1]
                upper = jnp.where(row_id < col_id, value, jnp.where(row_id > col_id, flipped, diag))
                place(i, i, upper)
                place(i + 1, i + 1, jnp.where(row_id < col_id, flipped, value))
            else:
                place(i, j, value)
                place(j, i, flipped)

    def dot(x, y):
        return jnp.dot(x, y, preferred_element_type=F32)

    inv_ref[...] = jnp.broadcast_to(inv, inv_ref.shape)
    for n, ref in enumerate(combs):
        start_ref[pl.ds(n * rows, rows), :] = (ref[...] * inv).astype(jnp.bfloat16)
    half_width = columns // 2
    top, low = pl.ds(0, half_width), pl.ds(half_width, half_width)
    iterate = start_ref[...]
    gram = gram_ref[...]
    for step in range(NS_ITERS):
        near = gram.astype(jnp.bfloat16)
        if step:
            iterate = newton_rows(iterate, poly)
        poly = (COEF_B * gram + COEF_C * dot(near, near)).astype(jnp.bfloat16)
        poly_ref[step] = poly
        if step + 1 == NS_ITERS:
            away_ref[...] = newton_rows(iterate, poly)
            return
        half = COEF_A * gram + dot(near, poly)
        high = half.astype(jnp.bfloat16)
        rest = (half - high.astype(F32)).astype(jnp.bfloat16)
        twice = jnp.concatenate([poly, poly], axis=1)
        both = jnp.concatenate([high, rest], axis=0)
        gram_ref[top, :] = COEF_A * half[:half_width] + dot(twice[:half_width], both)
        gram_ref[low, low] = COEF_A * half[half_width:, half_width:] + dot(
            twice[half_width:], both[:, half_width:]
        )
        gram_ref[low, top] = gram_ref[top, low].T
        gram = gram_ref[...]


def newton_rows(iterate, poly):
    moved = jnp.dot(iterate, poly, preferred_element_type=F32)
    return (COEF_A * iterate.astype(F32) + moved).astype(jnp.bfloat16)


def every_kernel(own_ref, *refs):
    got, out_ref = refs[:-1], refs[-1]
    body_rows = own_ref.shape[0] - TAIL
    sums = tree_sum(
        [own_ref[pl.ds(body_rows + 2, 1), :]]
        + [decode_row([ref[pl.ds(body_rows + 5 + n, 1), :] for n in range(4)]) for ref in got]
    )
    out_ref[...] = jnp.broadcast_to(sums, out_ref.shape)


def finish_kernel(domains, count, comb_ref, inv_ref, poly_ref, *refs):
    tiles, refs = refs[:count], refs[count:]
    share_ref, onehot_ref, counts_ref, rows_ref, out_ref, held_ref, sem = refs
    sums = tree_sum([ref[0:1, :] for ref in tiles])
    norm = jnp.sqrt(lane_pick(sums, 2 * domains))
    score = jnp.zeros(share_ref.shape, F32)
    for g in range(domains):
        aligned, squares = lane_pick(sums, g), lane_pick(sums, domains + g)
        cosine = aligned / (jnp.sqrt(squares) * norm + 1e-06)
        score = score + onehot_ref[g : g + 1, :] * cosine
    score = score / jnp.maximum(counts_ref[...], 1.0)
    raised = share_ref[...] * jnp.exp(ETA * score)
    held_ref[...] = raised / jnp.sum(raised, axis=1, keepdims=True)
    copy = pltpu.make_async_copy(held_ref, out_ref, sem)
    copy.start()
    iterate = (comb_ref[...] * inv_ref[0:1, 0:1]).astype(jnp.bfloat16)
    for step in range(NS_ITERS):
        iterate = newton_rows(iterate, poly_ref[step])
    rows_ref[...] = iterate
    copy.wait()


def call(kernel, out_shape, args, spaces, scratch=(), flops=0, outs=None):
    size = sum(math.prod(a.shape) * a.dtype.itemsize for a in (*args, *out_shape))
    outs = outs or [pltpu.VMEM] * len(out_shape)
    return pl.pallas_call(
        kernel,
        out_shape=tuple(out_shape),
        in_specs=[pl.BlockSpec(memory_space=s) for s in spaces],
        out_specs=tuple(pl.BlockSpec(memory_space=s) for s in outs),
        scratch_shapes=list(scratch),
        cost_estimate=pl.CostEstimate(flops=flops, bytes_accessed=size, transcendentals=0),
        compiler_params=pltpu.CompilerParams(vmem_limit_bytes=VMEM_GRANT),
    )(*args)


def spread_order(members, lanes):
    return sorted(range(1, members), key=lambda k: k // lanes == 0)


def body(gradients, row_counts, domain_ids, domain_weights):
    domains = lax.axis_size("domain")
    shards = lax.axis_size("fsdp")
    matrices, rows, columns = gradients.shape[1:]
    lanes = matrices // domains
    sets = shards // lanes
    members = domains * lanes
    full_rows = rows * shards
    domain_pos = lax.axis_index("domain")
    shard_pos = lax.axis_index("fsdp")
    lane_pos = shard_pos % lanes
    set_pos = shard_pos // lanes
    member = domain_pos * lanes + lane_pos
    quad = set_pos % SQUARE
    flip = [(k // lanes) * shards + k % lanes for k in range(members)]

    def exchange(value, mask):
        return lax.ppermute(value, AXES, [(i, i ^ mask) for i in range(domains * shards)])

    vmem, smem, hbm = pltpu.VMEM, pltpu.SMEM, pltpu.HBM
    tile = jax.ShapeDtypeStruct((rows, columns), gradients.dtype)

    def fetch(wanted):
        index = jnp.stack([member ^ k for k in wanted]).astype(jnp.int32)
        return call(
            functools.partial(fetch_kernel, len(wanted)),
            [tile] * len(wanted),
            [index, gradients[0]],
            [smem, hbm],
            [pltpu.SemaphoreType.DMA((len(wanted),))],
        )

    if members <= 8:
        order = spread_order(members, lanes)
        ahead = lax.dynamic_index_in_dim(gradients[0], member ^ order[0], 0, keepdims=False)
        fetched = (ahead, *fetch(order[1:] + [0]))
        pieces = dict(zip(order + [0], fetched))
        got = {k: exchange(pieces[k], flip[k]) for k in order}
        got[0] = pieces[0]
        blocks = [got[k] for k in range(members)]
    else:
        teams = [
            [d * shards + s * lanes + l for d in range(domains) for l in range(lanes)]
            for s in range(sets)
        ]
        moved = lax.all_to_all(
            gradients[0], AXES, split_axis=0, concat_axis=0, axis_index_groups=teams, tiled=True
        )
        blocks = [
            lax.dynamic_index_in_dim(moved, member ^ k, 0, keepdims=False) for k in range(members)
        ]

    weight_share, onehot, counts, group_mix = group_mixing(
        domain_ids, domain_weights, domain_weights.shape[0]
    )
    mix = jnp.take(group_mix, domain_pos ^ jnp.arange(domains, dtype=jnp.int32))
    lane_row = (set_pos * lanes + (lane_pos ^ jnp.arange(lanes, dtype=jnp.int32))) * rows
    limits = lax.dynamic_index_in_dim(row_counts, member, 0, keepdims=False) - lane_row
    position = jnp.stack([domain_pos, quad, lane_pos]).astype(jnp.int32)

    per_piece = len(block_plan(columns)[0]) * BLOCK
    packed = per_piece + TAIL
    pieces_scratch = [
        pltpu.VMEM((SQUARE, per_piece, BLOCK), F32),
        pltpu.VMEM((SQUARE, 8, BLOCK), F32),
    ]
    square = jax.ShapeDtypeStruct((columns, columns), F32)
    combs, carried = [], []
    for kl in range(lanes):
        last = kl == lanes - 1
        ahead = blocks[1:lanes] if kl == 0 else []
        results = [jax.ShapeDtypeStruct((rows, columns), F32)]
        if last:
            results += [jax.ShapeDtypeStruct((SQUARE, packed, BLOCK), F32)]
        else:
            results += [square, jax.ShapeDtypeStruct((8, BLOCK), F32)]
        comb, *carried = call(
            functools.partial(gram_kernel, domains, lanes - 1, kl, last),
            results,
            [mix, limits, position, *blocks[kl::lanes], *ahead, *carried],
            [smem] * 3 + [vmem] * (domains + len(ahead) + len(carried)),
            flops=2 * rows * columns * columns,
        )
        combs.append(comb)
    (payload,) = carried
    own = payload[0]
    scalar_lane = 2 * domains

    def add_up(own, got, tiles=()):
        return call(
            functools.partial(sum_kernel, scalar_lane, len(got), len(tiles)),
            [jax.ShapeDtypeStruct((packed, BLOCK), F32)] * 2,
            [own, *got, *tiles],
            [vmem] * (1 + len(got) + len(tiles)),
        )

    def half_width(value, mask):
        return exchange(value.astype(jnp.float16), mask).astype(F32)

    got = [half_width(payload[k], k * lanes) for k in range(1, SQUARE)]
    tiles = [own[per_piece : per_piece + 8]]
    if domains <= 4:
        tiles += [exchange(tiles[0], kd * shards) for kd in range(1, domains)]
    else:
        stride = 1
        while stride < domains:
            tiles = [tiles[0] + exchange(tiles[0], stride * shards)]
            stride *= 2
    own, packet = add_up(own, got, tiles)
    stride = SQUARE * lanes
    while stride < shards:
        own, packet = add_up(own, [half_width(packet, stride)])
        stride *= 2
    got = [half_width(packet, k * lanes) for k in range(1, SQUARE)]

    (every,) = call(
        every_kernel, [jax.ShapeDtypeStruct((8, BLOCK), F32)], [own, *got], [vmem] * SQUARE
    )
    tiles, stride = [every], 1
    while stride < lanes:
        every = tree_sum(tiles)
        tiles = [every, exchange(every, stride)]
        stride *= 2

    away, poly, inv = call(
        functools.partial(newton_kernel, scalar_lane, lanes),
        [
            jax.ShapeDtypeStruct(((lanes - 1) * rows, columns), jnp.bfloat16),
            jax.ShapeDtypeStruct((NS_ITERS, columns, columns), jnp.bfloat16),
            jax.ShapeDtypeStruct((8, BLOCK), F32),
        ],
        [position, own, *got, *combs[1:]],
        [smem] + [vmem] * (SQUARE + lanes - 1),
        pieces_scratch
        + [
            pltpu.VMEM((columns, columns), F32),
            pltpu.VMEM(((lanes - 1) * rows, columns), jnp.bfloat16),
        ],
        flops=9 * 2 * columns**3,
    )
    away = away.reshape(lanes - 1, rows, columns)
    returned = [exchange(away[k - 1], k) for k in range(1, lanes)]
    kinds = jax.ShapeDtypeStruct((1, weight_share.shape[0]), F32)
    kept, weights = call(
        functools.partial(finish_kernel, domains, len(tiles)),
        [jax.ShapeDtypeStruct((rows, columns), jnp.bfloat16), kinds],
        [combs[0], inv, poly, *tiles, weight_share[None], onehot, counts[None]],
        [vmem] * (6 + len(tiles)),
        [pltpu.VMEM(kinds.shape, F32), pltpu.SemaphoreType.DMA],
        flops=NS_ITERS * 2 * rows * columns * columns,
        outs=[vmem, hbm],
    )
    returned = [kept, *returned]
    if lanes == 2:
        first = lane_pos == 0
        ordered = [
            jnp.where(first, returned[0], returned[1]),
            jnp.where(first, returned[1], returned[0]),
        ]
    else:
        stacked = jnp.stack(returned)
        ordered = [
            lax.dynamic_index_in_dim(stacked, lane_pos ^ k, 0, keepdims=False)
            for k in range(lanes)
        ]
    updates = jnp.stack(ordered).astype(F32) * (MUON_SCALE * math.sqrt(full_rows))
    return (updates, weights[0])


def solution(mesh):
    placed = (P("domain", None, "fsdp", None), P(), P(), P())

    return jax.shard_map(
        body,
        mesh=mesh,
        in_specs=placed,
        out_specs=(P("domain", "fsdp", None), P()),
        check_vma=False,
    )
```
